32 devices in a mesh: dp: 8 (over y, x, core), tensor: 4 (over z).
Axes of the slice: x: 2, y: 2, z: 4, core: 2. Of those that a mesh axis runs over, the one named last changes fastest.
Arguments:
- block_in: bfloat16 [2, 16384, 1024], P(None, ('dp', 'tensor')), may hold values from -6 to 6
- norm1_gain: bfloat16 [1024], P('dp'), may hold values from 0.5 to 1.5
- norm1_bias: bfloat16 [1024], P('dp'), may hold values from -3 to 3
- w_query: bfloat16 [1024, 1024], P('dp', 'tensor'), may hold values from -0.1875 to 0.1875
- w_key: bfloat16 [1024, 1024], P('dp', 'tensor'), may hold values from -0.1875 to 0.1875
- w_value: bfloat16 [1024, 1024], P('dp', 'tensor'), may hold values from -0.1875 to 0.1875
- w_out: bfloat16 [1024, 1024], P('tensor', 'dp'), may hold values from -1.5 to 1.5
- norm2_gain: bfloat16 [1024], P('dp'), may hold values from 0.5 to 1.5
- norm2_bias: bfloat16 [1024], P('dp'), may hold values from -3 to 3
- w_up: bfloat16 [1024, 4096], P('dp', 'tensor'), may hold values from -0.1875 to 0.1875
- up_bias: bfloat16 [4, 1024], P('tensor', 'dp'), may hold values from -3 to 3
- w_down: bfloat16 [4096, 1024], P('tensor', 'dp'), may hold values from -0.125 to 0.125
- down_bias: bfloat16 [1024], P('dp'), may hold values from -3 to 3
- segments: int32 [2, 16384], P(None, 'dp'), may hold values from 0 to 10, as said below
- rand_blocks: int32 [2, 8, 16, 32, 3], P(None, 'dp', 'tensor'), may hold values from 0 to 31
- glob_blocks: int32 [2, 8, 2], P(None, 'dp'), may hold values from 0 to 31
- cotangent: bfloat16 [2, 16384, 1024], P(None, ('dp', 'tensor')), may hold values from -6 to 6
Outputs:
- block_out: bfloat16 [2, 16384, 1024], P(None, ('dp', 'tensor'))
- grad_in: float32 [2, 16384, 1024], P(None, ('dp', 'tensor'))
- grad_norm1_gain: float32 [1024], P(('dp', 'tensor'))
- grad_norm1_bias: float32 [1024], P(('dp', 'tensor'))
- grad_query: float32 [1024, 1024], P('dp', 'tensor')
- grad_key: float32 [1024, 1024], P('dp', 'tensor')
- grad_value: float32 [1024, 1024], P('dp', 'tensor')
- grad_out: float32 [1024, 1024], P('tensor', 'dp')
- grad_norm2_gain: float32 [1024], P(('dp', 'tensor'))
- grad_norm2_bias: float32 [1024], P(('dp', 'tensor'))
- grad_up: float32 [1024, 4096], P('dp', 'tensor')
- grad_up_bias: float32 [4, 1024], P('tensor', 'dp')
- grad_down: float32 [4096, 1024], P('tensor', 'dp')
- grad_down_bias: float32 [1024], P(('dp', 'tensor'))
The draws below stay inside these ranges and needn't reach their ends.
Inputs may be any that keep to these rules, and one draw needn't show every extreme that they name: `segments`: segment numbers start at 0 in every sequence and never fall along it; each document but a sequence's last holds between 204 and 2000 tokens; the largest number is reached in some sequence of every micro-batch.
All inputs are finite; a program needn't handle non-finite values.
Results may differ from the reference program's by a relative error of at most 0.019.
Values may be sent and summed in bfloat16 or wider, within the bound.
No kernel may reach another device: no remote copies, remote signals or barrier semaphores. Data moves between devices by JAX's collectives and lax.ppermute only.
A program may use at most 192 MiB of HBM per device.

```python
import jax
import jax.numpy as jnp
from jax import lax

D = 1024
H = 16
HD = 64
FF = 4096
BLOCK = 64
RAND = 3
GLOB = 2
SEQ = 2048
MB = 2
SEQS_MB = 8
ROWS = 16384
NB = 32
TGROUPS = 4
FF_T = 1024


def draw_segments(key, part):
    seq_total = MB * SEQS_MB
    lengths = jax.random.randint(key, (seq_total, 12), SEQ // 10, SEQ * 125 // 128 + 1)
    first_of_batch = jnp.arange(seq_total, dtype=jnp.int32) % SEQS_MB == 0
    lengths = jnp.where(first_of_batch[:, None], SEQ // 10, lengths)
    doc_ends = jnp.cumsum(lengths, axis=1)
    position = jnp.arange(SEQ, dtype=jnp.int32)
    segment = jnp.sum((position[None, :, None] >= doc_ends[:, None, :]).astype(jnp.int32), axis=2)
    return segment.reshape(MB, SEQS_MB * SEQ)


def plant(values, stream_key, low, largest):
    longest = values.shape.index(max(values.shape))
    spots = []
    for shift in (0, 1):
        where = [jax.random.randint(jax.random.fold_in(stream_key, axis), (), 0, length) for axis, length in enumerate(values.shape)]
        where[longest] = (where[longest] + shift) % values.shape[longest]
        spots.append(tuple(where))
    return values.at[spots[0]].set(low).at[spots[1]].set(largest)


def shard_levels(stream_key, shape, pieces, smallest, top_value):
    factor_of, own = 1.0, jax.random.fold_in(stream_key, 6)
    for dim, blocks in pieces:
        draws = jnp.exp(jax.random.uniform(jax.random.fold_in(own, dim), (blocks,), jnp.float32, smallest / len(pieces), top_value / len(pieces)))
        factor_of = factor_of * jnp.repeat(draws, shape[dim] // blocks).reshape([-1 if axis == dim else 1 for axis in range(len(shape))])
    return factor_of


def noise(stream_key, dims, deviation, bound, split=(), kind=jnp.bfloat16):
    level = shard_levels(stream_key, dims, split, -0.22, 0.18) if split else 1.0
    array = jax.random.normal(stream_key, dims, jnp.float32) * deviation * level
    return jnp.minimum(jnp.maximum(array, -bound), bound).astype(kind)


def setup_inputs(seed: int = 0) -> dict:
    splits = jax.random.split(jax.random.key(seed), 18)
    return {
        "block_in": noise(splits[0], (MB, ROWS, D), 1.0, 6.0, ((1, 32),)),
        "norm1_gain": jnp.clip(1.0 + 0.1 * jax.random.normal(splits[1], (D,), jnp.float32), 0.5, 1.5).astype(jnp.bfloat16),
        "norm1_bias": noise(splits[2], (D,), 0.5, 3.0, ((0, 8),)),
        "w_query": noise(splits[3], (D, D), D ** -0.5, 0.1875, ((0, 8), (1, 4))),
        "w_key": noise(splits[4], (D, D), D ** -0.5, 0.1875, ((0, 8), (1, 4))),
        "w_value": noise(splits[5], (D, D), D ** -0.5, 0.1875, ((0, 8), (1, 4))),
        "w_out": noise(splits[6], (D, D), (D // 64) ** -0.5, 1.5, ((0, 4), (1, 8))),
        "norm2_gain": jnp.clip(1.0 + 0.1 * jax.random.normal(splits[7], (D,), jnp.float32), 0.5, 1.5).astype(jnp.bfloat16),
        "norm2_bias": noise(splits[8], (D,), 0.5, 3.0, ((0, 8),)),
        "w_up": noise(splits[9], (D, FF), D ** -0.5, 0.1875, ((0, 8), (1, 4))),
        "up_bias": noise(splits[10], (TGROUPS, FF_T), 0.5, 3.0, ((0, 4), (1, 8))),
        "w_down": noise(splits[11], (FF, D), (FF // 2) ** -0.5, 0.125, ((0, 4), (1, 8))),
        "down_bias": noise(splits[12], (D,), 0.5, 3.0, ((0, 8),)),
        "segments": draw_segments(jax.random.fold_in(splits[17], 71), 0),
        "rand_blocks": plant(jax.random.randint(splits[14], (MB, SEQS_MB, H, NB, RAND), 0, NB), jax.random.fold_in(splits[14], 1), 0, NB - 1).astype(jnp.int32),
        "glob_blocks": plant(jax.random.randint(splits[15], (MB, SEQS_MB, GLOB), 0, NB), jax.random.fold_in(splits[15], 1), 0, NB - 1).astype(jnp.int32),
        "cotangent": noise(splits[16], (MB, ROWS, D), 1.0, 6.0, ((1, 32),)),
    }


@jax.custom_vjp
def low(v):
    return lax.optimization_barrier(v.astype(jnp.bfloat16)).astype(jnp.float32)

@jax.custom_vjp
def low_back(v):
    return v

def low_keep(v):
    return (low(v), None)

def low_pass(kept, grad):
    return (grad,)

def back_keep(v):
    return (v, None)

def back_low(kept, grad):
    return (low(grad),)
low.defvjp(low_keep, low_pass)
low_back.defvjp(back_keep, back_low)
epsilon = 1e-05
masked_score = -1e+30
highest = lax.Precision.HIGHEST

def matmul(left, right):
    return jnp.dot(left, right, precision=highest, preferred_element_type=jnp.float32)

def layer_norm(rows, gain, shift):
    center = rows - lax.optimization_barrier(jnp.mean(rows, axis=-1, keepdims=True))
    spread = lax.optimization_barrier(jnp.mean(center * center, axis=-1, keepdims=True))
    return center * lax.rsqrt(spread + epsilon) * gain + shift

def gelu_new(preact):
    inner = 0.7978845608028654 * (preact + 0.044715 * preact * preact * preact)
    return 0.5 * preact * (1.0 + jnp.tanh(inner))

def block_table(rand_rows, glob_row):
    block_index = jnp.arange(rand_rows.shape[0], dtype=jnp.int32)
    window = jnp.abs(block_index[:, None] - block_index[None, :]) <= 1
    chosen = jnp.any(rand_rows[:, :, None] == block_index[None, None, :], axis=1)
    glob_hit = jnp.any(glob_row[:, None] == block_index[None, :], axis=0)
    return window | chosen | glob_hit[None, :] | glob_hit[:, None]

def sequence_forward(params, resid_in, segment_row, rand_seq, glob_row):
    gain_one, shift_one, all_query, all_key, all_value, all_out, gain_two, shift_two, all_up, up_shift, all_down, down_shift = params
    length = resid_in.shape[0]
    normed = low(layer_norm(resid_in, gain_one, shift_one))
    query = low(low_back(matmul(normed, all_query)))
    key = low(low_back(matmul(normed, all_key)))
    value = low(low_back(matmul(normed, all_value)))
    same_doc = segment_row[:, None] == segment_row[None, :]

    def one_head(head_item):
        query_head, key_head, value_head, rand_rows = head_item
        table = block_table(rand_rows, glob_row)
        allowed = jnp.repeat(jnp.repeat(table, BLOCK, axis=0), BLOCK, axis=1) & same_doc
        scores = low_back(matmul(query_head, key_head.T) * 0.125)
        scores = jnp.where(allowed, scores, masked_score)
        row_max = lax.optimization_barrier(jnp.max(scores, axis=-1, keepdims=True))
        exponent = jnp.exp(scores - row_max)
        attn_probs = exponent / lax.optimization_barrier(jnp.sum(exponent, axis=-1, keepdims=True))
        return matmul(low(attn_probs), value_head)

    def split_heads(rows):
        return rows.reshape(length, H, HD).transpose(1, 0, 2)
    context = lax.map(jax.checkpoint(one_head), (split_heads(query), split_heads(key), split_heads(value), rand_seq))
    context = low(low_back(context.transpose(1, 0, 2).reshape(length, D)))
    resid = resid_in + low_back(matmul(context, all_out))
    normed_two = low(layer_norm(resid, gain_two, shift_two))
    up_val = low_back(matmul(normed_two, all_up) + up_shift.reshape(-1))
    act = low(gelu_new(up_val))
    return resid + matmul(act, all_down) + down_shift

def reference(block_in, norm1_gain, norm1_bias, w_query, w_key, w_value, w_out, norm2_gain, norm2_bias, w_up, up_bias, w_down, down_bias, segments, rand_blocks, glob_blocks, cotangent):
    params = tuple((argument.astype(jnp.float32) for argument in (norm1_gain, norm1_bias, w_query, w_key, w_value, w_out, norm2_gain, norm2_bias, w_up, up_bias, w_down, down_bias)))
    seq_total = MB * SEQS_MB
    inputs = block_in.astype(jnp.float32).reshape(seq_total, SEQ, D)
    grads_given = cotangent.astype(jnp.float32).reshape(seq_total, SEQ, D)
    seg_rows = segments.reshape(seq_total, SEQ)
    rand_all = rand_blocks.reshape(seq_total, H, NB, RAND)
    glob_all = glob_blocks.reshape(seq_total, GLOB)

    def one_sequence(totals, seq_item):
        resid_in, segment_row, rand_seq, glob_row, grad_rows = seq_item

        def forward(weights, rows):
            return sequence_forward(weights, rows, segment_row, rand_seq, glob_row)
        result, pullback = jax.vjp(forward, params, resid_in)
        weight_grads, input_grad = pullback(grad_rows)
        totals = jax.tree.map(lambda left, right: left + right, totals, weight_grads)
        return (totals, (result.astype(jnp.bfloat16), input_grad))
    zero_grads = jax.tree.map(jnp.zeros_like, params)
    totals, (outputs, input_grads) = lax.scan(one_sequence, zero_grads, (inputs, seg_rows, rand_all, glob_all, grads_given))
    out_shape = (MB, SEQS_MB * SEQ, D)
    return (outputs.reshape(out_shape), input_grads.reshape(out_shape), totals[0], totals[1], totals[2], totals[3], totals[4], totals[5], totals[6], totals[7], totals[8], totals[9], totals[10], totals[11])
```

```python
import functools
import jax
import jax.numpy as jnp
from jax import lax
from jax.sharding import PartitionSpec as P
from jax.experimental import pallas as pl
from jax.experimental.pallas import tpu as pltpu

HD = 64
BLOCK = 64
COMMON = 5
RAND = 3
BIG = 1e30
bf16 = jnp.bfloat16
f32 = jnp.float32


def dot_nt(left, right):
    return lax.dot_general(left, right, (((1,), (1,)), ((), ())), preferred_element_type=f32)


def dot_tn(left, right):
    return lax.dot_general(left, right, (((0,), (0,)), ((), ())), preferred_element_type=f32)


def dot_nn(left, right):
    return lax.dot_general(left, right, (((1,), (0,)), ((), ())), preferred_element_type=f32)


def low_half(shape):
    return lax.broadcasted_iota(jnp.int32, shape, 1) % 128 < HD


def slot_offsets(tab, layout, pair, block):
    common_at, rand_at, blocks, heads = layout
    shared = [
        pl.multiple_of(tab[common_at + block * COMMON + slot], BLOCK) for slot in range(COMMON)
    ]
    first = rand_at + (2 * pair * blocks + block) * RAND
    second = first + blocks * RAND
    drawn = [
        (pl.multiple_of(tab[first + slot], BLOCK), pl.multiple_of(tab[second + slot], BLOCK))
        for slot in range(RAND)
    ]
    return shared, drawn


def gather_rows(ref, shared, drawn, width):
    keep = low_half((BLOCK, width))
    parts = [ref[pl.ds(start, BLOCK), :width] for start in shared]
    for left, right in drawn:
        parts.append(
            jnp.where(keep, ref[pl.ds(left, BLOCK), :width], ref[pl.ds(right, BLOCK), :width])
        )
    return jnp.concatenate(parts, axis=0)


def block_diag(rows):
    keep = low_half(rows.shape)
    zero = jnp.zeros_like(rows)
    return jnp.concatenate([jnp.where(keep, rows, zero), jnp.where(keep, zero, rows)], axis=0)


def fold_heads(rows):
    keep = low_half((BLOCK, 128))
    return jnp.where(keep, rows[:BLOCK], rows[BLOCK:])


def query_rows(qbuf, kaug, start):
    scaled = qbuf[pl.ds(start, BLOCK), :]
    hot = kaug[pl.ds(start, BLOCK), 128:]
    penalty = (hot - jnp.ones_like(hot)) * jnp.asarray(BIG, bf16)
    return block_diag(jnp.concatenate([scaled, penalty], axis=1))


def fill_keys(tab, layout, seg_ref, kaug, half, k_own, k_oth):
    blocks = layout[2]

    @pl.when(pl.program_id(0) == 0)
    def _():
        lane = lax.broadcasted_iota(jnp.int32, (BLOCK, 128), 1) % HD

        def one(block, carry):
            row = pl.multiple_of(tab[block], BLOCK)
            seg = seg_ref[pl.ds(pl.multiple_of(block * BLOCK, BLOCK), BLOCK), :]
            kaug[pl.ds(row, BLOCK), 128:] = jnp.where(seg == lane, 1.0, 0.0).astype(bf16)
            return carry

        lax.fori_loop(0, blocks, one, 0)
        kaug[2 * half :, :128] = jnp.zeros((BLOCK, 128), bf16)
        kaug[2 * half :, 128:] = jnp.where(lane == HD - 1, 1.0, 0.0).astype(bf16)

    kaug[:half, :128] = k_own[0]
    kaug[half : 2 * half, :128] = k_oth[0]


def attn_fwd_kernel(
    layout, unroll, tab, q_own, q_oth, k_own, k_oth, v_own, v_oth, seg_ref,
    out_own, out_oth, lse_ref, kaug, vbuf, qbuf, obuf, sbuf,
):
    pair = pl.program_id(0)
    half = q_own.shape[1]
    blocks = layout[2]
    fill_keys(tab, layout, seg_ref, kaug, half, k_own, k_oth)
    vbuf[:half, :] = v_own[0]
    vbuf[half : 2 * half, :] = v_oth[0]
    vbuf[2 * half :, :] = jnp.zeros((BLOCK, 128), bf16)
    scale = jnp.asarray(0.125, bf16)
    qbuf[:half, :] = q_own[0] * scale
    qbuf[half:, :] = q_oth[0] * scale

    def one_block(block):
        row = pl.multiple_of(tab[block], BLOCK)
        shared, drawn = slot_offsets(tab, layout, pair, block)
        scores = dot_nt(gather_rows(kaug, shared, drawn, 256), query_rows(qbuf, kaug, row))
        top = jnp.max(scores, axis=0, keepdims=True)
        weight = jnp.exp(scores - top)
        total = jnp.sum(weight, axis=0, keepdims=True)
        probs = (weight * (1.0 / total)).astype(bf16)
        context = dot_tn(probs, gather_rows(vbuf, shared, drawn, 128))
        obuf[pl.ds(row, BLOCK), :] = fold_heads(context).astype(bf16)
        lse_ref[0, pl.ds(block, 1), :] = top + jnp.log(total)

    def step(index, carry):
        for part in range(unroll):
            one_block(index * unroll + part)
        return carry

    lax.fori_loop(0, blocks // unroll, step, 0)

    def dense_block(block):
        row = pl.multiple_of(tab[block], BLOCK)
        query = query_rows(qbuf, kaug, row)
        chunk = 512
        count = 2 * half // chunk
        top = jnp.full((1, 128), -3e38, f32)
        for part in range(count):
            scores = dot_nt(kaug[part * chunk : (part + 1) * chunk, :], query)
            sbuf[part * chunk : (part + 1) * chunk, :] = scores
            top = jnp.maximum(top, jnp.max(scores, axis=0, keepdims=True))
        total = jnp.zeros((1, 128), f32)
        for part in range(count):
            weight = jnp.exp(sbuf[part * chunk : (part + 1) * chunk, :] - top)
            sbuf[part * chunk : (part + 1) * chunk, :] = weight
            total = total + jnp.sum(weight, axis=0, keepdims=True)
        inverse = 1.0 / total
        context = jnp.zeros((128, 128), f32)
        for part in range(count):
            probs = (sbuf[part * chunk : (part + 1) * chunk, :] * inverse).astype(bf16)
            context = context + dot_tn(probs, vbuf[part * chunk : (part + 1) * chunk, :])
        obuf[pl.ds(row, BLOCK), :] = fold_heads(context).astype(bf16)
        lse_ref[0, pl.ds(block, 1), :] = top + jnp.log(total)

    first, second = tab[blocks], tab[blocks + 1]

    def dense_step(index, carry):
        dense_block(jnp.where(index == 0, first, second))
        return carry

    lax.fori_loop(0, jnp.where(first == second, 1, 2), dense_step, 0)
    out_own[0] = obuf[:half, :]
    out_oth[0] = obuf[half:, :]


def attn_bwd_kernel(
    layout, unroll, tab, q_own, q_oth, k_own, k_oth, v_own, v_oth, g_own, g_oth, seg_ref, lse_ref,
    dq_own, dq_oth, dk_own, dk_oth, dv_own, dv_oth,
    kaug, vbuf, qbuf, gbuf, dqbuf, dkbuf, dvbuf, sbuf, tbuf,
):
    pair = pl.program_id(0)
    half = q_own.shape[1]
    blocks = layout[2]
    fill_keys(tab, layout, seg_ref, kaug, half, k_own, k_oth)
    vbuf[:half, :] = v_own[0]
    vbuf[half : 2 * half, :] = v_oth[0]
    vbuf[2 * half :, :] = jnp.zeros((BLOCK, 128), bf16)
    scale = jnp.asarray(0.125, bf16)
    qbuf[:half, :] = q_own[0] * scale
    qbuf[half:, :] = q_oth[0] * scale
    gbuf[:half, :] = g_own[0]
    gbuf[half:, :] = g_oth[0]
    dkbuf[...] = jnp.zeros_like(dkbuf)
    dvbuf[...] = jnp.zeros_like(dvbuf)
    keep = low_half((BLOCK, 128))

    def scatter(ref, update, shared, drawn):
        for slot, start in enumerate(shared):
            ref[pl.ds(start, BLOCK), :] += update[slot * BLOCK : (slot + 1) * BLOCK]
        for slot, (left, right) in enumerate(drawn):
            at = (COMMON + slot) * BLOCK
            piece = update[at : at + BLOCK]
            ref[pl.ds(left, BLOCK), :] += jnp.where(keep, piece, 0.0)
            ref[pl.ds(right, BLOCK), :] += jnp.where(keep, 0.0, piece)

    def one_block(block):
        row = pl.multiple_of(tab[block], BLOCK)
        shared, drawn = slot_offsets(tab, layout, pair, block)
        query = query_rows(qbuf, kaug, row)
        grad = block_diag(gbuf[pl.ds(row, BLOCK), :])
        keys = gather_rows(kaug, shared, drawn, 256)
        scores = dot_nt(keys, query)
        probs = jnp.exp(scores - lse_ref[0, pl.ds(block, 1), :])
        grad_probs = dot_nt(gather_rows(vbuf, shared, drawn, 128), grad)
        delta = jnp.sum(probs * grad_probs, axis=0, keepdims=True)
        grad_scores = (probs * (grad_probs - delta)).astype(bf16)
        grad_query = dot_tn(grad_scores, keys[:, :128])
        dqbuf[pl.ds(row, BLOCK), :] = (fold_heads(grad_query) * 0.125).astype(bf16)
        scatter(dkbuf, dot_nn(grad_scores, query[:, :128]), shared, drawn)
        scatter(dvbuf, dot_nn(probs.astype(bf16), grad), shared, drawn)

    def step(index, carry):
        for part in range(unroll):
            one_block(index * unroll + part)
        return carry

    lax.fori_loop(0, blocks // unroll, step, 0)

    def dense_block(block):
        row = pl.multiple_of(tab[block], BLOCK)
        query = query_rows(qbuf, kaug, row)
        grad = block_diag(gbuf[pl.ds(row, BLOCK), :])
        lse = lse_ref[0, pl.ds(block, 1), :]
        chunk = 512
        count = 2 * half // chunk
        delta = jnp.zeros((1, 128), f32)
        for part in range(count):
            here = slice(part * chunk, (part + 1) * chunk)
            probs = jnp.exp(dot_nt(kaug[here, :], query) - lse)
            grad_probs = dot_nt(vbuf[here, :], grad)
            delta = delta + jnp.sum(probs * grad_probs, axis=0, keepdims=True)
            sbuf[here, :] = probs
            tbuf[here, :] = grad_probs
        grad_query = jnp.zeros((128, 128), f32)
        for part in range(count):
            here = slice(part * chunk, (part + 1) * chunk)
            probs = sbuf[here, :]
            grad_scores = (probs * (tbuf[here, :] - delta)).astype(bf16)
            grad_query = grad_query + dot_tn(grad_scores, kaug[here, :128])
            dkbuf[here, :] += dot_nn(grad_scores, query[:, :128])
            dvbuf[here, :] += dot_nn(probs.astype(bf16), grad)
        dqbuf[pl.ds(row, BLOCK), :] = (fold_heads(grad_query) * 0.125).astype(bf16)

    first, second = tab[blocks], tab[blocks + 1]

    def dense_step(index, carry):
        dense_block(jnp.where(index == 0, first, second))
        return carry

    lax.fori_loop(0, jnp.where(first == second, 1, 2), dense_step, 0)
    dq_own[0] = dqbuf[:half, :]
    dq_oth[0] = dqbuf[half:, :]
    dk_own[0] = dkbuf[:half, :].astype(bf16)
    dk_oth[0] = dkbuf[half : 2 * half, :].astype(bf16)
    dv_own[0] = dvbuf[:half, :].astype(bf16)
    dv_oth[0] = dvbuf[half : 2 * half, :].astype(bf16)


def table_layout(blocks, heads):
    common_at = blocks + 2
    rand_at = common_at + blocks * COMMON
    return (common_at, rand_at, blocks, heads)


def attention_table(rand_heads, glob_row, row_of, dummy_row):
    heads, blocks, _ = rand_heads.shape
    index = jnp.arange(blocks, dtype=jnp.int32)
    g0, g1 = glob_row[0], glob_row[1]
    dense = (index == g0) | (index == g1)
    near0, near1 = jnp.abs(index - g0) <= 1, jnp.abs(index - g1) <= 1
    full = jnp.broadcast_to
    shared = jnp.stack([index - 1, index, index + 1, full(g0, (blocks,)), full(g1, (blocks,))], axis=1)
    valid = jnp.stack(
        [index > 0, index >= 0, index < blocks - 1, ~near0, ~near1 & (g1 != g0)], axis=1
    ) & ~dense[:, None]
    shared = jnp.where(valid, row_of(jnp.clip(shared, 0, blocks - 1)), dummy_row)
    far = jnp.abs(rand_heads - index[None, :, None]) > 1
    far = far & (rand_heads != g0) & (rand_heads != g1) & ~dense[None, :, None]
    r0, r1, r2 = rand_heads[..., 0], rand_heads[..., 1], rand_heads[..., 2]
    fresh = jnp.stack([r0 == r0, r1 != r0, (r2 != r0) & (r2 != r1)], axis=-1)
    drawn = jnp.where(far & fresh, row_of(rand_heads), dummy_row)
    return jnp.concatenate(
        [row_of(index), glob_row, shared.reshape(-1), drawn.reshape(-1)]
    ).astype(jnp.int32)


def lane_spec(half, column):
    return pl.BlockSpec((1, half, 128), lambda p, tab: (p // 2, 0, column * 2 + p % 2))


def attn_fwd(tab, qkv_own, qkv_oth, seg_abs, blocks, unroll=4):
    half = qkv_own.shape[1]
    slots = qkv_own.shape[0]
    pairs = 2 * slots
    layout = table_layout(blocks, 2 * pairs)
    rows = 2 * half + BLOCK
    shape = jax.ShapeDtypeStruct((slots, half, 256), bf16)
    return pl.pallas_call(
        functools.partial(attn_fwd_kernel, layout, unroll),
        out_shape=(shape, shape, jax.ShapeDtypeStruct((pairs, blocks, 128), f32)),
        grid_spec=pltpu.PrefetchScalarGridSpec(
            num_scalar_prefetch=1,
            grid=(pairs,),
            in_specs=[
                lane_spec(half, 0), lane_spec(half, 0), lane_spec(half, 1), lane_spec(half, 1),
                lane_spec(half, 2), lane_spec(half, 2),
                pl.BlockSpec((2 * half, 128), lambda p, tab: (0, 0)),
            ],
            out_specs=(
                lane_spec(half, 0), lane_spec(half, 0),
                pl.BlockSpec((1, blocks, 128), lambda p, tab: (p, 0, 0)),
            ),
            scratch_shapes=[
                pltpu.VMEM((rows, 256), bf16), pltpu.VMEM((rows, 128), bf16),
                pltpu.VMEM((2 * half, 128), bf16), pltpu.VMEM((2 * half, 128), bf16),
                pltpu.VMEM((2 * half, 128), f32),
            ],
        ),
        compiler_params=pltpu.CompilerParams(vmem_limit_bytes=40 << 20),
        cost_estimate=pl.CostEstimate(flops=4 * 10**9, bytes_accessed=8 * 10**6, transcendentals=10**7),
        name="attn_fwd",
    )(tab, qkv_own, qkv_oth, qkv_own, qkv_oth, qkv_own, qkv_oth, seg_abs)


def attn_bwd(tab, qkv_own, qkv_oth, grad_own, grad_oth, seg_abs, lse, blocks, unroll=4):
    half = qkv_own.shape[1]
    slots = qkv_own.shape[0]
    pairs = 2 * slots
    layout = table_layout(blocks, 2 * pairs)
    rows = 2 * half + BLOCK
    shape = jax.ShapeDtypeStruct((slots, half, 256), bf16)
    return pl.pallas_call(
        functools.partial(attn_bwd_kernel, layout, unroll),
        out_shape=(shape,) * 6,
        grid_spec=pltpu.PrefetchScalarGridSpec(
            num_scalar_prefetch=1,
            grid=(pairs,),
            in_specs=[
                lane_spec(half, 0), lane_spec(half, 0), lane_spec(half, 1), lane_spec(half, 1),
                lane_spec(half, 2), lane_spec(half, 2), lane_spec(half, 0), lane_spec(half, 0),
                pl.BlockSpec((2 * half, 128), lambda p, tab: (0, 0)),
                pl.BlockSpec((1, blocks, 128), lambda p, tab: (p, 0, 0)),
            ],
            out_specs=(lane_spec(half, 0),) * 6,
            scratch_shapes=[
                pltpu.VMEM((rows, 256), bf16), pltpu.VMEM((rows, 128), bf16),
                pltpu.VMEM((2 * half, 128), bf16), pltpu.VMEM((2 * half, 128), bf16),
                pltpu.VMEM((2 * half, 128), bf16),
                pltpu.VMEM((rows, 128), f32), pltpu.VMEM((rows, 128), f32),
                pltpu.VMEM((2 * half, 128), f32), pltpu.VMEM((2 * half, 128), f32),
            ],
        ),
        compiler_params=pltpu.CompilerParams(vmem_limit_bytes=48 << 20),
        cost_estimate=pl.CostEstimate(flops=10**10, bytes_accessed=16 * 10**6, transcendentals=10**7),
        name="attn_bwd",
    )(tab, qkv_own, qkv_oth, qkv_own, qkv_oth, qkv_own, qkv_oth, grad_own, grad_oth, seg_abs, lse)


EPS = 1e-05
BOTH = ("dp", "tensor")
ROWS = 256


def gelu_pair(u):
    c = 0.7978845608028654
    square = u * u
    bend = jnp.tanh(u * (c + (c * 0.044715) * square))
    half = 0.5 * (1.0 + bend)
    slope = half + (0.5 * u) * (1.0 - bend * bend) * (c + (3.0 * c * 0.044715) * square)
    return u * half, slope


def normalise(rows):
    center = rows - jnp.mean(rows, axis=-1, keepdims=True)
    inverse = lax.rsqrt(jnp.mean(center * center, axis=-1, keepdims=True) + EPS)
    return center * inverse, inverse


def norm_back(grad, unit, inverse, gain):
    scaled = grad * gain
    mean = jnp.mean(scaled, axis=-1, keepdims=True)
    along = jnp.mean(scaled * unit, axis=-1, keepdims=True)
    return inverse * (scaled - mean - unit * along)


def params(mib):
    return pltpu.CompilerParams(vmem_limit_bytes=mib << 20)


def project_kernel(core, x_ref, vec_ref, w_ref, send_ref, own_ref, n_ref, nbuf):
    slot, tile = pl.program_id(0), pl.program_id(1)
    here = pl.ds(pl.multiple_of(tile * ROWS, ROWS), ROWS)

    @pl.when(slot == 0)
    def _():
        unit, _ = normalise(x_ref[...].astype(f32))
        normed = (unit * vec_ref[0:1, :] + vec_ref[1:2, :]).astype(bf16)
        nbuf[here, :] = normed
        n_ref[...] = normed

    width = send_ref.shape[2]
    result = dot_nn(nbuf[here, :], w_ref[0, :, :width]).astype(bf16)

    @pl.when(slot < 2)
    def _():
        send_ref[0] = result

    @pl.when(slot >= 2)
    def _():
        own_ref[0] = result


def project(core, x, vecs, weights):
    rows, width = x.shape
    tiles = rows // ROWS
    out = width * 3 // 4
    shape = jax.ShapeDtypeStruct((2, rows, out), bf16)
    return pl.pallas_call(
        project_kernel,
        out_shape=(shape, shape, jax.ShapeDtypeStruct((rows, width), bf16)),
        grid_spec=pltpu.PrefetchScalarGridSpec(
            num_scalar_prefetch=1,
            grid=(4, tiles),
            in_specs=[
                pl.BlockSpec((ROWS, width), lambda s, i, c: (jnp.where(s == 0, i, tiles - 1), 0)),
                pl.BlockSpec(vecs.shape, lambda s, i, c: (0, 0)),
                pl.BlockSpec((1, width, width), lambda s, i, c: ((2 - 2 * c[0] + s) % 4, 0, 0)),
            ],
            out_specs=(
                pl.BlockSpec(
                    (1, ROWS, out),
                    lambda s, i, c: (jnp.minimum(s, 1), jnp.where(s < 2, i, tiles - 1), 0),
                ),
                pl.BlockSpec(
                    (1, ROWS, out),
                    lambda s, i, c: (jnp.maximum(s - 2, 0), jnp.where(s < 2, 0, i), 0),
                ),
                pl.BlockSpec((ROWS, width), lambda s, i, c: (jnp.where(s == 0, i, tiles - 1), 0)),
            ),
            scratch_shapes=[pltpu.VMEM((rows, width), bf16)],
        ),
        compiler_params=params(40),
        name="project",
    )(core, x, vecs, weights)


def out_kernel(core, x_ref, own_ref, oth_ref, w0, w1, w2, w3, vec_ref, resid_ref, n_ref):
    total = x_ref[...].astype(f32)
    total = total + dot_nt(own_ref[0], w0[0]) + dot_nt(own_ref[1], w1[0])
    total = total + dot_nt(oth_ref[0], w2[0]) + dot_nt(oth_ref[1], w3[0])
    resid_ref[...] = total
    unit, _ = normalise(total)
    n_ref[...] = (unit * vec_ref[2:3, :] + vec_ref[3:4, :]).astype(bf16)


def out_weight_specs(width):
    return [
        pl.BlockSpec((1, width, width // 4), lambda i, c, s=s: ((2 * c[0] + s) % 4, 0, 3))
        for s in range(4)
    ]


def out_project(core, x, ctx_own, ctx_oth, weights, vecs):
    rows, width = x.shape
    tile = pl.BlockSpec((ROWS, width), lambda i, c: (i, 0))
    part = pl.BlockSpec((2, ROWS, width // 4), lambda i, c: (0, i, 0))
    return pl.pallas_call(
        out_kernel,
        out_shape=(
            jax.ShapeDtypeStruct((rows, width), f32), jax.ShapeDtypeStruct((rows, width), bf16),
        ),
        grid_spec=pltpu.PrefetchScalarGridSpec(
            num_scalar_prefetch=1,
            grid=(rows // ROWS,),
            in_specs=[tile, part, part, *out_weight_specs(width),
                      pl.BlockSpec(vecs.shape, lambda i, c: (0, 0))],
            out_specs=(tile, tile),
        ),
        compiler_params=params(32),
        name="out_project",
    )(core, x, ctx_own, ctx_oth, weights, weights, weights, weights, vecs)


def ffn_kernel(n_ref, cot_ref, up_ref, down_ref, bias_ref,
               ffn_ref, gn_ref, gup_ref, gdown_ref, gbias_ref, nt, ct, act, gup):
    slot = pl.program_id(0)
    rows = n_ref.shape[0]

    @pl.when(slot == 0)
    def _():
        for at in range(0, rows, ROWS):
            nt[:, at : at + ROWS] = n_ref[at : at + ROWS, :].T
            ct[:, at : at + ROWS] = cot_ref[at : at + ROWS, :].T
        ffn_ref[...] = jnp.zeros_like(ffn_ref)
        gn_ref[...] = jnp.zeros_like(gn_ref)

    gbias_ref[...] = jnp.zeros_like(gbias_ref)

    def tile(index, carry):
        here = pl.ds(pl.multiple_of(index * ROWS, ROWS), ROWS)
        value = dot_nn(n_ref[here, :], up_ref[0]) + bias_ref[0]
        out, slope = gelu_pair(value)
        out = out.astype(bf16)
        act[here, :] = out
        back = (dot_nn(cot_ref[here, :], down_ref[0]) * slope).astype(bf16)
        gup[here, :] = back
        gbias_ref[0] += jnp.sum(back.astype(f32), axis=0, keepdims=True)
        ffn_ref[here, :] += dot_nt(out, down_ref[0])
        gn_ref[here, :] += dot_nt(back, up_ref[0])
        return carry

    lax.fori_loop(0, rows // ROWS, tile, 0)

    def grads(index, carry):
        here = pl.ds(pl.multiple_of(index * ROWS, ROWS), ROWS)
        gup_ref[0, here, :] = dot_nn(nt[here, :], gup[...]).astype(bf16)
        gdown_ref[0, here, :] = dot_nn(ct[here, :], act[...]).astype(bf16)
        return carry

    lax.fori_loop(0, gup_ref.shape[1] // ROWS, grads, 0)


def feed_forward(normed, cot, up, down, bias):
    rows, width = normed.shape
    slots, _, hidden = up.shape
    once = pl.Buffered(1)
    whole = pl.BlockSpec((rows, width), lambda s: (0, 0), pipeline_mode=once)
    weight = pl.BlockSpec((1, width, hidden), lambda s: (s, 0, 0))
    vector = pl.BlockSpec((1, 1, hidden), lambda s: (s, 0, 0))
    total = pl.BlockSpec((rows, width), lambda s: (0, 0))
    return pl.pallas_call(
        ffn_kernel,
        out_shape=(
            jax.ShapeDtypeStruct((rows, width), f32), jax.ShapeDtypeStruct((rows, width), f32),
            jax.ShapeDtypeStruct(up.shape, bf16), jax.ShapeDtypeStruct(up.shape, bf16),
            jax.ShapeDtypeStruct((slots, 1, hidden), f32),
        ),
        grid=(slots,),
        in_specs=[whole, whole, weight, weight, vector],
        out_specs=(total, total, weight, weight, vector),
        scratch_shapes=[
            pltpu.VMEM((width, rows), bf16), pltpu.VMEM((width, rows), bf16),
            pltpu.VMEM((rows, hidden), bf16), pltpu.VMEM((rows, hidden), bf16),
        ],
        compiler_params=params(58),
        name="feed_forward",
    )(normed, cot, up, down, bias)


def mid_kernel(core, resid_ref, ffn_ref, gn_ref, cot_ref, w0, w1, w2, w3, vec_ref,
               out_ref, gres_ref, low_ref, own_ref, send_ref, sums_ref):
    tile = pl.program_id(0)
    resid = resid_ref[...]
    cot = cot_ref[...].astype(f32)
    out_ref[...] = (resid + ffn_ref[...] + vec_ref[4:5, :]).astype(bf16)
    unit, inverse = normalise(resid)
    grad = gn_ref[...]
    gres = cot + norm_back(grad, unit, inverse, vec_ref[2:3, :])
    gres_ref[...] = gres
    low = gres.astype(bf16)
    low_ref[...] = low
    own_ref[0] = dot_nn(low, w0[0]).astype(bf16)
    own_ref[1] = dot_nn(low, w1[0]).astype(bf16)
    send_ref[0] = dot_nn(low, w2[0]).astype(bf16)
    send_ref[1] = dot_nn(low, w3[0]).astype(bf16)

    @pl.when(tile == 0)
    def _():
        sums_ref[...] = jnp.zeros_like(sums_ref)

    sums_ref[0:1, :] += jnp.sum(grad * unit, axis=0, keepdims=True)
    sums_ref[1:2, :] += jnp.sum(grad, axis=0, keepdims=True)
    sums_ref[2:3, :] += jnp.sum(cot, axis=0, keepdims=True)


def middle(core, resid, ffn, gn, cot, weights, vecs):
    rows, width = resid.shape
    tile = pl.BlockSpec((ROWS, width), lambda i, c: (i, 0))
    part = pl.BlockSpec((2, ROWS, width // 4), lambda i, c: (0, i, 0))
    piece = jax.ShapeDtypeStruct((2, rows, width // 4), bf16)
    return pl.pallas_call(
        mid_kernel,
        out_shape=(
            jax.ShapeDtypeStruct((rows, width), bf16), jax.ShapeDtypeStruct((rows, width), f32),
            jax.ShapeDtypeStruct((rows, width), bf16), piece, piece,
            jax.ShapeDtypeStruct((8, width), f32),
        ),
        grid_spec=pltpu.PrefetchScalarGridSpec(
            num_scalar_prefetch=1,
            grid=(rows // ROWS,),
            in_specs=[tile, tile, tile, tile, *out_weight_specs(width),
                      pl.BlockSpec(vecs.shape, lambda i, c: (0, 0))],
            out_specs=(tile, tile, tile, part, part, pl.BlockSpec((8, width), lambda i, c: (0, 0))),
        ),
        compiler_params=params(48),
        name="middle",
    )(core, resid, ffn, gn, cot, weights, weights, weights, weights, vecs)


def last_kernel(core, x_ref, n_ref, low_ref, gres_ref, dq0, dk0, dv0, c0, dq1, dk1, dv1, c1,
                w_ref, vec_ref, gin_ref, gw_ref, sums_ref, nt, lt, gn):
    slot = pl.program_id(0)
    rows, width = n_ref.shape
    quarter = width // 4

    @pl.when(slot == 0)
    def _():
        for at in range(0, rows, ROWS):
            nt[:, at : at + ROWS] = n_ref[at : at + ROWS, :].T
            lt[:, at : at + ROWS] = low_ref[at : at + ROWS, :].T
        gn[...] = jnp.zeros_like(gn)

    def work(refs):
        def tile(index, carry):
            here = pl.ds(pl.multiple_of(index * ROWS, ROWS), ROWS)
            total = gn[here, :]
            for part in range(3):
                columns = slice(part * quarter, (part + 1) * quarter)
                total = total + dot_nt(refs[part][0, here, :], w_ref[0, :, columns])
            gn[here, :] = total
            return carry

        lax.fori_loop(0, rows // ROWS, tile, 0)

        def grads(index, carry):
            here = pl.ds(pl.multiple_of(index * ROWS, ROWS), ROWS)
            for part in range(4):
                columns = slice(part * quarter, (part + 1) * quarter)
                left = lt if part == 3 else nt
                gw_ref[0, here, columns] = dot_nn(left[here, :], refs[part][0]).astype(bf16)
            return carry

        lax.fori_loop(0, width // ROWS, grads, 0)

    @pl.when(slot < 2)
    def _():
        work((dq0, dk0, dv0, c0))

    @pl.when(slot >= 2)
    def _():
        work((dq1, dk1, dv1, c1))

    @pl.when(slot == 3)
    def _():
        sums_ref[...] = jnp.zeros_like(sums_ref)

        def tile(index, carry):
            here = pl.ds(pl.multiple_of(index * ROWS, ROWS), ROWS)
            unit, inverse = normalise(x_ref[here, :].astype(f32))
            grad = gn[here, :]
            result = gres_ref[here, :] + norm_back(grad, unit, inverse, vec_ref[0:1, :])
            gin_ref[here, :] = result.astype(bf16)
            sums_ref[0:1, :] += jnp.sum(grad * unit, axis=0, keepdims=True)
            sums_ref[1:2, :] += jnp.sum(grad, axis=0, keepdims=True)
            return carry

        lax.fori_loop(0, rows // ROWS, tile, 0)


def last(core, x, normed, low, gres, own, oth, weights, vecs):
    rows, width = x.shape
    once = pl.Buffered(1)
    whole = pl.BlockSpec((rows, width), lambda s, c: (0, 0), pipeline_mode=once)
    first = pl.BlockSpec((1, rows, width // 4), lambda s, c: (jnp.minimum(s, 1), 0, 0))
    second = pl.BlockSpec((1, rows, width // 4), lambda s, c: (jnp.maximum(s - 2, 0), 0, 0))
    weight = pl.BlockSpec((1, width, width), lambda s, c: ((2 * c[0] + s) % 4, 0, 0))
    return pl.pallas_call(
        last_kernel,
        out_shape=(
            jax.ShapeDtypeStruct((rows, width), bf16),
            jax.ShapeDtypeStruct((4, width, width), bf16),
            jax.ShapeDtypeStruct((8, width), f32),
        ),
        grid_spec=pltpu.PrefetchScalarGridSpec(
            num_scalar_prefetch=1,
            grid=(4,),
            in_specs=[whole, whole, whole, whole, *[first] * 4, *[second] * 4, weight,
                      pl.BlockSpec(vecs.shape, lambda s, c: (0, 0))],
            out_specs=(
                pl.BlockSpec((rows, width), lambda s, c: (0, 0)), weight,
                pl.BlockSpec((8, width), lambda s, c: (0, 0)),
            ),
            scratch_shapes=[
                pltpu.VMEM((width, rows), bf16), pltpu.VMEM((width, rows), bf16),
                pltpu.VMEM((rows, width), f32),
            ],
        ),
        compiler_params=params(58),
        name="last",
    )(core, x, normed, low, gres, *own, *oth, weights, vecs)


def token_routes(dp_count, tensor_count, turn):
    routes = []
    for d in range(dp_count):
        for z in range(tensor_count):
            piece = z ^ turn
            target = (d - d % 2 + piece % 2) * tensor_count + 2 * (piece // 2) + d % 2
            routes.append((d * tensor_count + z, target))
    return routes


def per_device(
    block_in, norm1_gain, norm1_bias, w_query, w_key, w_value, w_out, norm2_gain, norm2_bias,
    w_up, up_bias, w_down, down_bias, segments, rand_blocks, glob_blocks, cotangent,
):
    dp_count, tensor_count = lax.axis_size("dp"), lax.axis_size("tensor")
    d, z = lax.axis_index("dp"), lax.axis_index("tensor")
    core = d % 2
    core_ref = core.astype(jnp.int32)[None]
    batches, local, width = block_in.shape
    share = local // 2
    blocks = segments.shape[1] // BLOCK
    swap = [
        (a * tensor_count + b, (a ^ 1) * tensor_count + b)
        for a in range(dp_count)
        for b in range(tensor_count)
    ]

    def other_core(value):
        return lax.ppermute(value, BOTH, swap)

    routes = [token_routes(dp_count, tensor_count, turn) for turn in range(tensor_count)]

    def bring(value):
        pieces = value.reshape(2 * batches, share, width)
        return jnp.concatenate(
            [
                lax.ppermute(
                    lax.dynamic_index_in_dim(pieces, z ^ turn, 0, keepdims=False), BOTH, routes[turn]
                )
                for turn in range(tensor_count)
            ],
            axis=0,
        )

    def give(value):
        back = [
            lax.ppermute(
                value[turn * share : (turn + 1) * share], BOTH, [(b, a) for a, b in routes[turn]]
            )
            for turn in range(tensor_count)
        ]
        low_bit, high_bit = z % 2 == 1, z // 2 == 1
        pairs = [jnp.where(low_bit, back[t ^ 1], back[t]) for t in range(4)]
        whole = [jnp.where(high_bit, pairs[t ^ 2], pairs[t]) for t in range(4)]
        return jnp.stack(whole).reshape(batches, local, width)

    ints = jnp.concatenate([rand_blocks.reshape(batches, -1), glob_blocks.reshape(batches, -1)], axis=1)
    ints = lax.all_gather(ints, "tensor", axis=0, tiled=False)
    head_count = rand_blocks.shape[2]
    mine = jnp.concatenate([ints.reshape(-1), segments.reshape(-1)])
    theirs = other_core(mine)
    mine = jnp.where(z % 2 == core, mine, theirs)
    ints = mine[: ints.size].reshape(ints.shape)[:, z // 2]
    segment_row = lax.dynamic_index_in_dim(
        mine[ints.size * batches :].reshape(segments.shape), z // 2, 0, keepdims=False
    )
    rand_size = head_count * blocks * RAND
    rand_heads = lax.dynamic_slice_in_dim(ints, 2 * core, 2, 0)[:, :rand_size]
    rand_heads = rand_heads.reshape(2 * head_count, blocks, RAND)
    glob_row = ints[0, rand_size:]
    segment_lanes = jnp.broadcast_to(segment_row[:, None], (segment_row.shape[0], 128))
    per_piece = share // BLOCK
    half = tensor_count * share

    def row_of(block):
        source, place = block // (2 * per_piece), block % (2 * per_piece)
        side = place // per_piece
        position = source ^ (2 * (z // 2) + side)
        return (
            jnp.where(side == core, 0, half) + position * share + (place % per_piece) * BLOCK
        )

    table = attention_table(rand_heads, glob_row, row_of, 2 * half)

    vectors = jnp.stack(
        [norm1_gain, norm1_bias, norm2_gain, norm2_bias, down_bias, up_bias[0]]
    )
    vectors = lax.all_gather(vectors, BOTH, axis=0, tiled=False)
    vectors = vectors.reshape(dp_count, tensor_count, 6, -1).astype(f32)
    vecs = vectors[:, 0, :5].transpose(1, 0, 2).reshape(5, width)
    vecs = jnp.concatenate([vecs, jnp.zeros((3, width), f32)])
    up_shift = vectors[:, :, 5].transpose(1, 0, 2).reshape(tensor_count, 1, -1)

    def gather(shard):
        whole = lax.all_gather(shard, ("tensor", "dp"), axis=0, tiled=True)
        return whole.reshape(tensor_count, width, -1)

    attn_weights = gather(jnp.concatenate([w_query, w_key, w_value, w_out.T], axis=1))
    x = bring(block_in)
    cot = bring(cotangent)
    up = gather(w_up)
    down = gather(w_down.T)

    send, own, normed = project(core_ref, x, vecs, attn_weights)
    oth = other_core(send)
    ctx_own, ctx_send, lse = attn_fwd(table, own, oth, segment_lanes, blocks)
    ctx_oth = other_core(ctx_send)
    resid, normed_two = out_project(core_ref, x, ctx_own, ctx_oth, attn_weights, vecs)
    ffn, grad_two, grad_up, grad_down, grad_bias = feed_forward(normed_two, cot, up, down, up_shift)
    out, grad_resid, low, gctx_own, gctx_send, sums_two = middle(
        core_ref, resid, ffn, grad_two, cot, attn_weights, vecs
    )
    gctx_oth = other_core(gctx_send)
    block_out = give(out)
    dq0, dq1, dk0, dk1, dv0, dv1 = attn_bwd(
        table, own, oth, gctx_own, gctx_oth, segment_lanes, lse, blocks
    )
    dq1, dk1, dv1 = other_core(dq1), other_core(dk1), other_core(dv1)
    grad_in, grad_attn, sums_one = last(
        core_ref, x, normed, low, grad_resid,
        (dq0, dk0, dv0, ctx_own), (dq1, dk1, dv1, ctx_oth), attn_weights, vecs,
    )
    grad_in = give(grad_in).astype(f32)

    def scatter(units):
        flat = units.reshape(-1, units.shape[-1])
        return lax.psum_scatter(flat, ("tensor", "dp"), scatter_dimension=0, tiled=True).astype(f32)

    g_up, g_down, g_attn = scatter(grad_up), scatter(grad_down), scatter(grad_attn)
    quarter = width // 4
    five = jnp.concatenate([sums_one[:2], sums_two[:3]]).reshape(5, dp_count, tensor_count, -1)
    five = five.transpose(1, 2, 0, 3).reshape(dp_count * tensor_count, -1)
    shift = grad_bias.reshape(tensor_count, dp_count, -1).transpose(1, 0, 2)
    small = jnp.concatenate([five, shift.reshape(dp_count * tensor_count, -1)], axis=1)
    small = lax.psum_scatter(small, BOTH, scatter_dimension=0, tiled=True)[0]
    piece = width // (dp_count * tensor_count)
    vector_grads = [small[i * piece : (i + 1) * piece] for i in range(5)]
    return (
        block_out, grad_in, vector_grads[0], vector_grads[1],
        g_attn[:, :quarter], g_attn[:, quarter : 2 * quarter], g_attn[:, 2 * quarter : 3 * quarter],
        g_attn[:, 3 * quarter :].T, vector_grads[2], vector_grads[3],
        g_up, small[5 * piece :][None], g_down.T, vector_grads[4],
    )


def solution(mesh):
    rows, both = P(None, BOTH, None), P(BOTH)
    dp, split, turned = P("dp"), P("dp", "tensor"), P("tensor", "dp")
    return jax.shard_map(
        per_device,
        mesh=mesh,
        in_specs=(
            rows, dp, dp, split, split, split, turned, dp, dp, split, turned, turned, dp,
            P(None, "dp"), P(None, "dp", "tensor", None, None), P(None, "dp", None), rows,
        ),
        out_specs=(
            rows, rows, both, both, split, split, split, turned, both, both, split, turned, turned,
            both,
        ),
        check_vma=False,
    )
```

```python
import functools
import jax
import jax.numpy as jnp
from jax import lax
from jax.sharding import PartitionSpec as P
from jax.experimental import pallas as pl
from jax.experimental.pallas import tpu as pltpu

HD = 64
BLOCK = 64
COMMON = 5
RAND = 3
BIG = 1e30
bf16 = jnp.bfloat16
f32 = jnp.float32


def cost(micros):
    return pl.CostEstimate(flops=int(micros * 10**9), bytes_accessed=1000, transcendentals=0)


def dot_nt(left, right):
    return lax.dot_general(left, right, (((1,), (1,)), ((), ())), preferred_element_type=f32)


def dot_tn(left, right):
    return lax.dot_general(left, right, (((0,), (0,)), ((), ())), preferred_element_type=f32)


def dot_nn(left, right):
    return lax.dot_general(left, right, (((1,), (0,)), ((), ())), preferred_element_type=f32)


def low_half(shape):
    return lax.broadcasted_iota(jnp.int32, shape, 1) % 128 < HD


def slot_offsets(tab, layout, pair, block):
    common_at, rand_at, blocks, heads = layout
    shared = [
        pl.multiple_of(tab[common_at + block * COMMON + slot], BLOCK) for slot in range(COMMON)
    ]
    first = rand_at + (2 * pair * blocks + block) * RAND
    second = first + blocks * RAND
    drawn = [
        (pl.multiple_of(tab[first + slot], BLOCK), pl.multiple_of(tab[second + slot], BLOCK))
        for slot in range(RAND)
    ]
    return shared, drawn


def gather_rows(ref, shared, drawn, width):
    keep = low_half((BLOCK, width))
    parts = [ref[pl.ds(start, BLOCK), :width] for start in shared]
    for left, right in drawn:
        parts.append(
            jnp.where(keep, ref[pl.ds(left, BLOCK), :width], ref[pl.ds(right, BLOCK), :width])
        )
    return jnp.concatenate(parts, axis=0)


def block_diag(rows):
    keep = low_half(rows.shape)
    zero = jnp.zeros_like(rows)
    return jnp.concatenate([jnp.where(keep, rows, zero), jnp.where(keep, zero, rows)], axis=0)


def fold_heads(rows):
    keep = low_half((BLOCK, 128))
    return jnp.where(keep, rows[:BLOCK], rows[BLOCK:])


def query_rows(qbuf, kaug, start):
    scaled = qbuf[pl.ds(start, BLOCK), :]
    hot = kaug[pl.ds(start, BLOCK), 128:]
    penalty = (hot - jnp.ones_like(hot)) * jnp.asarray(BIG, bf16)
    return block_diag(jnp.concatenate([scaled, penalty], axis=1))


def fill_keys(tab, layout, seg_ref, kaug, half, k_own, k_oth):
    blocks = layout[2]

    @pl.when(pl.program_id(0) == 0)
    def _():
        lane = lax.broadcasted_iota(jnp.int32, (BLOCK, 128), 1) % HD

        def one(block, carry):
            row = pl.multiple_of(tab[block], BLOCK)
            seg = seg_ref[pl.ds(pl.multiple_of(block * BLOCK, BLOCK), BLOCK), :]
            kaug[pl.ds(row, BLOCK), 128:] = jnp.where(seg == lane, 1.0, 0.0).astype(bf16)
            return carry

        lax.fori_loop(0, blocks, one, 0)
        kaug[2 * half :, :128] = jnp.zeros((BLOCK, 128), bf16)
        kaug[2 * half :, 128:] = jnp.where(lane == HD - 1, 1.0, 0.0).astype(bf16)

    kaug[:half, :128] = k_own[0]
    kaug[half : 2 * half, :128] = k_oth[0]


def attn_fwd_kernel(
    layout, first_pair, unroll, tab, q_own, q_oth, k_own, k_oth, v_own, v_oth, seg_ref,
    out_own, out_oth, lse_ref, kaug, vbuf, qbuf, obuf, sbuf,
):
    pair = first_pair + pl.program_id(0)
    half = q_own.shape[1]
    blocks = layout[2]
    fill_keys(tab, layout, seg_ref, kaug, half, k_own, k_oth)
    vbuf[:half, :] = v_own[0]
    vbuf[half : 2 * half, :] = v_oth[0]
    vbuf[2 * half :, :] = jnp.zeros((BLOCK, 128), bf16)
    scale = jnp.asarray(0.125, bf16)
    qbuf[:half, :] = q_own[0] * scale
    qbuf[half:, :] = q_oth[0] * scale

    def one_block(block):
        row = pl.multiple_of(tab[block], BLOCK)
        shared, drawn = slot_offsets(tab, layout, pair, block)
        scores = dot_nt(gather_rows(kaug, shared, drawn, 256), query_rows(qbuf, kaug, row))
        top = jnp.max(scores, axis=0, keepdims=True)
        weight = jnp.exp(scores - top)
        total = jnp.sum(weight, axis=0, keepdims=True)
        probs = (weight * (1.0 / total)).astype(bf16)
        context = dot_tn(probs, gather_rows(vbuf, shared, drawn, 128))
        obuf[pl.ds(row, BLOCK), :] = fold_heads(context).astype(bf16)
        lse_ref[0, pl.ds(block, 1), :] = top + jnp.log(total)

    def step(index, carry):
        for part in range(unroll):
            one_block(index * unroll + part)
        return carry

    lax.fori_loop(0, blocks // unroll, step, 0)

    def dense_block(block):
        row = pl.multiple_of(tab[block], BLOCK)
        query = query_rows(qbuf, kaug, row)
        chunk = 512
        count = 2 * half // chunk
        top = jnp.full((1, 128), -3e38, f32)
        for part in range(count):
            scores = dot_nt(kaug[part * chunk : (part + 1) * chunk, :], query)
            sbuf[part * chunk : (part + 1) * chunk, :] = scores
            top = jnp.maximum(top, jnp.max(scores, axis=0, keepdims=True))
        total = jnp.zeros((1, 128), f32)
        for part in range(count):
            weight = jnp.exp(sbuf[part * chunk : (part + 1) * chunk, :] - top)
            sbuf[part * chunk : (part + 1) * chunk, :] = weight
            total = total + jnp.sum(weight, axis=0, keepdims=True)
        inverse = 1.0 / total
        context = jnp.zeros((128, 128), f32)
        for part in range(count):
            probs = (sbuf[part * chunk : (part + 1) * chunk, :] * inverse).astype(bf16)
            context = context + dot_tn(probs, vbuf[part * chunk : (part + 1) * chunk, :])
        obuf[pl.ds(row, BLOCK), :] = fold_heads(context).astype(bf16)
        lse_ref[0, pl.ds(block, 1), :] = top + jnp.log(total)

    first, second = tab[blocks], tab[blocks + 1]

    def dense_step(index, carry):
        dense_block(jnp.where(index == 0, first, second))
        return carry

    lax.fori_loop(0, jnp.where(first == second, 1, 2), dense_step, 0)
    out_own[0] = obuf[:half, :]
    out_oth[0] = obuf[half:, :]


def attn_bwd_kernel(
    layout, first_pair, unroll, tab, q_own, q_oth, k_own, k_oth, v_own, v_oth, g_own, g_oth, seg_ref, lse_ref,
    own_ref, oth_ref,
    kaug, vbuf, qbuf, gbuf, dqbuf, dkbuf, dvbuf, sbuf, tbuf,
):
    pair = first_pair + pl.program_id(0)
    half = q_own.shape[1]
    blocks = layout[2]
    fill_keys(tab, layout, seg_ref, kaug, half, k_own, k_oth)
    vbuf[:half, :] = v_own[0]
    vbuf[half : 2 * half, :] = v_oth[0]
    vbuf[2 * half :, :] = jnp.zeros((BLOCK, 128), bf16)
    scale = jnp.asarray(0.125, bf16)
    qbuf[:half, :] = q_own[0] * scale
    qbuf[half:, :] = q_oth[0] * scale
    gbuf[:half, :] = g_own[0]
    gbuf[half:, :] = g_oth[0]
    dkbuf[...] = jnp.zeros_like(dkbuf)
    dvbuf[...] = jnp.zeros_like(dvbuf)
    keep = low_half((BLOCK, 128))

    def scatter(ref, update, shared, drawn):
        for slot, start in enumerate(shared):
            ref[pl.ds(start, BLOCK), :] += update[slot * BLOCK : (slot + 1) * BLOCK]
        for slot, (left, right) in enumerate(drawn):
            at = (COMMON + slot) * BLOCK
            piece = update[at : at + BLOCK]
            ref[pl.ds(left, BLOCK), :] += jnp.where(keep, piece, 0.0)
            ref[pl.ds(right, BLOCK), :] += jnp.where(keep, 0.0, piece)

    def one_block(block):
        row = pl.multiple_of(tab[block], BLOCK)
        shared, drawn = slot_offsets(tab, layout, pair, block)
        query = query_rows(qbuf, kaug, row)
        grad = block_diag(gbuf[pl.ds(row, BLOCK), :])
        keys = gather_rows(kaug, shared, drawn, 256)
        scores = dot_nt(keys, query)
        probs = jnp.exp(scores - lse_ref[0, pl.ds(block, 1), :])
        grad_probs = dot_nt(gather_rows(vbuf, shared, drawn, 128), grad)
        delta = jnp.sum(probs * grad_probs, axis=0, keepdims=True)
        grad_scores = (probs * (grad_probs - delta)).astype(bf16)
        grad_query = dot_tn(grad_scores, keys[:, :128])
        dqbuf[pl.ds(row, BLOCK), :] = (fold_heads(grad_query) * 0.125).astype(bf16)
        scatter(dkbuf, dot_nn(grad_scores, query[:, :128]), shared, drawn)
        scatter(dvbuf, dot_nn(probs.astype(bf16), grad), shared, drawn)

    def step(index, carry):
        for part in range(unroll):
            one_block(index * unroll + part)
        return carry

    lax.fori_loop(0, blocks // unroll, step, 0)

    def dense_block(block):
        row = pl.multiple_of(tab[block], BLOCK)
        query = query_rows(qbuf, kaug, row)
        grad = block_diag(gbuf[pl.ds(row, BLOCK), :])
        lse = lse_ref[0, pl.ds(block, 1), :]
        chunk = 512
        count = 2 * half // chunk
        delta = jnp.zeros((1, 128), f32)
        for part in range(count):
            here = slice(part * chunk, (part + 1) * chunk)
            probs = jnp.exp(dot_nt(kaug[here, :], query) - lse)
            grad_probs = dot_nt(vbuf[here, :], grad)
            delta = delta + jnp.sum(probs * grad_probs, axis=0, keepdims=True)
            sbuf[here, :] = probs
            tbuf[here, :] = grad_probs
        grad_query = jnp.zeros((128, 128), f32)
        for part in range(count):
            here = slice(part * chunk, (part + 1) * chunk)
            probs = sbuf[here, :]
            grad_scores = (probs * (tbuf[here, :] - delta)).astype(bf16)
            grad_query = grad_query + dot_tn(grad_scores, kaug[here, :128])
            dkbuf[here, :] += dot_nn(grad_scores, query[:, :128])
            dvbuf[here, :] += dot_nn(probs.astype(bf16), grad)
        dqbuf[pl.ds(row, BLOCK), :] = (fold_heads(grad_query) * 0.125).astype(bf16)

    first, second = tab[blocks], tab[blocks + 1]

    def dense_step(index, carry):
        dense_block(jnp.where(index == 0, first, second))
        return carry

    lax.fori_loop(0, jnp.where(first == second, 1, 2), dense_step, 0)
    for part, buffer in enumerate((dqbuf, dkbuf, dvbuf)):
        lanes = pl.ds(pl.multiple_of((2 * part + pl.program_id(0)) * 128, 128), 128)
        own_ref[0, :, lanes] = buffer[:half, :].astype(bf16)
        oth_ref[0, :, lanes] = buffer[half : 2 * half, :].astype(bf16)


def table_layout(blocks, heads):
    common_at = blocks + 2
    rand_at = common_at + blocks * COMMON
    return (common_at, rand_at, blocks, heads)


def attention_table(rand_heads, glob_row, row_of, dummy_row):
    heads, blocks, _ = rand_heads.shape
    index = jnp.arange(blocks, dtype=jnp.int32)
    g0, g1 = glob_row[0], glob_row[1]
    dense = (index == g0) | (index == g1)
    near0, near1 = jnp.abs(index - g0) <= 1, jnp.abs(index - g1) <= 1
    full = jnp.broadcast_to
    shared = jnp.stack([index - 1, index, index + 1, full(g0, (blocks,)), full(g1, (blocks,))], axis=1)
    valid = jnp.stack(
        [index > 0, index >= 0, index < blocks - 1, ~near0, ~near1 & (g1 != g0)], axis=1
    ) & ~dense[:, None]
    shared = jnp.where(valid, row_of(jnp.clip(shared, 0, blocks - 1)), dummy_row)
    far = jnp.abs(rand_heads - index[None, :, None]) > 1
    far = far & (rand_heads != g0) & (rand_heads != g1) & ~dense[None, :, None]
    r0, r1, r2 = rand_heads[..., 0], rand_heads[..., 1], rand_heads[..., 2]
    fresh = jnp.stack([r0 == r0, r1 != r0, (r2 != r0) & (r2 != r1)], axis=-1)
    drawn = jnp.where(far & fresh, row_of(rand_heads), dummy_row)
    return jnp.concatenate(
        [row_of(index), glob_row, shared.reshape(-1), drawn.reshape(-1)]
    ).astype(jnp.int32)


def lane_spec(half, slot, column):
    return pl.BlockSpec((1, half, 128), lambda p, tab: (slot, 0, column * 2 + p))


def attn_fwd(tab, qkv_own, qkv_oth, seg_abs, blocks, slot, unroll=4):
    half = qkv_own.shape[1]
    layout = table_layout(blocks, 4 * qkv_own.shape[0])
    rows = 2 * half + BLOCK
    shape = jax.ShapeDtypeStruct((1, half, 256), bf16)
    result = pl.BlockSpec((1, half, 128), lambda p, tab: (0, 0, p))
    return pl.pallas_call(
        functools.partial(attn_fwd_kernel, layout, 2 * slot, unroll),
        out_shape=(shape, shape, jax.ShapeDtypeStruct((2, blocks, 128), f32)),
        grid_spec=pltpu.PrefetchScalarGridSpec(
            num_scalar_prefetch=1,
            grid=(2,),
            in_specs=[
                *[lane_spec(half, slot, column) for column in (0, 0, 1, 1, 2, 2)],
                pl.BlockSpec((2 * half, 128), lambda p, tab: (0, 0)),
            ],
            out_specs=(result, result, pl.BlockSpec((1, blocks, 128), lambda p, tab: (p, 0, 0))),
            scratch_shapes=[
                pltpu.VMEM((rows, 256), bf16), pltpu.VMEM((rows, 128), bf16),
                pltpu.VMEM((2 * half, 128), bf16), pltpu.VMEM((2 * half, 128), bf16),
                pltpu.VMEM((2 * half, 128), f32),
            ],
        ),
        compiler_params=pltpu.CompilerParams(vmem_limit_bytes=40 << 20),
        cost_estimate=cost(32),
        name="attn_fwd",
    )(tab, qkv_own, qkv_oth, qkv_own, qkv_oth, qkv_own, qkv_oth, seg_abs)


def attn_bwd(tab, qkv_own, qkv_oth, grad_own, grad_oth, seg_abs, lse, blocks, slot, unroll=4):
    half = qkv_own.shape[1]
    layout = table_layout(blocks, 4 * qkv_own.shape[0])
    rows = 2 * half + BLOCK
    shape = jax.ShapeDtypeStruct((1, half, 768), bf16)
    result = pl.BlockSpec((1, half, 768), lambda p, tab: (0, 0, 0))
    return pl.pallas_call(
        functools.partial(attn_bwd_kernel, layout, 2 * slot, unroll),
        out_shape=(shape, shape),
        grid_spec=pltpu.PrefetchScalarGridSpec(
            num_scalar_prefetch=1,
            grid=(2,),
            in_specs=[
                *[lane_spec(half, slot, column) for column in (0, 0, 1, 1, 2, 2, 0, 0)],
                pl.BlockSpec((2 * half, 128), lambda p, tab: (0, 0)),
                pl.BlockSpec((1, blocks, 128), lambda p, tab: (p, 0, 0)),
            ],
            out_specs=(result, result),
            scratch_shapes=[
                pltpu.VMEM((rows, 256), bf16), pltpu.VMEM((rows, 128), bf16),
                pltpu.VMEM((2 * half, 128), bf16), pltpu.VMEM((2 * half, 128), bf16),
                pltpu.VMEM((2 * half, 128), bf16),
                pltpu.VMEM((rows, 128), f32), pltpu.VMEM((rows, 128), f32),
                pltpu.VMEM((2 * half, 128), f32), pltpu.VMEM((2 * half, 128), f32),
            ],
        ),
        compiler_params=pltpu.CompilerParams(vmem_limit_bytes=48 << 20),
        cost_estimate=cost(37),
        name="attn_bwd",
    )(tab, qkv_own, qkv_oth, qkv_own, qkv_oth, qkv_own, qkv_oth, grad_own, grad_oth, seg_abs, lse)


EPS = 1e-05
BOTH = ("dp", "tensor")
ROWS = 256


def gelu_pair(u):
    c = 0.7978845608028654
    square = u * u
    bend = jnp.tanh(u * (c + (c * 0.044715) * square))
    half = 0.5 * (1.0 + bend)
    slope = half + (0.5 * u) * (1.0 - bend * bend) * (c + (3.0 * c * 0.044715) * square)
    return u * half, slope


def normalise(rows):
    center = rows - jnp.mean(rows, axis=-1, keepdims=True)
    inverse = lax.rsqrt(jnp.mean(center * center, axis=-1, keepdims=True) + EPS)
    return center * inverse, inverse


def norm_back(grad, unit, inverse, gain):
    scaled = grad * gain
    mean = jnp.mean(scaled, axis=-1, keepdims=True)
    along = jnp.mean(scaled * unit, axis=-1, keepdims=True)
    return inverse * (scaled - mean - unit * along)


def params(mib):
    return pltpu.CompilerParams(vmem_limit_bytes=mib << 20)


def prefetch(grid, in_specs, out_specs, scratch=()):
    return pltpu.PrefetchScalarGridSpec(
        num_scalar_prefetch=1, grid=grid, in_specs=in_specs, out_specs=out_specs,
        scratch_shapes=list(scratch),
    )


def struct(shape, dtype):
    return jax.ShapeDtypeStruct(shape, dtype)


def nn_halves(rows, low_ref, high_ref):
    split = rows.shape[1] // 2
    return dot_nn(rows[:, :split], low_ref) + dot_nn(rows[:, split:], high_ref)


def nt_halves(rows, low_ref, high_ref):
    return jnp.concatenate([dot_nt(rows, low_ref), dot_nt(rows, high_ref)], axis=1)


def chunk_at(d, place, count):
    return d ^ (2 * (place % (count // 2)) + place // (count // 2))


def restore_kernel(count, where, own_ref, oth_ref, out_ref):
    batches, rows, width = oth_ref.shape
    chunk = width // count
    core, d = where[0], where[1]
    for batch in range(batches):
        for place in range(count):
            lanes = slice(place * chunk, (place + 1) * chunk)
            here = pl.ds(pl.multiple_of(chunk_at(d, place, count) * chunk, chunk), chunk)
            out_ref[batch, core, :, here] = own_ref[2 * batch + core, :, lanes].astype(out_ref.dtype)
            there = pl.ds(pl.multiple_of(chunk_at(d ^ 1, place, count) * chunk, chunk), chunk)
            out_ref[batch, 1 - core, :, there] = oth_ref[batch, :, lanes].astype(out_ref.dtype)


def chunk_matrix(d, width, count):
    chunk = width // count
    index = jnp.arange(width, dtype=jnp.int32)
    source = chunk_at(d, index // chunk, count) * chunk + index % chunk
    return (index[:, None] == source[None, :]).astype(bf16)


def restore(where, own, oth, count, dtype):
    batches, rows, width = oth.shape
    core, d = where[0], where[1]
    if (width // count) % 128:
        mine = lax.dynamic_index_in_dim(own.reshape(batches, 2, rows, width), core, 1, False)
        pair = []
        for piece, owner in ((mine, d), (oth, d ^ 1)):
            matrix = chunk_matrix(owner, width, count).T
            pair.append(jnp.dot(piece, matrix, preferred_element_type=f32).astype(dtype))
        return jnp.where(core == 0, jnp.stack(pair, axis=1), jnp.stack(pair[::-1], axis=1))
    whole = lambda shape: pl.BlockSpec(shape, lambda i, w: (0,) * len(shape))
    shape = (batches, 2, rows, width)
    return pl.pallas_call(
        functools.partial(restore_kernel, count),
        out_shape=struct(shape, dtype),
        grid_spec=prefetch((1,), [whole(own.shape), whole(oth.shape)], whole(shape)),
        compiler_params=params(24),
        cost_estimate=cost(3),
        name="restore",
    )(where, own, oth)


def scatter_chunks(where, ref, rows, count):
    chunk = rows.shape[1] // count
    if chunk % 128:
        ref[...] = rows
        return
    for place in range(count):
        target = pl.ds(pl.multiple_of(chunk_at(where[1], place, count) * chunk, chunk), chunk)
        ref[:, target] = rows[:, place * chunk : (place + 1) * chunk]


def gather_chunks(where, ref, count):
    chunk = ref.shape[1] // count
    if chunk % 128:
        return ref[...]
    return jnp.concatenate(
        [
            ref[:, pl.ds(pl.multiple_of(chunk_at(where[1], place, count) * chunk, chunk), chunk)]
            for place in range(count)
        ],
        axis=1,
    )


def project_kernel(count, where, x_ref, vec_ref, wa_ref, wb_ref, out_ref, rel_ref, n_ref, nbuf):
    slot, tile = pl.program_id(0), pl.program_id(1)
    here = pl.ds(pl.multiple_of(tile * ROWS, ROWS), ROWS)

    @pl.when(slot == 0)
    def _():
        rows = gather_chunks(where, x_ref, count)
        rel_ref[...] = rows
        unit, _ = normalise(rows.astype(f32))
        normed = (unit * vec_ref[0:1, :] + vec_ref[1:2, :]).astype(bf16)
        nbuf[here, :] = normed
        n_ref[...] = normed

    out_ref[0] = nn_halves(nbuf[here, :], wa_ref[0], wb_ref[0]).astype(bf16)


def project_more_kernel(where, n_ref, wa_ref, wb_ref, out_ref):
    out_ref[0] = nn_halves(n_ref[...], wa_ref[0], wb_ref[0]).astype(bf16)


def project(where, x, vecs, weights, first, count):
    rows, width = x.shape
    tiles = rows // ROWS
    out = width * 3 // 4
    half = width // 2
    weight = pl.BlockSpec(
        (1, half, out), lambda s, i, w: (2 * (1 - w[0] if first else w[0]) + s, 0, 0)
    )
    outs = pl.BlockSpec((1, ROWS, out), lambda s, i, w: (s, i, 0))
    once = pl.BlockSpec((ROWS, width), lambda s, i, w: (jnp.where(s == 0, i, tiles - 1), 0))
    shape = struct((2, rows, out), bf16)
    if first:
        return pl.pallas_call(
            functools.partial(project_kernel, count),
            out_shape=(shape, struct((rows, width), bf16), struct((rows, width), bf16)),
            grid_spec=prefetch(
                (2, tiles),
                [once, pl.BlockSpec(vecs.shape, lambda s, i, w: (0, 0)), weight, weight],
                (outs, once, once),
                [pltpu.VMEM((rows, width), bf16)],
            ),
            compiler_params=params(32),
            cost_estimate=cost(9),
            name="project",
        )(where, x, vecs, *weights)
    return pl.pallas_call(
        project_more_kernel,
        out_shape=shape,
        grid_spec=prefetch(
            (2, tiles),
            [pl.BlockSpec((ROWS, width), lambda s, i, w: (i, 0)), weight, weight],
            outs,
        ),
        compiler_params=params(32),
        cost_estimate=cost(8),
        name="project_more",
    )(where, x, *weights)


def out_kernel(count, where, x_ref, c0, c1, c2, c3, a0, a1, a2, a3, b0, b1, b2, b3, vec_ref,
               resid_ref, n_ref):
    total = x_ref[...].astype(f32)
    for part, low, high in ((c0, a0, b0), (c1, a1, b1), (c2, a2, b2), (c3, a3, b3)):
        total = total + nt_halves(part[0], low[0], high[0])
    resid_ref[...] = total
    unit, _ = normalise(total)
    scatter_chunks(where, n_ref, (unit * vec_ref[2:3, :] + vec_ref[3:4, :]).astype(bf16), count)


def out_weight_specs(width):
    return [
        pl.BlockSpec((1, width // 2, width // 4), lambda i, w, s=s: ((2 * w[0] + s) % 4, 0, 3))
        for s in range(4)
    ]


def out_project(where, x, contexts, weights, vecs, count):
    rows, width = x.shape
    tile = pl.BlockSpec((ROWS, width), lambda i, w: (i, 0))
    part = pl.BlockSpec((1, ROWS, width // 4), lambda i, w: (0, i, 0))
    return pl.pallas_call(
        functools.partial(out_kernel, count),
        out_shape=(struct((rows, width), f32), struct((rows, width), bf16)),
        grid_spec=prefetch(
            (rows // ROWS,),
            [tile, *[part] * 4, *out_weight_specs(width) * 2,
             pl.BlockSpec(vecs.shape, lambda i, w: (0, 0))],
            (tile, tile),
        ),
        compiler_params=params(32),
        cost_estimate=cost(7),
        name="out_project",
    )(where, x, *contexts, *[weights[0]] * 4, *[weights[1]] * 4, vecs)


def ffn_kernel(first, where, n_ref, cot_ref, nt_in, ct_in, up_ref, down_ref, bias_ref,
               ffn_ref, gn_ref, own_ref, oth_ref, gbias_ref, nt_out, ct_out, nt, ct, act, gup):
    step = pl.program_id(0)
    rows, width = n_ref.shape
    hidden = act.shape[1]
    up = up_ref[...].reshape(width, hidden)
    down = down_ref[...].reshape(width, hidden)
    chunk = own_ref.shape[3]
    count = width // chunk

    @pl.when(step == 0)
    def _():
        if first:
            for index in range(count):
                place = (index % 2 ^ where[0]) * (count // 2) + index // 2
                target = pl.ds(pl.multiple_of(place * chunk, chunk), chunk)
                lanes = slice(index * chunk, (index + 1) * chunk)
                nt[target, :] = n_ref[:, lanes].T
                ct[target, :] = cot_ref[:, lanes].T
            nt_out[...] = nt[...]
            ct_out[...] = ct[...]
        else:
            nt[...] = nt_in[...]
            ct[...] = ct_in[...]
        ffn_ref[...] = jnp.zeros_like(ffn_ref)
        gn_ref[...] = jnp.zeros_like(gn_ref)

    gbias_ref[...] = jnp.zeros_like(gbias_ref)

    def tile(index, carry):
        here = pl.ds(pl.multiple_of(index * ROWS, ROWS), ROWS)
        value = dot_nn(n_ref[here, :], up) + bias_ref[0]
        out, slope = gelu_pair(value)
        out = out.astype(bf16)
        act[here, :] = out
        back = (dot_nn(cot_ref[here, :], down) * slope).astype(bf16)
        gup[here, :] = back
        gbias_ref[0] += jnp.sum(back.astype(f32), axis=0, keepdims=True)
        ffn_ref[here, :] += dot_nt(out, down)
        gn_ref[here, :] += dot_nt(back, up)
        return carry

    lax.fori_loop(0, rows // ROWS, tile, 0)
    many = ROWS // chunk

    for grad_ref, start in ((own_ref, 0), (oth_ref, width // 2)):

        def grads(index, carry, grad_ref=grad_ref, start=start):
            here = pl.ds(pl.multiple_of(start + index * ROWS, ROWS), ROWS)
            there = pl.ds(index * many, many)
            shape = (many, chunk, hidden)
            grad_ref[there, 0, 0] = dot_nn(nt[here, :], gup[...]).astype(bf16).reshape(shape)
            grad_ref[there, 0, 1] = dot_nn(ct[here, :], act[...]).astype(bf16).reshape(shape)
            return carry

        lax.fori_loop(0, width // 2 // ROWS, grads, 0)


def ffn_first_kernel(where, n_ref, cot_ref, up_ref, down_ref, bias_ref,
                     ffn_ref, gn_ref, own_ref, oth_ref, gbias_ref, nt_out, ct_out, *scratch):
    ffn_kernel(True, where, n_ref, cot_ref, None, None, up_ref, down_ref, bias_ref,
               ffn_ref, gn_ref, own_ref, oth_ref, gbias_ref, nt_out, ct_out, *scratch)


def ffn_second_kernel(where, n_ref, cot_ref, nt_in, ct_in, up_ref, down_ref, bias_ref,
                      ffn_ref, gn_ref, own_ref, oth_ref, gbias_ref, *scratch):
    ffn_kernel(False, where, n_ref, cot_ref, nt_in, ct_in, up_ref, down_ref, bias_ref,
               ffn_ref, gn_ref, own_ref, oth_ref, gbias_ref, None, None, *scratch)


def feed_forward(where, normed, cot, weights, bias, turned=None):
    rows, width = normed.shape
    count, slots, _, chunk, hidden = weights.shape
    offset = 0 if turned is None else 2
    once = pl.Buffered(1)
    fixed = lambda shape: pl.BlockSpec(shape, lambda s, w: (0, 0), pipeline_mode=once)
    whole, flipped = fixed((rows, width)), fixed((width, rows))
    slot = lambda s, w: (w[2] + offset + s) % slots
    weight = lambda k: pl.BlockSpec(
        (count, 1, 1, chunk, hidden), lambda s, w: (0, slot(s, w), k, 0, 0)
    )
    grad = pl.BlockSpec((count // 2, 1, 2, chunk, hidden), lambda s, w: (0, s, 0, 0, 0))
    total = pl.BlockSpec((rows, width), lambda s, w: (0, 0))
    shape = struct((count // 2, 2, 2, chunk, hidden), bf16)
    outs = (
        struct((rows, width), f32), struct((rows, width), f32), shape, shape,
        struct((2, 1, hidden), f32),
    )
    out_specs = (total, total, grad, grad, pl.BlockSpec((1, 1, hidden), lambda s, w: (s, 0, 0)))
    vector = pl.BlockSpec((1, 1, hidden), lambda s, w: (slot(s, w), 0, 0))
    if turned is None:
        outs += (struct((width, rows), bf16), struct((width, rows), bf16))
        out_specs += (pl.BlockSpec((width, rows), lambda s, w: (0, 0)),) * 2
    scratch = [
        pltpu.VMEM((width, rows), bf16), pltpu.VMEM((width, rows), bf16),
        pltpu.VMEM((rows, hidden), bf16), pltpu.VMEM((rows, hidden), bf16),
    ]
    return pl.pallas_call(
        ffn_first_kernel if turned is None else ffn_second_kernel,
        out_shape=outs,
        grid_spec=prefetch(
            (2,),
            [whole, whole, *([flipped, flipped] if turned else []), weight(0), weight(1), vector],
            out_specs,
            scratch,
        ),
        compiler_params=params(60),
        cost_estimate=cost(36),
        name="feed_forward",
    )(where, normed, cot, *(turned or ()), weights, weights, bias)


def mid_kernel(count, where, resid_ref, f0_ref, f1_ref, n0_ref, n1_ref, cot_ref, a0, a1, a2, a3, b0, b1, b2, b3, vec_ref,
               out_ref, gres_ref, low_ref, own_ref, send_ref, sums_ref):
    tile = pl.program_id(0)
    resid = resid_ref[...]
    cot = gather_chunks(where, cot_ref, count).astype(f32)
    result = resid + gather_chunks(where, f0_ref, count) + gather_chunks(where, f1_ref, count)
    out_ref[...] = (result + vec_ref[4:5, :]).astype(bf16)
    unit, inverse = normalise(resid)
    grad = gather_chunks(where, n0_ref, count) + gather_chunks(where, n1_ref, count)
    gres = cot + norm_back(grad, unit, inverse, vec_ref[2:3, :])
    gres_ref[...] = gres
    low = gres.astype(bf16)
    low_ref[...] = low
    own_ref[0] = nn_halves(low, a0[0], b0[0]).astype(bf16)
    own_ref[1] = nn_halves(low, a1[0], b1[0]).astype(bf16)
    send_ref[0] = nn_halves(low, a2[0], b2[0]).astype(bf16)
    send_ref[1] = nn_halves(low, a3[0], b3[0]).astype(bf16)

    @pl.when(tile == 0)
    def _():
        sums_ref[...] = jnp.zeros_like(sums_ref)

    sums_ref[0:1, :] += jnp.sum(grad * unit, axis=0, keepdims=True)
    sums_ref[1:2, :] += jnp.sum(grad, axis=0, keepdims=True)
    sums_ref[2:3, :] += jnp.sum(cot, axis=0, keepdims=True)


def middle(where, resid, ffn, gn, cot, weights, vecs, count):
    rows, width = resid.shape
    tile = pl.BlockSpec((ROWS, width), lambda i, w: (i, 0))
    part = pl.BlockSpec((2, ROWS, width // 4), lambda i, w: (0, i, 0))
    piece = struct((2, rows, width // 4), bf16)
    return pl.pallas_call(
        functools.partial(mid_kernel, count),
        out_shape=(
            struct((rows, width), bf16), struct((rows, width), f32), struct((rows, width), bf16),
            piece, piece, struct((8, width), f32),
        ),
        grid_spec=prefetch(
            (rows // ROWS,),
            [*[tile] * 6, *out_weight_specs(width) * 2,
             pl.BlockSpec(vecs.shape, lambda i, w: (0, 0))],
            (tile, tile, tile, part, part, pl.BlockSpec((8, width), lambda i, w: (0, 0))),
        ),
        compiler_params=params(48),
        cost_estimate=cost(12),
        name="middle",
    )(where, resid, *ffn, *gn, cot, *[weights[0]] * 4, *[weights[1]] * 4, vecs)


def qkv_back(nt, lt, refs, context, a_ref, b_ref, total, ga_ref, gb_ref):
    rows, width = total.shape
    quarter, half = width // 4, width // 2

    def tile(index, carry):
        here = pl.ds(pl.multiple_of(index * ROWS, ROWS), ROWS)
        inner = refs[0, here, :]
        total[here, :] += nt_halves(inner, a_ref[0, :, : 3 * quarter], b_ref[0, :, : 3 * quarter])
        return carry

    lax.fori_loop(0, rows // ROWS, tile, 0)

    for grad_ref, start in ((ga_ref, 0), (gb_ref, half)):

        def grads(index, carry, grad_ref=grad_ref, start=start):
            here = pl.ds(pl.multiple_of(index * ROWS, ROWS), ROWS)
            there = pl.ds(pl.multiple_of(start + index * ROWS, ROWS), ROWS)
            grad_ref[0, here, : 3 * quarter] = dot_nn(nt[there, :], refs[0]).astype(bf16)
            grad_ref[0, here, 3 * quarter :] = dot_nn(lt[there, :], context[0]).astype(bf16)
            return carry

        lax.fori_loop(0, half // ROWS, grads, 0)


def early_kernel(where, n_ref, low_ref, d0, c0, d1, c1, a_ref, b_ref,
                 total_ref, ga_ref, gb_ref, nt, lt):
    step = pl.program_id(0)
    rows = n_ref.shape[0]

    @pl.when(step == 0)
    def _():
        for at in range(0, rows, ROWS):
            nt[:, at : at + ROWS] = n_ref[at : at + ROWS, :].T
            lt[:, at : at + ROWS] = low_ref[at : at + ROWS, :].T
        total_ref[...] = jnp.zeros_like(total_ref)
        qkv_back(nt, lt, d0, c0, a_ref, b_ref, total_ref, ga_ref, gb_ref)

    @pl.when(step == 1)
    def _():
        qkv_back(nt, lt, d1, c1, a_ref, b_ref, total_ref, ga_ref, gb_ref)


def late_kernel(where, n_ref, low_ref, d0, c0, d1, c1, a_ref, b_ref, before_ref, x_ref, gres_ref,
                vec_ref, gin_ref, ga_ref, gb_ref, sums_ref, nt, lt, total):
    step = pl.program_id(0)
    rows = n_ref.shape[0]

    @pl.when(step == 0)
    def _():
        for at in range(0, rows, ROWS):
            nt[:, at : at + ROWS] = n_ref[at : at + ROWS, :].T
            lt[:, at : at + ROWS] = low_ref[at : at + ROWS, :].T
        total[...] = before_ref[...]
        qkv_back(nt, lt, d0, c0, a_ref, b_ref, total, ga_ref, gb_ref)

    @pl.when(step == 1)
    def _():
        qkv_back(nt, lt, d1, c1, a_ref, b_ref, total, ga_ref, gb_ref)
        sums_ref[...] = jnp.zeros_like(sums_ref)

        def tile(index, carry):
            here = pl.ds(pl.multiple_of(index * ROWS, ROWS), ROWS)
            unit, inverse = normalise(x_ref[here, :].astype(f32))
            grad = total[here, :]
            result = gres_ref[here, :] + norm_back(grad, unit, inverse, vec_ref[0:1, :])
            gin_ref[here, :] = result.astype(bf16)
            sums_ref[0:1, :] += jnp.sum(grad * unit, axis=0, keepdims=True)
            sums_ref[1:2, :] += jnp.sum(grad, axis=0, keepdims=True)
            return carry

        lax.fori_loop(0, rows // ROWS, tile, 0)


def project_back(where, normed, low, grads, contexts, weights, part, rest=None):
    rows, width = normed.shape
    once = pl.Buffered(1)
    whole = pl.BlockSpec((rows, width), lambda s, w: (0, 0), pipeline_mode=once)
    total = pl.BlockSpec((rows, width), lambda s, w: (0, 0))
    slice_of = lambda lanes: pl.BlockSpec((1, rows, lanes), lambda s, w: (0, 0, 0), pipeline_mode=once)
    side = lambda s, w: jnp.where(s == 0, w[0], 1 - w[0])
    weight = pl.BlockSpec((1, width // 2, width), lambda s, w: (2 * side(s, w) + part, 0, 0))
    grad = pl.BlockSpec((1, width // 2, width), lambda s, w: (side(s, w), 0, 0))
    inner, context = slice_of(width * 3 // 4), slice_of(width // 4)
    shape = struct((2, width // 2, width), bf16)
    specs = [whole, whole, inner, context, inner, context, weight, weight]
    args = (where, normed, low, grads[0], contexts[0], grads[1], contexts[1], *weights)
    turned = [pltpu.VMEM((width, rows), bf16), pltpu.VMEM((width, rows), bf16)]
    if rest is None:
        return pl.pallas_call(
            early_kernel,
            out_shape=(struct((rows, width), f32), shape, shape),
            grid_spec=prefetch((2,), specs, (total, grad, grad), turned),
            compiler_params=params(56),
            cost_estimate=cost(19),
            name="project_back",
        )(*args)
    before, x, gres, vecs = rest
    return pl.pallas_call(
        late_kernel,
        out_shape=(struct((rows, width), bf16), shape, shape, struct((8, width), f32)),
        grid_spec=prefetch(
            (2,),
            [*specs, whole, whole, whole, pl.BlockSpec(vecs.shape, lambda s, w: (0, 0))],
            (total, grad, grad, pl.BlockSpec((8, width), lambda s, w: (0, 0))),
            [*turned, pltpu.VMEM((rows, width), f32)],
        ),
        compiler_params=params(58),
        cost_estimate=cost(25),
        name="project_back_last",
    )(*args, before, x, gres, vecs)


def after(value, *others):
    return lax.optimization_barrier((value, others))[0]


def unpack_kernel(p0, p1, p2, p3, up_ref, down_ref):
    total = p0[...].astype(f32) + p1[...].astype(f32) + p2[...].astype(f32) + p3[...].astype(f32)
    up_ref[...] = total[0]
    down_ref[...] = total[1].T


def unpack_pair(*pairs):
    _, rows, width = pairs[0].shape
    return pl.pallas_call(
        unpack_kernel,
        out_shape=(struct((rows, width), f32), struct((width, rows), f32)),
        compiler_params=params(16),
        name="unpack_pair",
    )(*pairs)


def per_device(
    block_in, norm1_gain, norm1_bias, w_query, w_key, w_value, w_out, norm2_gain, norm2_bias,
    w_up, up_bias, w_down, down_bias, segments, rand_blocks, glob_blocks, cotangent,
):
    dp_count, tensor_count = lax.axis_size("dp"), lax.axis_size("tensor")
    d, z = lax.axis_index("dp").astype(jnp.int32), lax.axis_index("tensor").astype(jnp.int32)
    core = d % 2
    where = jnp.stack([core, d, z])
    batches, local, width = block_in.shape
    share = local // 2
    blocks = segments.shape[1] // BLOCK
    pairs = dp_count // 2

    def move(value, to):
        routes = [
            (a * tensor_count + b, to(a, b)[0] * tensor_count + to(a, b)[1] % tensor_count)
            for a in range(dp_count)
            for b in range(tensor_count)
        ]
        return lax.ppermute(value, BOTH, routes)

    def other_core(value):
        return move(value, lambda a, b: (a ^ 1, b))

    def along(value, step):
        return move(value, lambda a, b: (a, b + step + tensor_count))

    def across(value, r):
        return move(value, lambda a, b: (a ^ (2 * r), b))

    def exchange(value):
        return lax.all_to_all(value, "tensor", split_axis=0, concat_axis=0, tiled=True)

    def half_of(value, which):
        value = value.reshape(batches, 2, share, width)
        return lax.dynamic_index_in_dim(value, which, 1, keepdims=False)

    def both_halves(keep, come):
        both = jnp.where(core == 0, jnp.stack([keep, come], 1), jnp.stack([come, keep], 1))
        return both.reshape(2 * batches * share, width)

    def give(value):
        return exchange(value).reshape(2 * batches, share, width)

    def finish(own, dtype):
        pairs_of = own.reshape(batches, 2, share, width)
        oth = other_core(lax.dynamic_index_in_dim(pairs_of, 1 - core, 1, keepdims=False))
        return restore(where, own, oth, dp_count, dtype).reshape(batches, local, width)


    rand_size = rand_blocks.shape[2] * blocks * RAND
    chunk = norm1_gain.shape[0]
    small = jnp.concatenate(
        [norm1_gain, norm1_bias, norm2_gain, norm2_bias, down_bias, up_bias[0],
         rand_blocks.reshape(-1).astype(bf16), glob_blocks.reshape(-1).astype(bf16)]
    )
    devices = dp_count * tensor_count
    small = jnp.broadcast_to(small[None], (devices, small.shape[0]))
    small = lax.all_to_all(small, BOTH, split_axis=0, concat_axis=0, tiled=True)
    shard = jnp.concatenate([w_query, w_key, w_value, w_out.T], axis=1)
    attn_slots = [along(shard, -k) for k in range(1, tensor_count)]
    their_segments = other_core(segments)
    x_come, cot_come = other_core(half_of(block_in, 1 - core)), other_core(half_of(cotangent, 1 - core))
    small, attn_slots, their_segments, x_come, cot_come = lax.optimization_barrier(
        (small, attn_slots, their_segments, x_come, cot_come)
    )
    small = small.reshape(dp_count, tensor_count, -1)
    vectors = small[..., : 6 * chunk].reshape(dp_count, tensor_count, 6, chunk).astype(f32)
    up_shift = vectors[:, :, 5].transpose(1, 0, 2).reshape(tensor_count, 1, -1)
    places = jnp.arange(dp_count, dtype=jnp.int32)
    order = chunk_at(d, places, dp_count)
    vecs = jnp.take(vectors[:, 0, :5], order, axis=0).transpose(1, 0, 2).reshape(5, width)
    vecs = jnp.concatenate([vecs, jnp.zeros((3, width), f32)])
    ints = lax.dynamic_index_in_dim(small, d - core + z % 2, 0, keepdims=False)[:, 6 * chunk :]
    ints = ints.astype(jnp.int32)
    rand_heads = ints[:, : batches * rand_size].reshape(tensor_count, batches, -1)
    rand_heads = lax.dynamic_index_in_dim(rand_heads, z // 2, 1, keepdims=False)
    rand_heads = lax.dynamic_slice_in_dim(jnp.roll(rand_heads, -z, axis=0), 2 * core, 2, 0)
    rand_heads = rand_heads.reshape(2 * rand_blocks.shape[2], blocks, RAND)
    glob_row = lax.dynamic_index_in_dim(
        ints[0, batches * rand_size :].reshape(batches, -1), z // 2, 0, keepdims=False
    )
    segment_row = lax.dynamic_index_in_dim(
        jnp.where(z % 2 == core, segments, their_segments), z // 2, 0, keepdims=False
    )
    segment_lanes = jnp.broadcast_to(segment_row[:, None], (segment_row.shape[0], 128))
    per_piece = share // BLOCK
    half = tensor_count * share

    def row_of(block):
        source, place = block // (2 * per_piece), block % (2 * per_piece)
        side = place // per_piece
        return jnp.where(side == core, 0, half) + source * share + (place % per_piece) * BLOCK

    table = attention_table(rand_heads, glob_row, row_of, 2 * half)

    attn_slots = jnp.stack([shard, *attn_slots])
    x = exchange(both_halves(half_of(block_in, core), x_come))
    attn_own = [attn_slots] + [across(attn_slots, r) for r in range(1, pairs)]
    pair_shard = after(jnp.stack([w_up, w_down.T]), attn_slots)
    pair_weights = lax.all_gather(pair_shard, BOTH, axis=0, tiled=False)
    pair_weights = pair_weights.reshape(dp_count, tensor_count, 2, *w_up.shape)
    cot_half = both_halves(half_of(cotangent, core), cot_come)
    x, attn_own, table, segment_lanes, vecs, up_shift, cot_half = lax.optimization_barrier(
        (x, attn_own, table, segment_lanes, vecs, up_shift, cot_half)
    )
    attn_own = jnp.concatenate(attn_own, axis=-2)
    attn_weights = (attn_own, other_core(attn_own))
    aligned = chunk % 128 == 0
    own_features = chunk_matrix(d, width, dp_count)
    if not aligned:
        x = jnp.dot(x, own_features, preferred_element_type=f32).astype(bf16)

    send, x, normed = project(where, x, vecs, attn_weights, True, dp_count)
    oth = other_core(send)
    own = project(where, normed, vecs, attn_weights, False, dp_count)
    ctx_own0, ctx_send0, lse0 = attn_fwd(table, own, oth, segment_lanes, blocks, 0)
    ctx_oth0 = other_core(ctx_send0)
    ctx_own1, ctx_send1, lse1 = attn_fwd(table, own, oth, segment_lanes, blocks, 1)
    ctx_oth1 = other_core(ctx_send1)
    cot = exchange(after(cot_half, own))
    resid, normed_two = out_project(
        where, x, (ctx_own0, ctx_own1, ctx_oth0, ctx_oth1), attn_weights, vecs, dp_count
    )
    if not aligned:
        normed_two = jnp.dot(normed_two, own_features.T, preferred_element_type=f32).astype(bf16)
    ffn0, gn0, pair_own0, pair_oth0, bias0, *turned = feed_forward(
        where, normed_two, cot, pair_weights, up_shift
    )
    pair_come0 = other_core(pair_oth0)
    ffn1, gn1, pair_own1, pair_oth1, bias1 = feed_forward(
        where, normed_two, cot, pair_weights, up_shift, turned
    )
    grad_bias = jnp.concatenate([bias0, bias1])
    ffn, grad_two = (ffn0, ffn1), (gn0, gn1)
    if not aligned:
        reorder = lambda v: jnp.dot(
            v, own_features.astype(v.dtype), precision=lax.Precision.HIGHEST,
            preferred_element_type=f32,
        ).astype(v.dtype)
        ffn, grad_two = map(reorder, ffn), map(reorder, grad_two)
        cot = reorder(cot)

    groups = [
        [(2 * xy + c) * tensor_count + t for xy in range(pairs)]
        for c in range(2)
        for t in range(tensor_count)
    ]

    def add_low(left, right):
        return (left.astype(f32) + right.astype(f32)).astype(left.dtype)

    def reduce_groups(total):
        flat = total.reshape(-1, total.shape[-1])
        result = lax.psum_scatter(
            flat, BOTH, scatter_dimension=0, axis_index_groups=groups, tiled=True
        )
        return result.reshape(total.shape[1:])

    pair_come0, ffn1 = lax.optimization_barrier((pair_come0, ffn1))
    ffn = (ffn[0], ffn1) if aligned else tuple(ffn)
    pair_total0 = reduce_groups(add_low(pair_own0, pair_come0))
    pair_come1 = other_core(pair_oth1)
    def reduce_core(own_half, other_half):
        theirs = other_core(other_half)
        size = own_half.shape[-2] // pairs
        return [
            (
                own_half[..., r * size : (r + 1) * size, :].astype(f32)
                + theirs[..., r * size : (r + 1) * size, :].astype(f32)
            ).astype(own_half.dtype)
            for r in range(pairs)
        ]

    def reduce_across(parts):
        total = parts[0].astype(f32)
        for r in range(1, pairs):
            total = total + across(parts[r], r).astype(f32)
        return total.astype(parts[0].dtype)

    def reduce_along(total, slots):
        return sum(
            (along(total[i], k) if k else total[i]).astype(f32) for i, k in enumerate(slots)
        )

    out, grad_resid, low, gctx_own, gctx_send, sums_two = middle(
        where, resid, ffn, tuple(grad_two), cot, attn_weights, vecs, dp_count
    )
    gctx_oth = other_core(gctx_send)
    pair_come1, gctx_oth = lax.optimization_barrier((pair_come1, gctx_oth))
    pair_total1 = reduce_groups(add_low(pair_own1, pair_come1))
    out_back = give(out)
    d_own0, d_send0 = attn_bwd(
        table, own, oth, gctx_own, gctx_oth, segment_lanes, lse0, blocks, 0
    )
    d_send0, out_back = lax.optimization_barrier((d_send0, out_back))
    d_oth0 = other_core(d_send0)
    total_one, ga0, gb0 = project_back(
        where, normed, low, (d_own0, d_oth0), (ctx_own0, ctx_oth0), attn_weights, 0
    )
    attn_parts0 = reduce_core(ga0, gb0)
    out_other = other_core(half_of(out_back, 1 - core))
    lse1, attn_parts0, out_other = lax.optimization_barrier((lse1, attn_parts0, out_other))
    pair_next = [along(pair_total0[1], 1)]
    d_own1, d_send1 = attn_bwd(
        table, own, oth, gctx_own, gctx_oth, segment_lanes, lse1, blocks, 1
    )
    d_send1, pair_next = lax.optimization_barrier((d_send1, pair_next))
    d_oth1 = other_core(d_send1)
    attn_total0 = reduce_across(attn_parts0)
    pair_next += [along(pair_total1[0], 2), along(pair_total1[1], 3)]
    grad_in, ga1, gb1, sums_one = project_back(
        where, normed, low, (d_own1, d_oth1), (ctx_own1, ctx_oth1), attn_weights, 1,
        (total_one, x, grad_resid, vecs),
    )
    block_out = restore(where, out_back, out_other, dp_count, bf16).reshape(batches, local, width)
    attn_total1 = reduce_across(reduce_core(ga1, gb1))
    grad_in = finish(give(grad_in), f32)
    g_attn = reduce_along(attn_total0, (0, 2)) + reduce_along(attn_total1, (1, 3))
    g_up, g_down = unpack_pair(pair_total0[0], *pair_next)

    piece = width // devices
    five = jnp.concatenate([sums_one[:2], sums_two[:3]]).reshape(5, dp_count, chunk)
    relative = places ^ d
    back = (relative % 2) * pairs + relative // 2
    five = jnp.take(five, back, axis=1).reshape(5, devices, piece).transpose(1, 0, 2)
    shift = jnp.roll(grad_bias, z, axis=0)
    shift = shift.reshape(tensor_count, dp_count, -1).transpose(1, 0, 2)
    sums = jnp.concatenate([five.reshape(devices, -1), shift.reshape(devices, -1)], axis=1)
    sums = lax.all_to_all(sums, BOTH, split_axis=0, concat_axis=0, tiled=True)
    sums = jnp.sum(sums, axis=0)
    vector_grads = [sums[i * piece : (i + 1) * piece] for i in range(5)]
    quarter = width // 4
    return (
        block_out, grad_in, vector_grads[0], vector_grads[1],
        g_attn[:, :quarter], g_attn[:, quarter : 2 * quarter], g_attn[:, 2 * quarter : 3 * quarter],
        g_attn[:, 3 * quarter :].T, vector_grads[2], vector_grads[3],
        g_up, sums[5 * piece :][None], g_down, vector_grads[4],
    )


def solution(mesh):
    rows, both = P(None, BOTH, None), P(BOTH)
    dp, split, turned = P("dp"), P("dp", "tensor"), P("tensor", "dp")
    return jax.shard_map(
        per_device,
        mesh=mesh,
        in_specs=(
            rows, dp, dp, split, split, split, turned, dp, dp, split, turned, turned, dp,
            P(None, "dp"), P(None, "dp", "tensor", None, None), P(None, "dp", None), rows,
        ),
        out_specs=(
            rows, rows, both, both, split, split, split, turned, both, both, split, turned, turned,
            both,
        ),
        check_vma=False,
    )
```

```python
import functools
import jax
import jax.numpy as jnp
from jax import lax
from jax.sharding import PartitionSpec as P
from jax.experimental import pallas as pl
from jax.experimental.pallas import tpu as pltpu

HD = 64
BLOCK = 64
COMMON = 5
RAND = 3
BIG = 1e30
bf16 = jnp.bfloat16
f32 = jnp.float32


def cost(micros):
    return pl.CostEstimate(flops=int(micros * 10**9), bytes_accessed=1000, transcendentals=0)


def dot_nt(left, right):
    return lax.dot_general(left, right, (((1,), (1,)), ((), ())), preferred_element_type=f32)


def dot_tn(left, right):
    return lax.dot_general(left, right, (((0,), (0,)), ((), ())), preferred_element_type=f32)


def dot_nn(left, right):
    return lax.dot_general(left, right, (((1,), (0,)), ((), ())), preferred_element_type=f32)


def low_half(shape):
    return lax.broadcasted_iota(jnp.int32, shape, 1) % 128 < HD


def slot_offsets(tab, layout, pair, block):
    common_at, rand_at, blocks, heads = layout
    shared = [
        pl.multiple_of(tab[common_at + block * COMMON + slot], BLOCK) for slot in range(COMMON)
    ]
    first = rand_at + (2 * pair * blocks + block) * RAND
    second = first + blocks * RAND
    drawn = [
        (pl.multiple_of(tab[first + slot], BLOCK), pl.multiple_of(tab[second + slot], BLOCK))
        for slot in range(RAND)
    ]
    return shared, drawn


def gather_rows(ref, shared, drawn, width):
    keep = low_half((BLOCK, width))
    parts = [ref[pl.ds(start, BLOCK), :width] for start in shared]
    for left, right in drawn:
        parts.append(
            jnp.where(keep, ref[pl.ds(left, BLOCK), :width], ref[pl.ds(right, BLOCK), :width])
        )
    return jnp.concatenate(parts, axis=0)


def block_diag(rows):
    keep = low_half(rows.shape)
    zero = jnp.zeros_like(rows)
    return jnp.concatenate([jnp.where(keep, rows, zero), jnp.where(keep, zero, rows)], axis=0)


def fold_heads(rows):
    keep = low_half((BLOCK, 128))
    return jnp.where(keep, rows[:BLOCK], rows[BLOCK:])


def query_rows(qbuf, kaug, start):
    scaled = qbuf[pl.ds(start, BLOCK), :]
    hot = kaug[pl.ds(start, BLOCK), 128:]
    penalty = (hot - jnp.ones_like(hot)) * jnp.asarray(BIG, bf16)
    return block_diag(jnp.concatenate([scaled, penalty], axis=1))


def fill_keys(tab, layout, seg_ref, kaug, half, k_own, k_oth):
    blocks = layout[2]

    @pl.when(pl.program_id(0) == 0)
    def _():
        lane = lax.broadcasted_iota(jnp.int32, (BLOCK, 128), 1) % HD

        def one(block, carry):
            row = pl.multiple_of(tab[block], BLOCK)
            seg = seg_ref[pl.ds(pl.multiple_of(block * BLOCK, BLOCK), BLOCK), :]
            kaug[pl.ds(row, BLOCK), 128:] = jnp.where(seg == lane, 1.0, 0.0).astype(bf16)
            return carry

        lax.fori_loop(0, blocks, one, 0)
        kaug[2 * half :, :128] = jnp.zeros((BLOCK, 128), bf16)
        kaug[2 * half :, 128:] = jnp.where(lane == HD - 1, 1.0, 0.0).astype(bf16)

    kaug[:half, :128] = k_own[0]
    kaug[half : 2 * half, :128] = k_oth[0]


def attn_fwd_kernel(
    layout, first_pair, unroll, tab, q_own, q_oth, k_own, k_oth, v_own, v_oth, seg_ref,
    out_own, out_oth, lse_ref, kaug, vbuf, qbuf, obuf, sbuf,
):
    pair = first_pair + pl.program_id(0)
    half = q_own.shape[1]
    blocks = layout[2]
    fill_keys(tab, layout, seg_ref, kaug, half, k_own, k_oth)
    vbuf[:half, :] = v_own[0]
    vbuf[half : 2 * half, :] = v_oth[0]
    vbuf[2 * half :, :] = jnp.zeros((BLOCK, 128), bf16)
    scale = jnp.asarray(0.125, bf16)
    qbuf[:half, :] = q_own[0] * scale
    qbuf[half:, :] = q_oth[0] * scale

    def one_block(block):
        row = pl.multiple_of(tab[block], BLOCK)
        shared, drawn = slot_offsets(tab, layout, pair, block)
        scores = dot_nt(gather_rows(kaug, shared, drawn, 256), query_rows(qbuf, kaug, row))
        top = jnp.max(scores, axis=0, keepdims=True)
        weight = jnp.exp(scores - top)
        total = jnp.sum(weight, axis=0, keepdims=True)
        probs = (weight * (1.0 / total)).astype(bf16)
        context = dot_tn(probs, gather_rows(vbuf, shared, drawn, 128))
        obuf[pl.ds(row, BLOCK), :] = fold_heads(context).astype(bf16)
        lse_ref[0, pl.ds(block, 1), :] = top + jnp.log(total)

    def step(index, carry):
        for part in range(unroll):
            one_block(index * unroll + part)
        return carry

    lax.fori_loop(0, blocks // unroll, step, 0)

    def dense_block(block):
        row = pl.multiple_of(tab[block], BLOCK)
        query = query_rows(qbuf, kaug, row)
        chunk = 512
        count = 2 * half // chunk
        top = jnp.full((1, 128), -3e38, f32)
        for part in range(count):
            scores = dot_nt(kaug[part * chunk : (part + 1) * chunk, :], query)
            sbuf[part * chunk : (part + 1) * chunk, :] = scores
            top = jnp.maximum(top, jnp.max(scores, axis=0, keepdims=True))
        total = jnp.zeros((1, 128), f32)
        for part in range(count):
            weight = jnp.exp(sbuf[part * chunk : (part + 1) * chunk, :] - top)
            sbuf[part * chunk : (part + 1) * chunk, :] = weight
            total = total + jnp.sum(weight, axis=0, keepdims=True)
        inverse = 1.0 / total
        context = jnp.zeros((128, 128), f32)
        for part in range(count):
            probs = (sbuf[part * chunk : (part + 1) * chunk, :] * inverse).astype(bf16)
            context = context + dot_tn(probs, vbuf[part * chunk : (part + 1) * chunk, :])
        obuf[pl.ds(row, BLOCK), :] = fold_heads(context).astype(bf16)
        lse_ref[0, pl.ds(block, 1), :] = top + jnp.log(total)

    first, second = tab[blocks], tab[blocks + 1]

    def dense_step(index, carry):
        dense_block(jnp.where(index == 0, first, second))
        return carry

    lax.fori_loop(0, jnp.where(first == second, 1, 2), dense_step, 0)
    out_own[0] = obuf[:half, :]
    out_oth[0] = obuf[half:, :]


def attn_bwd_kernel(
    layout, first_pair, unroll, tab, q_own, q_oth, k_own, k_oth, v_own, v_oth, g_own, g_oth, seg_ref, lse_ref,
    own_ref, oth_ref,
    kaug, vbuf, qbuf, gbuf, dqbuf, dkbuf, dvbuf, sbuf, tbuf,
):
    pair = first_pair + pl.program_id(0)
    half = q_own.shape[1]
    blocks = layout[2]
    fill_keys(tab, layout, seg_ref, kaug, half, k_own, k_oth)
    vbuf[:half, :] = v_own[0]
    vbuf[half : 2 * half, :] = v_oth[0]
    vbuf[2 * half :, :] = jnp.zeros((BLOCK, 128), bf16)
    scale = jnp.asarray(0.125, bf16)
    qbuf[:half, :] = q_own[0] * scale
    qbuf[half:, :] = q_oth[0] * scale
    gbuf[:half, :] = g_own[0]
    gbuf[half:, :] = g_oth[0]
    dkbuf[...] = jnp.zeros_like(dkbuf)
    dvbuf[...] = jnp.zeros_like(dvbuf)
    keep = low_half((BLOCK, 128))

    def scatter(ref, update, shared, drawn):
        for slot, start in enumerate(shared):
            ref[pl.ds(start, BLOCK), :] += update[slot * BLOCK : (slot + 1) * BLOCK]
        for slot, (left, right) in enumerate(drawn):
            at = (COMMON + slot) * BLOCK
            piece = update[at : at + BLOCK]
            ref[pl.ds(left, BLOCK), :] += jnp.where(keep, piece, 0.0)
            ref[pl.ds(right, BLOCK), :] += jnp.where(keep, 0.0, piece)

    def one_block(block):
        row = pl.multiple_of(tab[block], BLOCK)
        shared, drawn = slot_offsets(tab, layout, pair, block)
        query = query_rows(qbuf, kaug, row)
        grad = block_diag(gbuf[pl.ds(row, BLOCK), :])
        keys = gather_rows(kaug, shared, drawn, 256)
        scores = dot_nt(keys, query)
        probs = jnp.exp(scores - lse_ref[0, pl.ds(block, 1), :])
        grad_probs = dot_nt(gather_rows(vbuf, shared, drawn, 128), grad)
        delta = jnp.sum(probs * grad_probs, axis=0, keepdims=True)
        grad_scores = (probs * (grad_probs - delta)).astype(bf16)
        grad_query = dot_tn(grad_scores, keys[:, :128])
        dqbuf[pl.ds(row, BLOCK), :] = (fold_heads(grad_query) * 0.125).astype(bf16)
        scatter(dkbuf, dot_nn(grad_scores, query[:, :128]), shared, drawn)
        scatter(dvbuf, dot_nn(probs.astype(bf16), grad), shared, drawn)

    def step(index, carry):
        for part in range(unroll):
            one_block(index * unroll + part)
        return carry

    lax.fori_loop(0, blocks // unroll, step, 0)

    def dense_block(block):
        row = pl.multiple_of(tab[block], BLOCK)
        query = query_rows(qbuf, kaug, row)
        grad = block_diag(gbuf[pl.ds(row, BLOCK), :])
        lse = lse_ref[0, pl.ds(block, 1), :]
        chunk = 512
        count = 2 * half // chunk
        delta = jnp.zeros((1, 128), f32)
        for part in range(count):
            here = slice(part * chunk, (part + 1) * chunk)
            probs = jnp.exp(dot_nt(kaug[here, :], query) - lse)
            grad_probs = dot_nt(vbuf[here, :], grad)
            delta = delta + jnp.sum(probs * grad_probs, axis=0, keepdims=True)
            sbuf[here, :] = probs
            tbuf[here, :] = grad_probs
        grad_query = jnp.zeros((128, 128), f32)
        for part in range(count):
            here = slice(part * chunk, (part + 1) * chunk)
            probs = sbuf[here, :]
            grad_scores = (probs * (tbuf[here, :] - delta)).astype(bf16)
            grad_query = grad_query + dot_tn(grad_scores, kaug[here, :128])
            dkbuf[here, :] += dot_nn(grad_scores, query[:, :128])
            dvbuf[here, :] += dot_nn(probs.astype(bf16), grad)
        dqbuf[pl.ds(row, BLOCK), :] = (fold_heads(grad_query) * 0.125).astype(bf16)

    first, second = tab[blocks], tab[blocks + 1]

    def dense_step(index, carry):
        dense_block(jnp.where(index == 0, first, second))
        return carry

    lax.fori_loop(0, jnp.where(first == second, 1, 2), dense_step, 0)
    for part, buffer in enumerate((dqbuf, dkbuf, dvbuf)):
        lanes = pl.ds(pl.multiple_of((2 * part + pl.program_id(0)) * 128, 128), 128)
        own_ref[0, :, lanes] = buffer[:half, :].astype(bf16)
        oth_ref[0, :, lanes] = buffer[half : 2 * half, :].astype(bf16)


def table_layout(blocks, heads):
    common_at = blocks + 2
    rand_at = common_at + blocks * COMMON
    return (common_at, rand_at, blocks, heads)


def attention_table(rand_heads, glob_row, row_of, dummy_row):
    heads, blocks, _ = rand_heads.shape
    index = jnp.arange(blocks, dtype=jnp.int32)
    g0, g1 = glob_row[0], glob_row[1]
    dense = (index == g0) | (index == g1)
    near0, near1 = jnp.abs(index - g0) <= 1, jnp.abs(index - g1) <= 1
    full = jnp.broadcast_to
    shared = jnp.stack([index - 1, index, index + 1, full(g0, (blocks,)), full(g1, (blocks,))], axis=1)
    valid = jnp.stack(
        [index > 0, index >= 0, index < blocks - 1, ~near0, ~near1 & (g1 != g0)], axis=1
    ) & ~dense[:, None]
    shared = jnp.where(valid, row_of(jnp.clip(shared, 0, blocks - 1)), dummy_row)
    far = jnp.abs(rand_heads - index[None, :, None]) > 1
    far = far & (rand_heads != g0) & (rand_heads != g1) & ~dense[None, :, None]
    r0, r1, r2 = rand_heads[..., 0], rand_heads[..., 1], rand_heads[..., 2]
    fresh = jnp.stack([r0 == r0, r1 != r0, (r2 != r0) & (r2 != r1)], axis=-1)
    drawn = jnp.where(far & fresh, row_of(rand_heads), dummy_row)
    return jnp.concatenate(
        [row_of(index), glob_row, shared.reshape(-1), drawn.reshape(-1)]
    ).astype(jnp.int32)


def lane_spec(half, slot, column):
    return pl.BlockSpec((1, half, 128), lambda p, tab: (slot, 0, column * 2 + p))


def attn_fwd(tab, qkv_own, qkv_oth, seg_abs, blocks, slot, unroll=4):
    half = qkv_own.shape[1]
    layout = table_layout(blocks, 4 * qkv_own.shape[0])
    rows = 2 * half + BLOCK
    shape = jax.ShapeDtypeStruct((1, half, 256), bf16)
    result = pl.BlockSpec((1, half, 128), lambda p, tab: (0, 0, p))
    return pl.pallas_call(
        functools.partial(attn_fwd_kernel, layout, 2 * slot, unroll),
        out_shape=(shape, shape, jax.ShapeDtypeStruct((2, blocks, 128), f32)),
        grid_spec=pltpu.PrefetchScalarGridSpec(
            num_scalar_prefetch=1,
            grid=(2,),
            in_specs=[
                *[lane_spec(half, slot, column) for column in (0, 0, 1, 1, 2, 2)],
                pl.BlockSpec((2 * half, 128), lambda p, tab: (0, 0)),
            ],
            out_specs=(result, result, pl.BlockSpec((1, blocks, 128), lambda p, tab: (p, 0, 0))),
            scratch_shapes=[
                pltpu.VMEM((rows, 256), bf16), pltpu.VMEM((rows, 128), bf16),
                pltpu.VMEM((2 * half, 128), bf16), pltpu.VMEM((2 * half, 128), bf16),
                pltpu.VMEM((2 * half, 128), f32),
            ],
        ),
        compiler_params=pltpu.CompilerParams(vmem_limit_bytes=40 << 20),
        cost_estimate=cost(32),
        name="attn_fwd",
    )(tab, qkv_own, qkv_oth, qkv_own, qkv_oth, qkv_own, qkv_oth, seg_abs)


def attn_bwd(tab, qkv_own, qkv_oth, grad_own, grad_oth, seg_abs, lse, blocks, slot, unroll=4):
    half = qkv_own.shape[1]
    layout = table_layout(blocks, 4 * qkv_own.shape[0])
    rows = 2 * half + BLOCK
    shape = jax.ShapeDtypeStruct((1, half, 768), bf16)
    result = pl.BlockSpec((1, half, 768), lambda p, tab: (0, 0, 0))
    return pl.pallas_call(
        functools.partial(attn_bwd_kernel, layout, 2 * slot, unroll),
        out_shape=(shape, shape),
        grid_spec=pltpu.PrefetchScalarGridSpec(
            num_scalar_prefetch=1,
            grid=(2,),
            in_specs=[
                *[lane_spec(half, slot, column) for column in (0, 0, 1, 1, 2, 2, 0, 0)],
                pl.BlockSpec((2 * half, 128), lambda p, tab: (0, 0)),
                pl.BlockSpec((1, blocks, 128), lambda p, tab: (p, 0, 0)),
            ],
            out_specs=(result, result),
            scratch_shapes=[
                pltpu.VMEM((rows, 256), bf16), pltpu.VMEM((rows, 128), bf16),
                pltpu.VMEM((2 * half, 128), bf16), pltpu.VMEM((2 * half, 128), bf16),
                pltpu.VMEM((2 * half, 128), bf16),
                pltpu.VMEM((rows, 128), f32), pltpu.VMEM((rows, 128), f32),
                pltpu.VMEM((2 * half, 128), f32), pltpu.VMEM((2 * half, 128), f32),
            ],
        ),
        compiler_params=pltpu.CompilerParams(vmem_limit_bytes=48 << 20),
        cost_estimate=cost(37),
        name="attn_bwd",
    )(tab, qkv_own, qkv_oth, qkv_own, qkv_oth, qkv_own, qkv_oth, grad_own, grad_oth, seg_abs, lse)


EPS = 1e-05
BOTH = ("dp", "tensor")
ROWS = 256


def gelu_pair(u):
    c = 0.7978845608028654
    square = u * u
    bend = jnp.tanh(u * (c + (c * 0.044715) * square))
    half = 0.5 * (1.0 + bend)
    slope = half + (0.5 * u) * (1.0 - bend * bend) * (c + (3.0 * c * 0.044715) * square)
    return u * half, slope


def normalise(rows):
    center = rows - jnp.mean(rows, axis=-1, keepdims=True)
    inverse = lax.rsqrt(jnp.mean(center * center, axis=-1, keepdims=True) + EPS)
    return center * inverse, inverse


def norm_back(grad, unit, inverse, gain):
    scaled = grad * gain
    mean = jnp.mean(scaled, axis=-1, keepdims=True)
    along = jnp.mean(scaled * unit, axis=-1, keepdims=True)
    return inverse * (scaled - mean - unit * along)


def params(mib):
    return pltpu.CompilerParams(vmem_limit_bytes=mib << 20)


def prefetch(grid, in_specs, out_specs, scratch=()):
    return pltpu.PrefetchScalarGridSpec(
        num_scalar_prefetch=1, grid=grid, in_specs=in_specs, out_specs=out_specs,
        scratch_shapes=list(scratch),
    )


def struct(shape, dtype):
    return jax.ShapeDtypeStruct(shape, dtype)


def nn_halves(rows, low_ref, high_ref):
    split = rows.shape[1] // 2
    return dot_nn(rows[:, :split], low_ref) + dot_nn(rows[:, split:], high_ref)


def nt_halves(rows, low_ref, high_ref):
    return jnp.concatenate([dot_nt(rows, low_ref), dot_nt(rows, high_ref)], axis=1)


def chunk_at(d, place, count):
    return d ^ (2 * (place % (count // 2)) + place // (count // 2))


def restore_kernel(count, where, own_ref, oth_ref, out_ref):
    batches, rows, width = oth_ref.shape
    chunk = width // count
    core, d = where[0], where[1]
    for batch in range(batches):
        for place in range(count):
            lanes = slice(place * chunk, (place + 1) * chunk)
            here = pl.ds(pl.multiple_of(chunk_at(d, place, count) * chunk, chunk), chunk)
            out_ref[batch, core, :, here] = own_ref[2 * batch + core, :, lanes].astype(out_ref.dtype)
            there = pl.ds(pl.multiple_of(chunk_at(d ^ 1, place, count) * chunk, chunk), chunk)
            out_ref[batch, 1 - core, :, there] = oth_ref[batch, :, lanes].astype(out_ref.dtype)


def restore_direct_kernel(count, where, p0, p1, p2, p3, out_ref):
    width = p0.shape[1]
    chunk = width // count
    core, d, z = where[0], where[1], where[2]
    for turn, piece in enumerate((p0, p1, p2, p3)):
        index = z ^ turn
        sender = d - core + index % 2
        for place in range(count):
            target = pl.ds(pl.multiple_of(chunk_at(sender, place, count) * chunk, chunk), chunk)
            out_ref[index, :, target] = piece[:, place * chunk : (place + 1) * chunk].astype(
                out_ref.dtype
            )


def chunk_matrix(d, width, count):
    chunk = width // count
    index = jnp.arange(width, dtype=jnp.int32)
    source = chunk_at(d, index // chunk, count) * chunk + index % chunk
    return (index[:, None] == source[None, :]).astype(bf16)


def restore(where, own, oth, count, dtype):
    batches, rows, width = oth.shape
    core, d = where[0], where[1]
    if (width // count) % 128:
        mine = lax.dynamic_index_in_dim(own.reshape(batches, 2, rows, width), core, 1, False)
        pair = []
        for piece, owner in ((mine, d), (oth, d ^ 1)):
            matrix = chunk_matrix(owner, width, count).T
            pair.append(jnp.dot(piece, matrix, preferred_element_type=f32).astype(dtype))
        return jnp.where(core == 0, jnp.stack(pair, axis=1), jnp.stack(pair[::-1], axis=1))
    whole = lambda shape: pl.BlockSpec(shape, lambda i, w: (0,) * len(shape))
    shape = (batches, 2, rows, width)
    return pl.pallas_call(
        functools.partial(restore_kernel, count),
        out_shape=struct(shape, dtype),
        grid_spec=prefetch((1,), [whole(own.shape), whole(oth.shape)], whole(shape)),
        compiler_params=params(24),
        cost_estimate=cost(3),
        name="restore",
    )(where, own, oth)


def scatter_chunks(where, ref, rows, count):
    chunk = rows.shape[1] // count
    if chunk % 128:
        ref[...] = rows
        return
    for place in range(count):
        target = pl.ds(pl.multiple_of(chunk_at(where[1], place, count) * chunk, chunk), chunk)
        ref[:, target] = rows[:, place * chunk : (place + 1) * chunk]


def gather_chunks(where, ref, count):
    chunk = ref.shape[1] // count
    if chunk % 128:
        return ref[...]
    return jnp.concatenate(
        [
            ref[:, pl.ds(pl.multiple_of(chunk_at(where[1], place, count) * chunk, chunk), chunk)]
            for place in range(count)
        ],
        axis=1,
    )


def project_kernel(count, where, x_ref, vec_ref, wa_ref, wb_ref, out_ref, rel_ref, n_ref, nbuf):
    slot, tile = pl.program_id(0), pl.program_id(1)
    here = pl.ds(pl.multiple_of(tile * ROWS, ROWS), ROWS)

    @pl.when(slot == 0)
    def _():
        rows = gather_chunks(where, x_ref, count)
        rel_ref[...] = rows
        unit, _ = normalise(rows.astype(f32))
        normed = (unit * vec_ref[0:1, :] + vec_ref[1:2, :]).astype(bf16)
        nbuf[here, :] = normed
        n_ref[...] = normed

    out_ref[0] = nn_halves(nbuf[here, :], wa_ref[0], wb_ref[0]).astype(bf16)


def project_more_kernel(where, n_ref, wa_ref, wb_ref, out_ref):
    out_ref[0] = nn_halves(n_ref[...], wa_ref[0], wb_ref[0]).astype(bf16)


def project(where, x, vecs, weights, first, count):
    rows, width = x.shape
    tiles = rows // ROWS
    out = width * 3 // 4
    half = width // 2
    weight = pl.BlockSpec(
        (1, half, out), lambda s, i, w: (2 * (1 - w[0] if first else w[0]) + s, 0, 0)
    )
    outs = pl.BlockSpec((1, ROWS, out), lambda s, i, w: (s, i, 0))
    once = pl.BlockSpec((ROWS, width), lambda s, i, w: (jnp.where(s == 0, i, tiles - 1), 0))
    shape = struct((2, rows, out), bf16)
    if first:
        return pl.pallas_call(
            functools.partial(project_kernel, count),
            out_shape=(shape, struct((rows, width), bf16), struct((rows, width), bf16)),
            grid_spec=prefetch(
                (2, tiles),
                [once, pl.BlockSpec(vecs.shape, lambda s, i, w: (0, 0)), weight, weight],
                (outs, once, once),
                [pltpu.VMEM((rows, width), bf16)],
            ),
            compiler_params=params(32),
            cost_estimate=cost(9),
            name="project",
        )(where, x, vecs, *weights)
    return pl.pallas_call(
        project_more_kernel,
        out_shape=shape,
        grid_spec=prefetch(
            (2, tiles),
            [pl.BlockSpec((ROWS, width), lambda s, i, w: (i, 0)), weight, weight],
            outs,
        ),
        compiler_params=params(32),
        cost_estimate=cost(8),
        name="project_more",
    )(where, x, *weights)


def out_kernel(count, where, x_ref, c0, c1, c2, c3, a0, a1, a2, a3, b0, b1, b2, b3, vec_ref,
               resid_ref, n_ref):
    total = x_ref[...].astype(f32)
    for part, low, high in ((c0, a0, b0), (c1, a1, b1), (c2, a2, b2), (c3, a3, b3)):
        total = total + nt_halves(part[0], low[0], high[0])
    resid_ref[...] = total
    unit, _ = normalise(total)
    scatter_chunks(where, n_ref, (unit * vec_ref[2:3, :] + vec_ref[3:4, :]).astype(bf16), count)


def out_weight_specs(width):
    return [
        pl.BlockSpec((1, width // 2, width // 4), lambda i, w, s=s: ((2 * w[0] + s) % 4, 0, 3))
        for s in range(4)
    ]


def out_project(where, x, contexts, weights, vecs, count):
    rows, width = x.shape
    tile = pl.BlockSpec((ROWS, width), lambda i, w: (i, 0))
    part = pl.BlockSpec((1, ROWS, width // 4), lambda i, w: (0, i, 0))
    return pl.pallas_call(
        functools.partial(out_kernel, count),
        out_shape=(struct((rows, width), f32), struct((rows, width), bf16)),
        grid_spec=prefetch(
            (rows // ROWS,),
            [tile, *[part] * 4, *out_weight_specs(width) * 2,
             pl.BlockSpec(vecs.shape, lambda i, w: (0, 0))],
            (tile, tile),
        ),
        compiler_params=params(32),
        cost_estimate=cost(7),
        name="out_project",
    )(where, x, *contexts, *[weights[0]] * 4, *[weights[1]] * 4, vecs)


def ffn_kernel(first, n_ref, cot_ref, nt_in, ct_in, up_ref, down_ref, bias_ref,
               ffn_ref, gn_ref, grad_ref, gbias_ref, nt_out, ct_out, nt, ct, act, gup, total, back_total):
    step = pl.program_id(0)
    rows, width = n_ref.shape
    hidden = act.shape[1]
    up = up_ref[...].reshape(width, hidden)
    down = down_ref[...].reshape(width, hidden)

    @pl.when(step == 0)
    def _():
        if first:
            for at in range(0, rows, ROWS):
                nt[:, at : at + ROWS] = n_ref[at : at + ROWS, :].T
                ct[:, at : at + ROWS] = cot_ref[at : at + ROWS, :].T
            nt_out[...] = nt[...]
            ct_out[...] = ct[...]
        total[...] = jnp.zeros_like(total)
        back_total[...] = jnp.zeros_like(back_total)

    if not first:
        nt, ct = nt_in, ct_in
    gbias_ref[...] = jnp.zeros_like(gbias_ref)

    def tile(index, carry):
        here = pl.ds(pl.multiple_of(index * ROWS, ROWS), ROWS)
        value = dot_nn(n_ref[here, :], up) + bias_ref[0]
        out, slope = gelu_pair(value)
        out = out.astype(bf16)
        act[here, :] = out
        back = (dot_nn(cot_ref[here, :], down) * slope).astype(bf16)
        gup[here, :] = back
        gbias_ref[0] += jnp.sum(back.astype(f32), axis=0, keepdims=True)
        total[here, :] += dot_nt(out, down)
        back_total[here, :] += dot_nt(back, up)
        return carry

    lax.fori_loop(0, rows // ROWS, tile, 0)
    chunk = grad_ref.shape[3]
    many = ROWS // chunk

    def grads(index, carry):
        here = pl.ds(pl.multiple_of(index * ROWS, ROWS), ROWS)
        there = pl.ds(index * many, many)
        shape = (many, chunk, hidden)
        grad_ref[there, 0, 0] = dot_nn(nt[here, :], gup[...]).astype(bf16).reshape(shape)
        grad_ref[there, 0, 1] = dot_nn(ct[here, :], act[...]).astype(bf16).reshape(shape)
        return carry

    lax.fori_loop(0, width // ROWS, grads, 0)

    @pl.when(step == pl.num_programs(0) - 1)
    def _():
        ffn_ref[...] = total[...].astype(bf16)
        gn_ref[...] = back_total[...].astype(bf16)


def ffn_first_kernel(where, n_ref, cot_ref, up_ref, down_ref, bias_ref,
                     ffn_ref, gn_ref, grad_ref, gbias_ref, nt_out, ct_out, nt, ct, *scratch):
    ffn_kernel(True, n_ref, cot_ref, None, None, up_ref, down_ref, bias_ref,
               ffn_ref, gn_ref, grad_ref, gbias_ref, nt_out, ct_out, nt, ct, *scratch)


def ffn_second_kernel(where, n_ref, cot_ref, nt_in, ct_in, up_ref, down_ref, bias_ref,
                      ffn_ref, gn_ref, grad_ref, gbias_ref, *scratch):
    ffn_kernel(False, n_ref, cot_ref, nt_in, ct_in, up_ref, down_ref, bias_ref,
               ffn_ref, gn_ref, grad_ref, gbias_ref, None, None, None, None, *scratch)


def feed_forward(where, normed, cot, weights, bias, slots_at, turned=None):
    rows, width = normed.shape
    count, slots, _, chunk, hidden = weights.shape
    once = pl.Buffered(1)
    fixed = lambda shape: pl.BlockSpec(shape, lambda s, w: (0, 0), pipeline_mode=once)
    whole, flipped = fixed((rows, width)), fixed((width, rows))
    slot = lambda s, w: (w[2] + slots_at + s) % slots
    weight = lambda k: pl.BlockSpec(
        (count, 1, 1, chunk, hidden), lambda s, w: (0, slot(s, w), k, 0, 0)
    )
    grad = pl.BlockSpec((count, 1, 2, chunk, hidden), lambda s, w: (0, s, 0, 0, 0))
    total = pl.BlockSpec((rows, width), lambda s, w: (0, 0))
    outs = (
        struct((rows, width), bf16), struct((rows, width), bf16),
        struct((count, 2, 2, chunk, hidden), bf16), struct((2, 1, hidden), f32),
    )
    out_specs = (total, total, grad, pl.BlockSpec((1, 1, hidden), lambda s, w: (s, 0, 0)))
    vector = pl.BlockSpec((1, 1, hidden), lambda s, w: (slot(s, w), 0, 0))
    scratch = [
        pltpu.VMEM((rows, hidden), bf16), pltpu.VMEM((rows, hidden), bf16),
        pltpu.VMEM((rows, width), f32), pltpu.VMEM((rows, width), f32),
    ]
    if turned is None:
        outs += (struct((width, rows), bf16), struct((width, rows), bf16))
        out_specs += (pl.BlockSpec((width, rows), lambda s, w: (0, 0)),) * 2
        scratch = [pltpu.VMEM((width, rows), bf16), pltpu.VMEM((width, rows), bf16), *scratch]
    return pl.pallas_call(
        ffn_first_kernel if turned is None else ffn_second_kernel,
        out_shape=outs,
        grid_spec=prefetch(
            (2,),
            [whole, whole, *([flipped, flipped] if turned else []), weight(0), weight(1), vector],
            out_specs,
            scratch,
        ),
        compiler_params=params(60),
        cost_estimate=cost(36),
        name="feed_forward",
    )(where, normed, cot, *(turned or ()), weights, weights, bias)


def mid_kernel(count, where, resid_ref, f0_ref, f1_ref, n0_ref, n1_ref, cot_ref, a0, a1, a2, a3, b0, b1, b2, b3, vec_ref,
               out_ref, gres_ref, low_ref, own_ref, send_ref, sums_ref):
    tile = pl.program_id(0)
    resid = resid_ref[...]
    cot = gather_chunks(where, cot_ref, count).astype(f32)
    result = resid + gather_chunks(where, f0_ref, count).astype(f32)
    result = result + gather_chunks(where, f1_ref, count).astype(f32)
    out_ref[...] = (result + vec_ref[4:5, :]).astype(bf16)
    unit, inverse = normalise(resid)
    grad = gather_chunks(where, n0_ref, count).astype(f32)
    grad = grad + gather_chunks(where, n1_ref, count).astype(f32)
    gres = cot + norm_back(grad, unit, inverse, vec_ref[2:3, :])
    gres_ref[...] = gres
    low = gres.astype(bf16)
    low_ref[...] = low
    own_ref[0] = nn_halves(low, a0[0], b0[0]).astype(bf16)
    own_ref[1] = nn_halves(low, a1[0], b1[0]).astype(bf16)
    send_ref[0] = nn_halves(low, a2[0], b2[0]).astype(bf16)
    send_ref[1] = nn_halves(low, a3[0], b3[0]).astype(bf16)

    @pl.when(tile == 0)
    def _():
        sums_ref[...] = jnp.zeros_like(sums_ref)

    sums_ref[0:1, :] += jnp.sum(grad * unit, axis=0, keepdims=True)
    sums_ref[1:2, :] += jnp.sum(grad, axis=0, keepdims=True)
    sums_ref[2:3, :] += jnp.sum(cot, axis=0, keepdims=True)


def middle(where, resid, ffn, gn, cot, weights, vecs, count):
    rows, width = resid.shape
    tile = pl.BlockSpec((ROWS, width), lambda i, w: (i, 0))
    part = pl.BlockSpec((2, ROWS, width // 4), lambda i, w: (0, i, 0))
    piece = struct((2, rows, width // 4), bf16)
    return pl.pallas_call(
        functools.partial(mid_kernel, count),
        out_shape=(
            struct((rows, width), bf16), struct((rows, width), f32), struct((rows, width), bf16),
            piece, piece, struct((8, width), f32),
        ),
        grid_spec=prefetch(
            (rows // ROWS,),
            [*[tile] * 6, *out_weight_specs(width) * 2,
             pl.BlockSpec(vecs.shape, lambda i, w: (0, 0))],
            (tile, tile, tile, part, part, pl.BlockSpec((8, width), lambda i, w: (0, 0))),
        ),
        compiler_params=params(48),
        cost_estimate=cost(12),
        name="middle",
    )(where, resid, *ffn, *gn, cot, *[weights[0]] * 4, *[weights[1]] * 4, vecs)


def token_part(inner, a_ref, b_ref, total):
    lanes = inner.shape[2]

    def tile(index, carry):
        here = pl.ds(pl.multiple_of(index * ROWS, ROWS), ROWS)
        total[here, :] += nt_halves(inner[0, here, :], a_ref[0, :, :lanes], b_ref[0, :, :lanes])
        return carry

    lax.fori_loop(0, total.shape[0] // ROWS, tile, 0)


def weight_part(nt, lt, inner, context, ga_ref, gb_ref):
    lanes = inner.shape[2]
    half = ga_ref.shape[1]
    for grad_ref, start in ((ga_ref, 0), (gb_ref, half)):

        def grads(index, carry, grad_ref=grad_ref, start=start):
            here = pl.ds(pl.multiple_of(index * ROWS, ROWS), ROWS)
            there = pl.ds(pl.multiple_of(start + index * ROWS, ROWS), ROWS)
            grad_ref[0, here, :lanes] = dot_nn(nt[there, :], inner[0]).astype(bf16)
            grad_ref[0, here, lanes:] = dot_nn(lt[there, :], context[0]).astype(bf16)
            return carry

        lax.fori_loop(0, half // ROWS, grads, 0)


def turn_rows(source, target):
    for at in range(0, source.shape[0], ROWS):
        target[:, at : at + ROWS] = source[at : at + ROWS, :].T


def back_early_kernel(where, d0, d1, a_ref, b_ref, n_ref, low_ref, c0, c1,
                      total_ref, ga_ref, gb_ref, nt_ref, lt_ref):
    step = pl.program_id(0)

    @pl.when(step == 0)
    def _():
        turn_rows(n_ref, nt_ref)
        turn_rows(low_ref, lt_ref)
        total_ref[...] = jnp.zeros_like(total_ref)
        token_part(d0, a_ref, b_ref, total_ref)
        weight_part(nt_ref, lt_ref, d0, c0, ga_ref, gb_ref)

    @pl.when(step == 1)
    def _():
        token_part(d1, a_ref, b_ref, total_ref)
        weight_part(nt_ref, lt_ref, d1, c1, ga_ref, gb_ref)


def back_tokens_kernel(where, d0, d1, a0, b0, a1, b1, before_ref, x_ref, gres_ref, vec_ref,
                       gin_ref, sums_ref):
    lanes = d0.shape[2]
    grad = before_ref[...] + nt_halves(d0[0], a0[0, :, :lanes], b0[0, :, :lanes])
    grad = grad + nt_halves(d1[0], a1[0, :, :lanes], b1[0, :, :lanes])
    unit, inverse = normalise(x_ref[...].astype(f32))
    result = gres_ref[...] + norm_back(grad, unit, inverse, vec_ref[0:1, :])
    gin_ref[...] = result.astype(bf16)

    @pl.when(pl.program_id(0) == 0)
    def _():
        sums_ref[...] = jnp.zeros_like(sums_ref)

    sums_ref[0:1, :] += jnp.sum(grad * unit, axis=0, keepdims=True)
    sums_ref[1:2, :] += jnp.sum(grad, axis=0, keepdims=True)


def back_weights_kernel(where, d0, d1, nt_ref, lt_ref, c0, c1, ga_ref, gb_ref):
    step = pl.program_id(0)

    @pl.when(step == 0)
    def _():
        weight_part(nt_ref, lt_ref, d0, c0, ga_ref, gb_ref)

    @pl.when(step == 1)
    def _():
        weight_part(nt_ref, lt_ref, d1, c1, ga_ref, gb_ref)


def side(s, w):
    return jnp.where(s == 0, w[0], 1 - w[0])


def fixed_spec(shape):
    return pl.BlockSpec(shape, lambda s, w: (0,) * len(shape), pipeline_mode=pl.Buffered(1))


def back_early(where, normed, low, grads, contexts, weights, part):
    rows, width = normed.shape
    whole, total = fixed_spec((rows, width)), pl.BlockSpec((rows, width), lambda s, w: (0, 0))
    inner, context = fixed_spec((1, rows, width * 3 // 4)), fixed_spec((1, rows, width // 4))
    weight = pl.BlockSpec((1, width // 2, width), lambda s, w: (2 * side(s, w) + part, 0, 0))
    grad = pl.BlockSpec((1, width // 2, width), lambda s, w: (side(s, w), 0, 0))
    shape = struct((2, width // 2, width), bf16)
    turned = struct((width, rows), bf16)
    return pl.pallas_call(
        back_early_kernel,
        out_shape=(struct((rows, width), f32), shape, shape, turned, turned),
        grid_spec=prefetch(
            (2,), [inner, inner, weight, weight, whole, whole, context, context],
            (total, grad, grad, total, total),
        ),
        compiler_params=params(56),
        cost_estimate=cost(19),
        name="back_early",
    )(where, *grads, *weights, normed, low, *contexts)


def back_tokens(where, grads, weights, part, before, x, gres, vecs):
    rows, width = x.shape
    tile = pl.BlockSpec((ROWS, width), lambda i, w: (i, 0))
    inner = pl.BlockSpec((1, ROWS, width * 3 // 4), lambda i, w: (0, i, 0))
    weight = lambda s: pl.BlockSpec(
        (1, width // 2, width), lambda i, w: (2 * side(s, w) + part, 0, 0)
    )
    return pl.pallas_call(
        back_tokens_kernel,
        out_shape=(struct((rows, width), bf16), struct((8, width), f32)),
        grid_spec=prefetch(
            (rows // ROWS,),
            [inner, inner, weight(0), weight(0), weight(1), weight(1), tile, tile, tile,
             pl.BlockSpec(vecs.shape, lambda i, w: (0, 0))],
            (
                pl.BlockSpec((ROWS, width), lambda i, w: (i ^ (w[2] // 2 * 2 + w[0]), 0)),
                pl.BlockSpec((8, width), lambda i, w: (0, 0)),
            ),
        ),
        compiler_params=params(48),
        cost_estimate=cost(11),
        name="back_tokens",
    )(where, *grads, *weights, *weights, before, x, gres, vecs)


def back_weights(where, grads, contexts, turned):
    width, rows = turned[0].shape
    inner, context = fixed_spec((1, rows, width * 3 // 4)), fixed_spec((1, rows, width // 4))
    grad = pl.BlockSpec((1, width // 2, width), lambda s, w: (side(s, w), 0, 0))
    shape = struct((2, width // 2, width), bf16)
    return pl.pallas_call(
        back_weights_kernel,
        out_shape=(shape, shape),
        grid_spec=prefetch(
            (2,), [inner, inner, *[fixed_spec((width, rows))] * 2, context, context], (grad, grad)
        ),
        compiler_params=params(40),
        cost_estimate=cost(10),
        name="back_weights",
    )(where, *grads, *turned, *contexts)


def restore_direct(where, pieces, count, dtype):
    rows, width = pieces[0].shape
    if (width // count) % 128:
        core, d, z = where[0], where[1], where[2]
        fixed = []
        for turn, piece in enumerate(pieces):
            matrix = chunk_matrix(d - core + (z ^ turn) % 2, width, count)
            fixed.append(jnp.dot(piece, matrix.T, preferred_element_type=f32).astype(dtype))
        fixed = jnp.stack(fixed)
        return jnp.stack([lax.dynamic_index_in_dim(fixed, z ^ i, 0, False) for i in range(4)])
    whole = lambda shape: pl.BlockSpec(shape, lambda i, w: (0,) * len(shape))
    return pl.pallas_call(
        functools.partial(restore_direct_kernel, count),
        out_shape=struct((4, rows, width), dtype),
        grid_spec=prefetch((1,), [whole((rows, width))] * 4, whole((4, rows, width))),
        compiler_params=params(24),
        cost_estimate=cost(4),
        name="restore_direct",
    )(where, *pieces)


def token_routes(dp_count, tensor_count, turn):
    routes = []
    for d in range(dp_count):
        for z in range(tensor_count):
            source = (2 * (z // 2) + d % 2) ^ turn
            routes.append((d * tensor_count + z, (d - d % 2 + z % 2) * tensor_count + source))
    return routes


def after(value, *others):
    return lax.optimization_barrier((value, others))[0]


def unpack_kernel(p0, p1, p2, p3, up_ref, down_ref):
    total = p0[...].astype(f32) + p1[...].astype(f32) + p2[...].astype(f32) + p3[...].astype(f32)
    up_ref[...] = total[0]
    down_ref[...] = total[1].T


def unpack_pair(*pairs):
    _, rows, width = pairs[0].shape
    return pl.pallas_call(
        unpack_kernel,
        out_shape=(struct((rows, width), f32), struct((width, rows), f32)),
        compiler_params=params(16),
        name="unpack_pair",
    )(*pairs)


def per_device(
    block_in, norm1_gain, norm1_bias, w_query, w_key, w_value, w_out, norm2_gain, norm2_bias,
    w_up, up_bias, w_down, down_bias, segments, rand_blocks, glob_blocks, cotangent,
):
    dp_count, tensor_count = lax.axis_size("dp"), lax.axis_size("tensor")
    d, z = lax.axis_index("dp").astype(jnp.int32), lax.axis_index("tensor").astype(jnp.int32)
    core = d % 2
    where = jnp.stack([core, d, z])
    batches, local, width = block_in.shape
    share = local // 2
    blocks = segments.shape[1] // BLOCK
    pairs = dp_count // 2

    def move(value, to):
        routes = [
            (a * tensor_count + b, to(a, b)[0] * tensor_count + to(a, b)[1] % tensor_count)
            for a in range(dp_count)
            for b in range(tensor_count)
        ]
        return lax.ppermute(value, BOTH, routes)

    def other_core(value):
        return move(value, lambda a, b: (a ^ 1, b))

    def along(value, step):
        return move(value, lambda a, b: (a, b + step + tensor_count))

    def across(value, r):
        return move(value, lambda a, b: (a ^ (2 * r), b))

    def exchange(value):
        return lax.all_to_all(value, "tensor", split_axis=0, concat_axis=0, tiled=True)

    def half_of(value, which):
        value = value.reshape(batches, 2, share, width)
        return lax.dynamic_index_in_dim(value, which, 1, keepdims=False)

    def both_halves(keep, come):
        both = jnp.where(core == 0, jnp.stack([keep, come], 1), jnp.stack([come, keep], 1))
        return both.reshape(2 * batches * share, width)

    def give(value):
        return exchange(value).reshape(2 * batches, share, width)

    rand_size = rand_blocks.shape[2] * blocks * RAND
    chunk = norm1_gain.shape[0]
    small = jnp.concatenate(
        [norm1_gain, norm1_bias, norm2_gain, norm2_bias, down_bias, up_bias[0],
         rand_blocks.reshape(-1).astype(bf16), glob_blocks.reshape(-1).astype(bf16)]
    )
    devices = dp_count * tensor_count
    small = jnp.broadcast_to(small[None], (devices, small.shape[0]))
    shard = jnp.concatenate([w_query, w_key, w_value, w_out.T], axis=1)
    attn_slots = [along(shard, -k) for k in range(1, tensor_count)]
    their_segments = other_core(segments)
    x_come, cot_come = other_core(half_of(block_in, 1 - core)), other_core(half_of(cotangent, 1 - core))
    x_half = both_halves(half_of(block_in, core), x_come)
    small, x_half = lax.optimization_barrier((small, x_half))
    small = lax.all_to_all(small, BOTH, split_axis=0, concat_axis=0, tiled=True)
    attn_slots, small = lax.optimization_barrier((attn_slots, small))
    attn_slots = jnp.stack([shard, *attn_slots])
    x = exchange(x_half)
    small = small.reshape(dp_count, tensor_count, -1)
    vectors = small[..., : 6 * chunk].reshape(dp_count, tensor_count, 6, chunk).astype(f32)
    up_shift = vectors[:, :, 5].transpose(1, 0, 2).reshape(tensor_count, 1, -1)
    places = jnp.arange(dp_count, dtype=jnp.int32)
    order = chunk_at(d, places, dp_count)
    vecs = jnp.take(vectors[:, 0, :5], order, axis=0).transpose(1, 0, 2).reshape(5, width)
    vecs = jnp.concatenate([vecs, jnp.zeros((3, width), f32)])
    ints = lax.dynamic_index_in_dim(small, d - core + z % 2, 0, keepdims=False)[:, 6 * chunk :]
    ints = ints.astype(jnp.int32)
    rand_heads = ints[:, : batches * rand_size].reshape(tensor_count, batches, -1)
    rand_heads = lax.dynamic_index_in_dim(rand_heads, z // 2, 1, keepdims=False)
    rand_heads = lax.dynamic_slice_in_dim(jnp.roll(rand_heads, -z, axis=0), 2 * core, 2, 0)
    rand_heads = rand_heads.reshape(2 * rand_blocks.shape[2], blocks, RAND)
    glob_row = lax.dynamic_index_in_dim(
        ints[0, batches * rand_size :].reshape(batches, -1), z // 2, 0, keepdims=False
    )
    segment_row = lax.dynamic_index_in_dim(
        jnp.where(z % 2 == core, segments, their_segments), z // 2, 0, keepdims=False
    )
    segment_lanes = jnp.broadcast_to(segment_row[:, None], (segment_row.shape[0], 128))
    per_piece = share // BLOCK
    half = tensor_count * share

    def row_of(block):
        source, place = block // (2 * per_piece), block % (2 * per_piece)
        side = place // per_piece
        return jnp.where(side == core, 0, half) + source * share + (place % per_piece) * BLOCK

    table = attention_table(rand_heads, glob_row, row_of, 2 * half)

    attn_own = [attn_slots] + [across(attn_slots, r) for r in range(1, pairs)]
    pair_shard = after(jnp.stack([w_up, w_down.T]), attn_slots)
    pair_weights = lax.all_gather(pair_shard, BOTH, axis=0, tiled=False)
    pair_weights = pair_weights.reshape(dp_count, tensor_count, 2, *w_up.shape)
    cot_half = both_halves(half_of(cotangent, core), cot_come)
    x, attn_own, table, segment_lanes, vecs, up_shift, cot_half = lax.optimization_barrier(
        (x, attn_own, table, segment_lanes, vecs, up_shift, cot_half)
    )
    attn_own = jnp.concatenate(attn_own, axis=-2)
    attn_weights = (attn_own, other_core(attn_own))
    aligned = chunk % 128 == 0
    own_features = chunk_matrix(d, width, dp_count)
    if not aligned:
        x = jnp.dot(x, own_features, preferred_element_type=f32).astype(bf16)

    send, x, normed = project(where, x, vecs, attn_weights, True, dp_count)
    oth = other_core(send)
    own = project(where, normed, vecs, attn_weights, False, dp_count)
    ctx_own0, ctx_send0, lse0 = attn_fwd(table, own, oth, segment_lanes, blocks, 0)
    ctx_oth0 = other_core(ctx_send0)
    ctx_own1, ctx_send1, lse1 = attn_fwd(table, own, oth, segment_lanes, blocks, 1)
    ctx_oth1 = other_core(ctx_send1)
    cot = exchange(after(cot_half, own))
    resid, normed_two = out_project(
        where, x, (ctx_own0, ctx_own1, ctx_oth0, ctx_oth1), attn_weights, vecs, dp_count
    )
    if not aligned:
        normed_two = jnp.dot(normed_two, own_features.T, preferred_element_type=f32).astype(bf16)
    ffn0, gn0, pair0, bias0, *turned = feed_forward(
        where, normed_two, cot, pair_weights, up_shift, 2
    )

    def reduce_rows(total):
        flat = total.reshape(-1, total.shape[-1])
        result = lax.psum_scatter(flat, "dp", scatter_dimension=0, tiled=True)
        return result.reshape(total.shape[1:])

    ffn1, gn1, pair1, bias1 = feed_forward(
        where, normed_two, cot, pair_weights, up_shift, 0, turned
    )
    pair_total0 = reduce_rows(pair0)
    pair_total1 = reduce_rows(pair1)
    grad_bias = jnp.concatenate([bias1, bias0])
    ffn, grad_two = (ffn0, ffn1), (gn0, gn1)
    if not aligned:
        reorder = lambda v: jnp.dot(v, own_features, preferred_element_type=f32).astype(bf16)
        ffn, grad_two, cot = map(reorder, ffn), map(reorder, grad_two), reorder(cot)

    def reduce_core(own_half, other_half):
        theirs = other_core(other_half)
        size = own_half.shape[-2] // pairs
        return [
            (
                own_half[..., r * size : (r + 1) * size, :].astype(f32)
                + theirs[..., r * size : (r + 1) * size, :].astype(f32)
            ).astype(own_half.dtype)
            for r in range(pairs)
        ]

    def add_parts(first, others):
        total = first.astype(f32)
        for part in others:
            total = total + part.astype(f32)
        return total.astype(first.dtype)

    def reduce_across(parts):
        return add_parts(parts[0], [across(parts[r], r) for r in range(1, pairs)])

    piece = width // devices

    def exchange_sums(sums_one, sums_two, grad_bias):
        five = jnp.concatenate([sums_one[:2], sums_two[:3]]).reshape(5, dp_count, chunk)
        relative = places ^ d
        back = (relative % 2) * pairs + relative // 2
        five = jnp.take(five, back, axis=1).reshape(5, devices, piece).transpose(1, 0, 2)
        shift = jnp.roll(grad_bias, z, axis=0)
        shift = shift.reshape(tensor_count, dp_count, -1).transpose(1, 0, 2)
        sums = jnp.concatenate([five.reshape(devices, -1), shift.reshape(devices, -1)], axis=1)
        return lax.all_to_all(sums, BOTH, split_axis=0, concat_axis=0, tiled=True)

    def reduce_along(total, slots):
        return sum(
            (along(total[i], k) if k else total[i]).astype(f32) for i, k in enumerate(slots)
        )

    out, grad_resid, low, gctx_own, gctx_send, sums_two = middle(
        where, resid, tuple(ffn), tuple(grad_two), cot, attn_weights, vecs, dp_count
    )
    gctx_oth = other_core(gctx_send)
    out_back = give(out)
    d_own0, d_send0 = attn_bwd(
        table, own, oth, gctx_own, gctx_oth, segment_lanes, lse0, blocks, 0
    )
    d_send0, out_back = lax.optimization_barrier((d_send0, out_back))
    d_oth0 = other_core(d_send0)
    total_one, ga0, gb0, *turned = back_early(
        where, normed, low, (d_own0, d_oth0), (ctx_own0, ctx_oth0), attn_weights, 0
    )
    attn_parts0 = reduce_core(ga0, gb0)
    out_other = other_core(half_of(out_back, 1 - core))
    lse1, attn_parts0, out_other = lax.optimization_barrier((lse1, attn_parts0, out_other))
    d_own1, d_send1 = attn_bwd(
        table, own, oth, gctx_own, gctx_oth, segment_lanes, lse1, blocks, 1
    )
    attn_total0 = reduce_across(attn_parts0)
    pair_next = [along(pair_total0[0], 2), along(pair_total0[1], 3)]
    d_send1, attn_total0, pair_next = lax.optimization_barrier((d_send1, attn_total0, pair_next))
    d_oth1 = other_core(d_send1)
    ga1, gb1 = back_weights(where, (d_own1, d_oth1), (ctx_own1, ctx_oth1), turned)
    total_one, ga1, gb1 = lax.optimization_barrier((total_one, ga1, gb1))
    grad_in, sums_one = back_tokens(
        where, (d_own1, d_oth1), attn_weights, 1, total_one, x, grad_resid, vecs
    )
    grad_back = [
        lax.ppermute(
            grad_in[turn * share : (turn + 1) * share], BOTH,
            token_routes(dp_count, tensor_count, turn),
        )
        for turn in range(tensor_count)
    ]
    attn_parts1 = reduce_core(ga1, gb1)
    pair_next.append(along(pair_total1[1], 1))
    sums_one, attn_parts1 = lax.optimization_barrier((sums_one, attn_parts1))
    sums = exchange_sums(sums_one, sums_two, grad_bias)
    attn_come1 = [across(attn_parts1[r], r) for r in range(1, pairs)]
    sums, attn_come1 = lax.optimization_barrier((sums, attn_come1))
    attn_total1 = add_parts(attn_parts1[0], attn_come1)
    block_out = restore(where, out_back, out_other, dp_count, bf16).reshape(batches, local, width)
    g_attn = reduce_along(attn_total0, (0, 2)) + reduce_along(attn_total1, (1, 3))
    g_up, g_down = unpack_pair(pair_total1[0], *pair_next)
    grad_in = restore_direct(where, grad_back, dp_count, f32).reshape(batches, local, width)

    sums = jnp.sum(sums, axis=0)
    vector_grads = [sums[i * piece : (i + 1) * piece] for i in range(5)]
    quarter = width // 4
    return (
        block_out, grad_in, vector_grads[0], vector_grads[1],
        g_attn[:, :quarter], g_attn[:, quarter : 2 * quarter], g_attn[:, 2 * quarter : 3 * quarter],
        g_attn[:, 3 * quarter :].T, vector_grads[2], vector_grads[3],
        g_up, sums[5 * piece :][None], g_down, vector_grads[4],
    )


def solution(mesh):
    rows, both = P(None, BOTH, None), P(BOTH)
    dp, split, turned = P("dp"), P("dp", "tensor"), P("tensor", "dp")
    return jax.shard_map(
        per_device,
        mesh=mesh,
        in_specs=(
            rows, dp, dp, split, split, split, turned, dp, dp, split, turned, turned, dp,
            P(None, "dp"), P(None, "dp", "tensor", None, None), P(None, "dp", None), rows,
        ),
        out_specs=(
            rows, rows, both, both, split, split, split, turned, both, both, split, turned, turned,
            both,
        ),
        check_vma=False,
    )
```

```python
import functools
import jax
import jax.numpy as jnp
from jax import lax
from jax.sharding import PartitionSpec as P
from jax.experimental import pallas as pl
from jax.experimental.pallas import tpu as pltpu

HD = 64
BLOCK = 64
COMMON = 5
RAND = 3
BIG = 1e30
bf16 = jnp.bfloat16
f32 = jnp.float32


def cost(micros):
    return pl.CostEstimate(flops=int(micros * 10**9), bytes_accessed=1000, transcendentals=0)


def dot_nt(left, right):
    return lax.dot_general(left, right, (((1,), (1,)), ((), ())), preferred_element_type=f32)


def dot_tn(left, right):
    return lax.dot_general(left, right, (((0,), (0,)), ((), ())), preferred_element_type=f32)


def dot_nn(left, right):
    return lax.dot_general(left, right, (((1,), (0,)), ((), ())), preferred_element_type=f32)


def low_half(shape):
    return lax.broadcasted_iota(jnp.int32, shape, 1) % 128 < HD


def slot_offsets(tab, layout, pair, block):
    common_at, rand_at, blocks, heads = layout
    shared = [
        pl.multiple_of(tab[common_at + block * COMMON + slot], BLOCK) for slot in range(COMMON)
    ]
    first = rand_at + (2 * pair * blocks + block) * RAND
    second = first + blocks * RAND
    drawn = [
        (pl.multiple_of(tab[first + slot], BLOCK), pl.multiple_of(tab[second + slot], BLOCK))
        for slot in range(RAND)
    ]
    return shared, drawn


def gather_rows(ref, shared, drawn, width):
    keep = low_half((BLOCK, width))
    parts = [ref[pl.ds(start, BLOCK), :width] for start in shared]
    for left, right in drawn:
        parts.append(
            jnp.where(keep, ref[pl.ds(left, BLOCK), :width], ref[pl.ds(right, BLOCK), :width])
        )
    return jnp.concatenate(parts, axis=0)


def block_diag(rows):
    keep = low_half(rows.shape)
    zero = jnp.zeros_like(rows)
    return jnp.concatenate([jnp.where(keep, rows, zero), jnp.where(keep, zero, rows)], axis=0)


def fold_heads(rows):
    keep = low_half((BLOCK, 128))
    return jnp.where(keep, rows[:BLOCK], rows[BLOCK:])


def query_rows(qbuf, kaug, start):
    scaled = qbuf[pl.ds(start, BLOCK), :]
    hot = kaug[pl.ds(start, BLOCK), 128:]
    penalty = (hot - jnp.ones_like(hot)) * jnp.asarray(BIG, bf16)
    return block_diag(jnp.concatenate([scaled, penalty], axis=1))


def fill_keys(tab, layout, seg_ref, kaug, half, k_own, k_oth):
    blocks = layout[2]

    @pl.when(pl.program_id(0) == 0)
    def _():
        lane = lax.broadcasted_iota(jnp.int32, (BLOCK, 128), 1) % HD

        def one(block, carry):
            row = pl.multiple_of(tab[block], BLOCK)
            seg = seg_ref[pl.ds(pl.multiple_of(block * BLOCK, BLOCK), BLOCK), :]
            kaug[pl.ds(row, BLOCK), 128:] = jnp.where(seg == lane, 1.0, 0.0).astype(bf16)
            return carry

        lax.fori_loop(0, blocks, one, 0)
        kaug[2 * half :, :128] = jnp.zeros((BLOCK, 128), bf16)
        kaug[2 * half :, 128:] = jnp.where(lane == HD - 1, 1.0, 0.0).astype(bf16)

    kaug[:half, :128] = k_own[0]
    kaug[half : 2 * half, :128] = k_oth[0]


def attn_fwd_kernel(
    layout, first_pair, unroll, tab, q_own, q_oth, k_own, k_oth, v_own, v_oth, seg_ref,
    out_own, out_oth, lse_ref, kaug, vbuf, qbuf, obuf, sbuf,
):
    pair = first_pair + pl.program_id(0)
    half = q_own.shape[1]
    blocks = layout[2]
    fill_keys(tab, layout, seg_ref, kaug, half, k_own, k_oth)
    vbuf[:half, :] = v_own[0]
    vbuf[half : 2 * half, :] = v_oth[0]
    vbuf[2 * half :, :] = jnp.zeros((BLOCK, 128), bf16)
    scale = jnp.asarray(0.125, bf16)
    qbuf[:half, :] = q_own[0] * scale
    qbuf[half:, :] = q_oth[0] * scale

    def step(index, carry):
        group = [index * unroll + part for part in range(unroll)]
        rows = [pl.multiple_of(tab[block], BLOCK) for block in group]
        slots = [slot_offsets(tab, layout, pair, block) for block in group]
        scores = [
            dot_nt(gather_rows(kaug, *slot, 256), query_rows(qbuf, kaug, row))
            for slot, row in zip(slots, rows)
        ]
        top = [jnp.max(score, axis=0, keepdims=True) for score in scores]
        weight = [jnp.exp(score - most) for score, most in zip(scores, top)]
        total = [jnp.sum(part, axis=0, keepdims=True) for part in weight]
        probs = [(part * (1.0 / whole)).astype(bf16) for part, whole in zip(weight, total)]
        context = [
            dot_tn(prob, gather_rows(vbuf, *slot, 128)) for prob, slot in zip(probs, slots)
        ]
        for block, row, part, most, whole in zip(group, rows, context, top, total):
            obuf[pl.ds(row, BLOCK), :] = fold_heads(part).astype(bf16)
            lse_ref[0, pl.ds(block, 1), :] = most + jnp.log(whole)
        return carry

    lax.fori_loop(0, blocks // unroll, step, 0)

    first, second = tab[blocks], tab[blocks + 1]
    rows = [pl.multiple_of(tab[block], BLOCK) for block in (first, second)]
    query = jnp.concatenate([query_rows(qbuf, kaug, row) for row in rows], axis=0)
    chunk = 512
    pieces = [slice(at, at + chunk) for at in range(0, 2 * half, chunk)]
    top = jnp.full((1, 256), -3e38, f32)
    for here in pieces:
        scores = dot_nt(kaug[here, :], query)
        sbuf[here, :] = scores
        top = jnp.maximum(top, jnp.max(scores, axis=0, keepdims=True))
    total = jnp.zeros((1, 256), f32)
    for here in pieces:
        weight = jnp.exp(sbuf[here, :] - top)
        sbuf[here, :] = weight
        total = total + jnp.sum(weight, axis=0, keepdims=True)
    inverse = 1.0 / total
    context = jnp.zeros((256, 128), f32)
    for here in pieces:
        context = context + dot_tn((sbuf[here, :] * inverse).astype(bf16), vbuf[here, :])
    lse = top + jnp.log(total)
    for index, (block, row) in enumerate(zip((first, second), rows)):
        lanes = slice(index * 128, (index + 1) * 128)
        obuf[pl.ds(row, BLOCK), :] = fold_heads(context[lanes]).astype(bf16)
        lse_ref[0, pl.ds(block, 1), :] = lse[:, lanes]
    out_own[0] = obuf[:half, :]
    out_oth[0] = obuf[half:, :]


def attn_bwd_kernel(
    layout, first_pair, unroll, tab, q_own, q_oth, k_own, k_oth, v_own, v_oth, g_own, g_oth, seg_ref, lse_ref,
    own_ref, oth_ref,
    kaug, vbuf, qbuf, gbuf, dqbuf, dkbuf, dvbuf, sbuf, tbuf,
):
    pair = first_pair + pl.program_id(0)
    half = q_own.shape[1]
    blocks = layout[2]
    fill_keys(tab, layout, seg_ref, kaug, half, k_own, k_oth)
    vbuf[:half, :] = v_own[0]
    vbuf[half : 2 * half, :] = v_oth[0]
    vbuf[2 * half :, :] = jnp.zeros((BLOCK, 128), bf16)
    scale = jnp.asarray(0.125, bf16)
    qbuf[:half, :] = q_own[0] * scale
    qbuf[half:, :] = q_oth[0] * scale
    gbuf[:half, :] = g_own[0]
    gbuf[half:, :] = g_oth[0]
    dkbuf[...] = jnp.zeros_like(dkbuf)
    dvbuf[...] = jnp.zeros_like(dvbuf)
    keep = low_half((BLOCK, 128))

    dummy = 2 * half
    ends = [pl.multiple_of(tab[tab_block], BLOCK) for tab_block in (tab[blocks], tab[blocks + 1])]

    def scatter(ref, updates, slots, base):
        piece = lambda part, slot: updates[part][slot * BLOCK : (slot + 1) * BLOCK]
        for shift in range(-1, unroll + 1):
            block = base + shift
            inside = (block >= 0) & (block < blocks)
            row = jnp.where(inside, tab[jnp.clip(block, 0, blocks - 1)], dummy)
            near = [piece(p, shift - p + 1) for p in range(unroll) if 0 <= shift - p + 1 <= 2]
            ref[pl.ds(pl.multiple_of(row, BLOCK), BLOCK), :] += functools.reduce(jnp.add, near)
        for slot, row in zip((3, 4), ends):
            every = [piece(p, slot) for p in range(unroll)]
            ref[pl.ds(row, BLOCK), :] += functools.reduce(jnp.add, every)
        for part, (_, drawn) in enumerate(slots):
            for slot, (left, right) in enumerate(drawn):
                one = piece(part, COMMON + slot)
                ref[pl.ds(left, BLOCK), :] += jnp.where(keep, one, 0.0)
                ref[pl.ds(right, BLOCK), :] += jnp.where(keep, 0.0, one)

    def step(index, carry):
        group = [index * unroll + part for part in range(unroll)]
        rows = [pl.multiple_of(tab[block], BLOCK) for block in group]
        slots = [slot_offsets(tab, layout, pair, block) for block in group]
        query = [query_rows(qbuf, kaug, row) for row in rows]
        grad = [block_diag(gbuf[pl.ds(row, BLOCK), :]) for row in rows]
        keys = [gather_rows(kaug, *slot, 256) for slot in slots]
        scores = [dot_nt(key, one) for key, one in zip(keys, query)]
        grad_probs = [
            dot_nt(gather_rows(vbuf, *slot, 128), one) for slot, one in zip(slots, grad)
        ]
        probs = [
            jnp.exp(score - lse_ref[0, pl.ds(block, 1), :]) for score, block in zip(scores, group)
        ]
        delta = [jnp.sum(p * g, axis=0, keepdims=True) for p, g in zip(probs, grad_probs)]
        grad_scores = [
            (p * (g - one)).astype(bf16) for p, g, one in zip(probs, grad_probs, delta)
        ]
        grad_query = [dot_tn(one, key[:, :128]) for one, key in zip(grad_scores, keys)]
        grad_key = [dot_nn(one, q[:, :128]) for one, q in zip(grad_scores, query)]
        grad_value = [dot_nn(p.astype(bf16), g) for p, g in zip(probs, grad)]
        for row, one in zip(rows, grad_query):
            dqbuf[pl.ds(row, BLOCK), :] = (fold_heads(one) * 0.125).astype(bf16)
        scatter(dkbuf, grad_key, slots, index * unroll)
        scatter(dvbuf, grad_value, slots, index * unroll)
        return carry

    lax.fori_loop(0, blocks // unroll, step, 0)

    first, second = tab[blocks], tab[blocks + 1]
    rows = [pl.multiple_of(tab[block], BLOCK) for block in (first, second)]
    query = jnp.concatenate([query_rows(qbuf, kaug, row) for row in rows], axis=0)
    grads = [block_diag(gbuf[pl.ds(row, BLOCK), :]) for row in rows]
    grads[1] = jnp.where(first == second, jnp.zeros_like(grads[1]), grads[1])
    grad = jnp.concatenate(grads, axis=0)
    lse = jnp.concatenate([lse_ref[0, pl.ds(block, 1), :] for block in (first, second)], axis=1)
    chunk = 512
    pieces = [slice(at, at + chunk) for at in range(0, 2 * half, chunk)]
    delta = jnp.zeros((1, 256), f32)
    for here in pieces:
        probs = jnp.exp(dot_nt(kaug[here, :], query) - lse)
        grad_probs = dot_nt(vbuf[here, :], grad)
        delta = delta + jnp.sum(probs * grad_probs, axis=0, keepdims=True)
        sbuf[here, :] = probs
        tbuf[here, :] = grad_probs
    grad_query = jnp.zeros((256, 128), f32)
    for here in pieces:
        probs = sbuf[here, :]
        grad_scores = (probs * (tbuf[here, :] - delta)).astype(bf16)
        grad_query = grad_query + dot_tn(grad_scores, kaug[here, :128])
        dkbuf[here, :] += dot_nn(grad_scores, query[:, :128])
        dvbuf[here, :] += dot_nn(probs.astype(bf16), grad)
    for index in (1, 0):
        part = fold_heads(grad_query[index * 128 : (index + 1) * 128]) * 0.125
        dqbuf[pl.ds(rows[index], BLOCK), :] = part.astype(bf16)
    for part, buffer in enumerate((dqbuf, dkbuf, dvbuf)):
        lanes = pl.ds(pl.multiple_of((2 * part + pl.program_id(0)) * 128, 128), 128)
        own_ref[0, :, lanes] = buffer[:half, :].astype(bf16)
        oth_ref[0, :, lanes] = buffer[half : 2 * half, :].astype(bf16)


def table_layout(blocks, heads):
    common_at = blocks + 2
    rand_at = common_at + blocks * COMMON
    return (common_at, rand_at, blocks, heads)


def attention_table(rand_heads, glob_row, row_of, dummy_row):
    heads, blocks, _ = rand_heads.shape
    index = jnp.arange(blocks, dtype=jnp.int32)
    g0, g1 = glob_row[0], glob_row[1]
    dense = (index == g0) | (index == g1)
    near0, near1 = jnp.abs(index - g0) <= 1, jnp.abs(index - g1) <= 1
    full = jnp.broadcast_to
    shared = jnp.stack([index - 1, index, index + 1, full(g0, (blocks,)), full(g1, (blocks,))], axis=1)
    valid = jnp.stack(
        [index > 0, index >= 0, index < blocks - 1, ~near0, ~near1 & (g1 != g0)], axis=1
    ) & ~dense[:, None]
    shared = jnp.where(valid, row_of(jnp.clip(shared, 0, blocks - 1)), dummy_row)
    far = jnp.abs(rand_heads - index[None, :, None]) > 1
    far = far & (rand_heads != g0) & (rand_heads != g1) & ~dense[None, :, None]
    r0, r1, r2 = rand_heads[..., 0], rand_heads[..., 1], rand_heads[..., 2]
    fresh = jnp.stack([r0 == r0, r1 != r0, (r2 != r0) & (r2 != r1)], axis=-1)
    drawn = jnp.where(far & fresh, row_of(rand_heads), dummy_row)
    return jnp.concatenate(
        [row_of(index), glob_row, shared.reshape(-1), drawn.reshape(-1)]
    ).astype(jnp.int32)


def lane_spec(half, slot, column):
    return pl.BlockSpec((1, half, 128), lambda p, tab: (slot, 0, column * 2 + p))


def attn_fwd(tab, qkv_own, qkv_oth, seg_abs, blocks, slot, unroll=8):
    half = qkv_own.shape[1]
    layout = table_layout(blocks, 4 * qkv_own.shape[0])
    rows = 2 * half + BLOCK
    shape = jax.ShapeDtypeStruct((1, half, 256), bf16)
    result = pl.BlockSpec((1, half, 128), lambda p, tab: (0, 0, p))
    return pl.pallas_call(
        functools.partial(attn_fwd_kernel, layout, 2 * slot, unroll),
        out_shape=(shape, shape, jax.ShapeDtypeStruct((2, blocks, 128), f32)),
        grid_spec=pltpu.PrefetchScalarGridSpec(
            num_scalar_prefetch=1,
            grid=(2,),
            in_specs=[
                *[lane_spec(half, slot, column) for column in (0, 0, 1, 1, 2, 2)],
                pl.BlockSpec((2 * half, 128), lambda p, tab: (0, 0)),
            ],
            out_specs=(result, result, pl.BlockSpec((1, blocks, 128), lambda p, tab: (p, 0, 0))),
            scratch_shapes=[
                pltpu.VMEM((rows, 256), bf16), pltpu.VMEM((rows, 128), bf16),
                pltpu.VMEM((2 * half, 128), bf16), pltpu.VMEM((2 * half, 128), bf16),
                pltpu.VMEM((2 * half, 256), f32),
            ],
        ),
        compiler_params=pltpu.CompilerParams(vmem_limit_bytes=40 << 20),
        cost_estimate=cost(17),
        name="attn_fwd",
    )(tab, qkv_own, qkv_oth, qkv_own, qkv_oth, qkv_own, qkv_oth, seg_abs)


def attn_bwd(tab, qkv_own, qkv_oth, grad_own, grad_oth, seg_abs, lse, blocks, slot, unroll=8):
    half = qkv_own.shape[1]
    layout = table_layout(blocks, 4 * qkv_own.shape[0])
    rows = 2 * half + BLOCK
    shape = jax.ShapeDtypeStruct((1, half, 768), bf16)
    result = pl.BlockSpec((1, half, 768), lambda p, tab: (0, 0, 0))
    return pl.pallas_call(
        functools.partial(attn_bwd_kernel, layout, 2 * slot, unroll),
        out_shape=(shape, shape),
        grid_spec=pltpu.PrefetchScalarGridSpec(
            num_scalar_prefetch=1,
            grid=(2,),
            in_specs=[
                *[lane_spec(half, slot, column) for column in (0, 0, 1, 1, 2, 2, 0, 0)],
                pl.BlockSpec((2 * half, 128), lambda p, tab: (0, 0)),
                pl.BlockSpec((1, blocks, 128), lambda p, tab: (p, 0, 0)),
            ],
            out_specs=(result, result),
            scratch_shapes=[
                pltpu.VMEM((rows, 256), bf16), pltpu.VMEM((rows, 128), bf16),
                pltpu.VMEM((2 * half, 128), bf16), pltpu.VMEM((2 * half, 128), bf16),
                pltpu.VMEM((2 * half, 128), bf16),
                pltpu.VMEM((rows, 128), f32), pltpu.VMEM((rows, 128), f32),
                pltpu.VMEM((2 * half, 256), f32), pltpu.VMEM((2 * half, 256), f32),
            ],
        ),
        compiler_params=pltpu.CompilerParams(vmem_limit_bytes=48 << 20),
        cost_estimate=cost(29),
        name="attn_bwd",
    )(tab, qkv_own, qkv_oth, qkv_own, qkv_oth, qkv_own, qkv_oth, grad_own, grad_oth, seg_abs, lse)


EPS = 1e-05
BOTH = ("dp", "tensor")
ROWS = 256
WIDE = 512


def gelu_pair(u):
    c = 0.7978845608028654
    square = u * u
    bend = jnp.tanh(u * (c + (c * 0.044715) * square))
    half = 0.5 * (1.0 + bend)
    slope = half + (0.5 * u) * (1.0 - bend * bend) * (c + (3.0 * c * 0.044715) * square)
    return u * half, slope


def normalise(rows):
    center = rows - jnp.mean(rows, axis=-1, keepdims=True)
    inverse = lax.rsqrt(jnp.mean(center * center, axis=-1, keepdims=True) + EPS)
    return center * inverse, inverse


def norm_back(grad, unit, inverse, gain):
    scaled = grad * gain
    mean = jnp.mean(scaled, axis=-1, keepdims=True)
    along = jnp.mean(scaled * unit, axis=-1, keepdims=True)
    return inverse * (scaled - mean - unit * along)


def params(mib):
    return pltpu.CompilerParams(vmem_limit_bytes=mib << 20)


def prefetch(grid, in_specs, out_specs, scratch=()):
    return pltpu.PrefetchScalarGridSpec(
        num_scalar_prefetch=1, grid=grid, in_specs=in_specs, out_specs=out_specs,
        scratch_shapes=list(scratch),
    )


def struct(shape, dtype):
    return jax.ShapeDtypeStruct(shape, dtype)


def nn_halves(rows, low_ref, high_ref):
    split = rows.shape[1] // 2
    return dot_nn(rows[:, :split], low_ref) + dot_nn(rows[:, split:], high_ref)


def nt_halves(rows, low_ref, high_ref):
    return jnp.concatenate([dot_nt(rows, low_ref), dot_nt(rows, high_ref)], axis=1)


def chunk_at(d, place, count):
    return d ^ (2 * (place % (count // 2)) + place // (count // 2))


def restore_kernel(count, where, own_ref, oth_ref, out_ref):
    batches, rows, width = oth_ref.shape
    chunk = width // count
    core, d = where[0], where[1]
    for batch in range(batches):
        for place in range(count):
            lanes = slice(place * chunk, (place + 1) * chunk)
            here = pl.ds(pl.multiple_of(chunk_at(d, place, count) * chunk, chunk), chunk)
            out_ref[batch, core, :, here] = own_ref[2 * batch + core, :, lanes].astype(out_ref.dtype)
            there = pl.ds(pl.multiple_of(chunk_at(d ^ 1, place, count) * chunk, chunk), chunk)
            out_ref[batch, 1 - core, :, there] = oth_ref[batch, :, lanes].astype(out_ref.dtype)


def restore_direct_kernel(count, where, p0, p1, p2, p3, out_ref):
    width = p0.shape[1]
    chunk = width // count
    core, d, z = where[0], where[1], where[2]
    for turn, piece in enumerate((p0, p1, p2, p3)):
        index = z ^ turn
        sender = d - core + index % 2
        for place in range(count):
            target = pl.ds(pl.multiple_of(chunk_at(sender, place, count) * chunk, chunk), chunk)
            out_ref[index, :, target] = piece[:, place * chunk : (place + 1) * chunk].astype(
                out_ref.dtype
            )


def chunk_matrix(d, width, count):
    chunk = width // count
    index = jnp.arange(width, dtype=jnp.int32)
    source = chunk_at(d, index // chunk, count) * chunk + index % chunk
    return (index[:, None] == source[None, :]).astype(bf16)


def restore(where, own, oth, count, dtype):
    batches, rows, width = oth.shape
    core, d = where[0], where[1]
    if (width // count) % 128:
        mine = lax.dynamic_index_in_dim(own.reshape(batches, 2, rows, width), core, 1, False)
        pair = []
        for piece, owner in ((mine, d), (oth, d ^ 1)):
            matrix = chunk_matrix(owner, width, count).T
            pair.append(jnp.dot(piece, matrix, preferred_element_type=f32).astype(dtype))
        return jnp.where(core == 0, jnp.stack(pair, axis=1), jnp.stack(pair[::-1], axis=1))
    whole = lambda shape: pl.BlockSpec(shape, lambda i, w: (0,) * len(shape))
    shape = (batches, 2, rows, width)
    return pl.pallas_call(
        functools.partial(restore_kernel, count),
        out_shape=struct(shape, dtype),
        grid_spec=prefetch((1,), [whole(own.shape), whole(oth.shape)], whole(shape)),
        compiler_params=params(24),
        cost_estimate=cost(3),
        name="restore",
    )(where, own, oth)


def scatter_chunks(where, ref, rows, count):
    chunk = rows.shape[1] // count
    if chunk % 128:
        ref[...] = rows
        return
    for place in range(count):
        target = pl.ds(pl.multiple_of(chunk_at(where[1], place, count) * chunk, chunk), chunk)
        ref[:, target] = rows[:, place * chunk : (place + 1) * chunk]


def gather_chunks(where, ref, count):
    chunk = ref.shape[1] // count
    if chunk % 128:
        return ref[...]
    return jnp.concatenate(
        [
            ref[:, pl.ds(pl.multiple_of(chunk_at(where[1], place, count) * chunk, chunk), chunk)]
            for place in range(count)
        ],
        axis=1,
    )


def project_kernel(count, where, x_ref, vec_ref, wa_ref, wb_ref, out_ref, rel_ref, n_ref, nbuf):
    slot, tile = pl.program_id(0), pl.program_id(1)
    here = pl.ds(pl.multiple_of(tile * WIDE, WIDE), WIDE)

    @pl.when(slot == 0)
    def _():
        rows = gather_chunks(where, x_ref, count)
        rel_ref[...] = rows
        unit, _ = normalise(rows.astype(f32))
        normed = (unit * vec_ref[0:1, :] + vec_ref[1:2, :]).astype(bf16)
        nbuf[here, :] = normed
        n_ref[...] = normed

    out_ref[0] = nn_halves(nbuf[here, :], wa_ref[0], wb_ref[0]).astype(bf16)


def project_more_kernel(where, n_ref, wa_ref, wb_ref, out_ref):
    out_ref[0] = nn_halves(n_ref[...], wa_ref[0], wb_ref[0]).astype(bf16)


def project(where, x, vecs, weights, first, count):
    rows, width = x.shape
    tiles = rows // WIDE
    out = width * 3 // 4
    half = width // 2
    weight = pl.BlockSpec(
        (1, half, out), lambda s, i, w: (2 * (1 - w[0] if first else w[0]) + s, 0, 0)
    )
    outs = pl.BlockSpec((1, WIDE, out), lambda s, i, w: (s, i, 0))
    once = pl.BlockSpec((WIDE, width), lambda s, i, w: (jnp.where(s == 0, i, tiles - 1), 0))
    shape = struct((2, rows, out), bf16)
    if first:
        return pl.pallas_call(
            functools.partial(project_kernel, count),
            out_shape=(shape, struct((rows, width), bf16), struct((rows, width), bf16)),
            grid_spec=prefetch(
                (2, tiles),
                [once, pl.BlockSpec(vecs.shape, lambda s, i, w: (0, 0)), weight, weight],
                (outs, once, once),
                [pltpu.VMEM((rows, width), bf16)],
            ),
            compiler_params=params(32),
            cost_estimate=cost(9),
            name="project",
        )(where, x, vecs, *weights)
    return pl.pallas_call(
        project_more_kernel,
        out_shape=shape,
        grid_spec=prefetch(
            (2, tiles),
            [pl.BlockSpec((WIDE, width), lambda s, i, w: (i, 0)), weight, weight],
            outs,
        ),
        compiler_params=params(32),
        cost_estimate=cost(8),
        name="project_more",
    )(where, x, *weights)


def out_kernel(count, where, x_ref, c0, c1, c2, c3, a0, a1, a2, a3, b0, b1, b2, b3, vec_ref,
               resid_ref, n_ref):
    total = x_ref[...].astype(f32)
    for part, low, high in ((c0, a0, b0), (c1, a1, b1), (c2, a2, b2), (c3, a3, b3)):
        total = total + nt_halves(part[0], low[0], high[0])
    resid_ref[...] = total
    unit, _ = normalise(total)
    scatter_chunks(where, n_ref, (unit * vec_ref[2:3, :] + vec_ref[3:4, :]).astype(bf16), count)


def out_weight_specs(width):
    return [
        pl.BlockSpec((1, width // 2, width // 4), lambda i, w, s=s: ((2 * w[0] + s) % 4, 0, 3))
        for s in range(4)
    ]


def out_project(where, x, contexts, weights, vecs, count):
    rows, width = x.shape
    tile = pl.BlockSpec((ROWS, width), lambda i, w: (i, 0))
    part = pl.BlockSpec((1, ROWS, width // 4), lambda i, w: (0, i, 0))
    return pl.pallas_call(
        functools.partial(out_kernel, count),
        out_shape=(struct((rows, width), f32), struct((rows, width), bf16)),
        grid_spec=prefetch(
            (rows // ROWS,),
            [tile, *[part] * 4, *out_weight_specs(width) * 2,
             pl.BlockSpec(vecs.shape, lambda i, w: (0, 0))],
            (tile, tile),
        ),
        compiler_params=params(32),
        cost_estimate=cost(7),
        name="out_project",
    )(where, x, *contexts, *[weights[0]] * 4, *[weights[1]] * 4, vecs)


def ffn_kernel(where, n_ref, cot_ref, up_ref, down_ref, bias_ref,
               ffn_ref, gn_ref, grad_ref, gbias_ref, nt, ct, act, gup, total, back_total):
    step = pl.program_id(0)
    rows, width = n_ref.shape
    hidden = act.shape[1]
    up = up_ref[...].reshape(width, hidden)
    down = down_ref[...].reshape(width, hidden)

    @pl.when(step == 0)
    def _():
        turn_rows(n_ref, nt)
        turn_rows(cot_ref, ct)
        total[...] = jnp.zeros_like(total)
        back_total[...] = jnp.zeros_like(back_total)

    value = dot_nn(n_ref[...], up) + bias_ref[0]
    out, slope = gelu_pair(value)
    out = out.astype(bf16)
    act[...] = out
    back = (dot_nn(cot_ref[...], down) * slope).astype(bf16)
    gup[...] = back
    gbias_ref[0] = jnp.sum(back.astype(f32), axis=0, keepdims=True)
    total[...] += dot_nt(out, down)
    back_total[...] += dot_nt(back, up)
    shape = grad_ref.shape[0], grad_ref.shape[3], hidden
    grad_ref[:, 0, 0] = dot_nn(nt[...], gup[...]).astype(bf16).reshape(shape)
    grad_ref[:, 0, 1] = dot_nn(ct[...], act[...]).astype(bf16).reshape(shape)

    @pl.when(step == pl.num_programs(0) - 1)
    def _():
        ffn_ref[...] = total[...].astype(bf16)
        gn_ref[...] = back_total[...].astype(bf16)


def feed_forward(where, normed, cot, weights, bias, slots_at):
    rows, width = normed.shape
    count, slots, _, chunk, hidden = weights.shape
    whole = fixed_spec((rows, width))
    slot = lambda s, w: (w[2] + slots_at + s) % slots
    weight = lambda k: pl.BlockSpec(
        (count, 1, 1, chunk, hidden), lambda s, w: (0, slot(s, w), k, 0, 0)
    )
    total = pl.BlockSpec((rows, width), lambda s, w: (0, 0))
    return pl.pallas_call(
        ffn_kernel,
        out_shape=(
            struct((rows, width), bf16), struct((rows, width), bf16),
            struct((count, 2, 2, chunk, hidden), bf16), struct((2, 1, hidden), f32),
        ),
        grid_spec=prefetch(
            (2,),
            [whole, whole, weight(0), weight(1),
             pl.BlockSpec((1, 1, hidden), lambda s, w: (slot(s, w), 0, 0))],
            (
                total, total,
                pl.BlockSpec((count, 1, 2, chunk, hidden), lambda s, w: (0, s, 0, 0, 0)),
                pl.BlockSpec((1, 1, hidden), lambda s, w: (s, 0, 0)),
            ),
            [
                pltpu.VMEM((width, rows), bf16), pltpu.VMEM((width, rows), bf16),
                pltpu.VMEM((rows, hidden), bf16), pltpu.VMEM((rows, hidden), bf16),
                pltpu.VMEM((rows, width), f32), pltpu.VMEM((rows, width), f32),
            ],
        ),
        compiler_params=params(60),
        cost_estimate=cost(38),
        name="feed_forward",
    )(where, normed, cot, weights, weights, bias)


def mid_kernel(count, where, resid_ref, f0_ref, f1_ref, n0_ref, n1_ref, cot_ref, a0, a1, a2, a3, b0, b1, b2, b3, vec_ref,
               out_ref, gres_ref, low_ref, own_ref, send_ref, sums_ref):
    tile = pl.program_id(0)
    resid = resid_ref[...]
    cot = gather_chunks(where, cot_ref, count).astype(f32)
    result = resid + gather_chunks(where, f0_ref, count).astype(f32)
    result = result + gather_chunks(where, f1_ref, count).astype(f32)
    out_ref[...] = (result + vec_ref[4:5, :]).astype(bf16)
    unit, inverse = normalise(resid)
    grad = gather_chunks(where, n0_ref, count).astype(f32)
    grad = grad + gather_chunks(where, n1_ref, count).astype(f32)
    gres = cot + norm_back(grad, unit, inverse, vec_ref[2:3, :])
    gres_ref[...] = gres
    low = gres.astype(bf16)
    low_ref[...] = low
    own_ref[0] = nn_halves(low, a0[0], b0[0]).astype(bf16)
    own_ref[1] = nn_halves(low, a1[0], b1[0]).astype(bf16)
    send_ref[0] = nn_halves(low, a2[0], b2[0]).astype(bf16)
    send_ref[1] = nn_halves(low, a3[0], b3[0]).astype(bf16)

    @pl.when(tile == 0)
    def _():
        sums_ref[...] = jnp.zeros_like(sums_ref)

    sums_ref[0:1, :] += jnp.sum(grad * unit, axis=0, keepdims=True)
    sums_ref[1:2, :] += jnp.sum(grad, axis=0, keepdims=True)
    sums_ref[2:3, :] += jnp.sum(cot, axis=0, keepdims=True)


def middle(where, resid, ffn, gn, cot, weights, vecs, count):
    rows, width = resid.shape
    tile = pl.BlockSpec((ROWS, width), lambda i, w: (i, 0))
    part = pl.BlockSpec((2, ROWS, width // 4), lambda i, w: (0, i, 0))
    piece = struct((2, rows, width // 4), bf16)
    return pl.pallas_call(
        functools.partial(mid_kernel, count),
        out_shape=(
            struct((rows, width), bf16), struct((rows, width), f32), struct((rows, width), bf16),
            piece, piece, struct((8, width), f32),
        ),
        grid_spec=prefetch(
            (rows // ROWS,),
            [*[tile] * 6, *out_weight_specs(width) * 2,
             pl.BlockSpec(vecs.shape, lambda i, w: (0, 0))],
            (tile, tile, tile, part, part, pl.BlockSpec((8, width), lambda i, w: (0, 0))),
        ),
        compiler_params=params(48),
        cost_estimate=cost(12),
        name="middle",
    )(where, resid, *ffn, *gn, cot, *[weights[0]] * 4, *[weights[1]] * 4, vecs)


def token_part(inner, a_ref, b_ref, total):
    lanes = inner.shape[2]

    def tile(index, carry):
        here = pl.ds(pl.multiple_of(index * WIDE, WIDE), WIDE)
        total[here, :] += nt_halves(inner[0, here, :], a_ref[0, :, :lanes], b_ref[0, :, :lanes])
        return carry

    lax.fori_loop(0, total.shape[0] // WIDE, tile, 0)


def weight_part(nt, lt, inner, context, ga_ref, gb_ref):
    lanes = inner.shape[2]
    half = ga_ref.shape[1]
    for grad_ref, start in ((ga_ref, 0), (gb_ref, half)):

        def grads(index, carry, grad_ref=grad_ref, start=start):
            here = pl.ds(pl.multiple_of(index * WIDE, WIDE), WIDE)
            there = pl.ds(pl.multiple_of(start + index * WIDE, WIDE), WIDE)
            grad_ref[0, here, :lanes] = dot_nn(nt[there, :], inner[0]).astype(bf16)
            grad_ref[0, here, lanes:] = dot_nn(lt[there, :], context[0]).astype(bf16)
            return carry

        lax.fori_loop(0, half // WIDE, grads, 0)


def turn_rows(source, target):
    for at in range(0, source.shape[0], ROWS):
        target[:, at : at + ROWS] = source[at : at + ROWS, :].T


def back_early_kernel(where, d0, d1, a_ref, b_ref, n_ref, low_ref, c0, c1,
                      total_ref, ga_ref, gb_ref, nt_ref, lt_ref):
    step = pl.program_id(0)

    @pl.when(step == 0)
    def _():
        turn_rows(n_ref, nt_ref)
        turn_rows(low_ref, lt_ref)
        total_ref[...] = jnp.zeros_like(total_ref)
        token_part(d0, a_ref, b_ref, total_ref)
        weight_part(nt_ref, lt_ref, d0, c0, ga_ref, gb_ref)

    @pl.when(step == 1)
    def _():
        token_part(d1, a_ref, b_ref, total_ref)
        weight_part(nt_ref, lt_ref, d1, c1, ga_ref, gb_ref)


def back_tokens_kernel(where, d0, d1, a0, b0, a1, b1, before_ref, x_ref, gres_ref, vec_ref,
                       g0, g1, g2, g3, sums_ref):
    lanes = d0.shape[2]
    grad = before_ref[...] + nt_halves(d0[0], a0[0, :, :lanes], b0[0, :, :lanes])
    grad = grad + nt_halves(d1[0], a1[0, :, :lanes], b1[0, :, :lanes])
    unit, inverse = normalise(x_ref[...].astype(f32))
    result = gres_ref[...] + norm_back(grad, unit, inverse, vec_ref[0:1, :])
    result = result.astype(bf16)
    turn = pl.program_id(0) ^ (where[2] // 2 * 2 + where[0])
    for index, out_ref in enumerate((g0, g1, g2, g3)):

        @pl.when(turn == index)
        def _(out_ref=out_ref):
            out_ref[...] = result

    @pl.when(pl.program_id(0) == 0)
    def _():
        sums_ref[...] = jnp.zeros_like(sums_ref)

    sums_ref[0:1, :] += jnp.sum(grad * unit, axis=0, keepdims=True)
    sums_ref[1:2, :] += jnp.sum(grad, axis=0, keepdims=True)


def back_weights_kernel(where, d0, d1, nt_ref, lt_ref, c0, c1, ga_ref, gb_ref):
    step = pl.program_id(0)

    @pl.when(step == 0)
    def _():
        weight_part(nt_ref, lt_ref, d0, c0, ga_ref, gb_ref)

    @pl.when(step == 1)
    def _():
        weight_part(nt_ref, lt_ref, d1, c1, ga_ref, gb_ref)


def side(s, w):
    return jnp.where(s == 0, w[0], 1 - w[0])


def fixed_spec(shape):
    return pl.BlockSpec(shape, lambda s, w: (0,) * len(shape), pipeline_mode=pl.Buffered(1))


def back_early(where, normed, low, grads, contexts, weights, part):
    rows, width = normed.shape
    whole, total = fixed_spec((rows, width)), pl.BlockSpec((rows, width), lambda s, w: (0, 0))
    inner, context = fixed_spec((1, rows, width * 3 // 4)), fixed_spec((1, rows, width // 4))
    weight = pl.BlockSpec((1, width // 2, width), lambda s, w: (2 * side(s, w) + part, 0, 0))
    grad = pl.BlockSpec((1, width // 2, width), lambda s, w: (side(s, w), 0, 0))
    shape = struct((2, width // 2, width), bf16)
    turned = struct((width, rows), bf16)
    return pl.pallas_call(
        back_early_kernel,
        out_shape=(struct((rows, width), f32), shape, shape, turned, turned),
        grid_spec=prefetch(
            (2,), [inner, inner, weight, weight, whole, whole, context, context],
            (total, grad, grad, total, total),
        ),
        compiler_params=params(56),
        cost_estimate=cost(19),
        name="back_early",
    )(where, *grads, *weights, normed, low, *contexts)


def back_tokens(where, grads, weights, part, before, x, gres, vecs):
    rows, width = x.shape
    tile = pl.BlockSpec((ROWS, width), lambda i, w: (i, 0))
    inner = pl.BlockSpec((1, ROWS, width * 3 // 4), lambda i, w: (0, i, 0))
    weight = lambda s: pl.BlockSpec(
        (1, width // 2, width), lambda i, w: (2 * side(s, w) + part, 0, 0)
    )
    return pl.pallas_call(
        back_tokens_kernel,
        out_shape=(*[struct((ROWS, width), bf16)] * 4, struct((8, width), f32)),
        grid_spec=prefetch(
            (rows // ROWS,),
            [inner, inner, weight(0), weight(0), weight(1), weight(1), tile, tile, tile,
             pl.BlockSpec(vecs.shape, lambda i, w: (0, 0))],
            (
                *[pl.BlockSpec((ROWS, width), lambda i, w: (0, 0))] * 4,
                pl.BlockSpec((8, width), lambda i, w: (0, 0)),
            ),
        ),
        compiler_params=params(48),
        cost_estimate=cost(11),
        name="back_tokens",
    )(where, *grads, *weights, *weights, before, x, gres, vecs)


def back_weights(where, grads, contexts, turned):
    width, rows = turned[0].shape
    inner, context = fixed_spec((1, rows, width * 3 // 4)), fixed_spec((1, rows, width // 4))
    grad = pl.BlockSpec((1, width // 2, width), lambda s, w: (side(s, w), 0, 0))
    shape = struct((2, width // 2, width), bf16)
    return pl.pallas_call(
        back_weights_kernel,
        out_shape=(shape, shape),
        grid_spec=prefetch(
            (2,), [inner, inner, *[fixed_spec((width, rows))] * 2, context, context], (grad, grad)
        ),
        compiler_params=params(40),
        cost_estimate=cost(10),
        name="back_weights",
    )(where, *grads, *turned, *contexts)


def restore_direct(where, pieces, count, dtype):
    rows, width = pieces[0].shape
    if (width // count) % 128:
        core, d, z = where[0], where[1], where[2]
        fixed = []
        for turn, piece in enumerate(pieces):
            matrix = chunk_matrix(d - core + (z ^ turn) % 2, width, count)
            fixed.append(jnp.dot(piece, matrix.T, preferred_element_type=f32).astype(dtype))
        fixed = jnp.stack(fixed)
        return jnp.stack([lax.dynamic_index_in_dim(fixed, z ^ i, 0, False) for i in range(4)])
    whole = lambda shape: pl.BlockSpec(shape, lambda i, w: (0,) * len(shape))
    return pl.pallas_call(
        functools.partial(restore_direct_kernel, count),
        out_shape=struct((4, rows, width), dtype),
        grid_spec=prefetch((1,), [whole((rows, width))] * 4, whole((4, rows, width))),
        compiler_params=params(24),
        cost_estimate=cost(4),
        name="restore_direct",
    )(where, *pieces)


def token_routes(dp_count, tensor_count, turn):
    routes = []
    for d in range(dp_count):
        for z in range(tensor_count):
            source = (2 * (z // 2) + d % 2) ^ turn
            routes.append((d * tensor_count + z, (d - d % 2 + z % 2) * tensor_count + source))
    return routes


def pack_kernel(*refs):
    *vectors, rand_ref, glob_ref, out_ref = refs
    lanes = out_ref.shape[2]
    out_ref[...] = jnp.zeros_like(out_ref)
    copies = out_ref.shape[0]
    spread = lambda row: jnp.broadcast_to(row.astype(f32)[None], (copies, *row.shape)).astype(bf16)
    for index, vector in enumerate(vectors):
        out_ref[:, index : index + 1, : vector.shape[1]] = spread(vector[...])
    start = 8
    out_ref[:, start : start + rand_ref.shape[0], :] = spread(rand_ref[...])
    start += rand_ref.shape[0]
    out_ref[:, start : start + 1, : glob_ref.shape[1]] = spread(glob_ref[...])


def pack(vectors, rand, glob, copies):
    rows = 8 + rand.shape[0] + 1
    rows = -(-rows // 16) * 16
    return pl.pallas_call(
        pack_kernel,
        out_shape=struct((copies, rows, rand.shape[1]), bf16),
        compiler_params=params(8),
        name="pack",
    )(*vectors, rand, glob)


def after(value, *others):
    return lax.optimization_barrier((value, others))[0]


def unpack_kernel(p0, p1, p2, p3, up_ref, down_ref):
    total = p0[...].astype(f32) + p1[...].astype(f32) + p2[...].astype(f32) + p3[...].astype(f32)
    up_ref[...] = total[0]
    down_ref[...] = total[1].T


def unpack_pair(*pairs):
    _, rows, width = pairs[0].shape
    return pl.pallas_call(
        unpack_kernel,
        out_shape=(struct((rows, width), f32), struct((width, rows), f32)),
        compiler_params=params(16),
        name="unpack_pair",
    )(*pairs)


def per_device(
    block_in, norm1_gain, norm1_bias, w_query, w_key, w_value, w_out, norm2_gain, norm2_bias,
    w_up, up_bias, w_down, down_bias, segments, rand_blocks, glob_blocks, cotangent,
):
    dp_count, tensor_count = lax.axis_size("dp"), lax.axis_size("tensor")
    d, z = lax.axis_index("dp").astype(jnp.int32), lax.axis_index("tensor").astype(jnp.int32)
    core = d % 2
    where = jnp.stack([core, d, z])
    batches, local, width = block_in.shape
    share = local // 2
    blocks = segments.shape[1] // BLOCK
    pairs = dp_count // 2

    def move(value, to):
        routes = [
            (a * tensor_count + b, to(a, b)[0] * tensor_count + to(a, b)[1] % tensor_count)
            for a in range(dp_count)
            for b in range(tensor_count)
        ]
        return lax.ppermute(value, BOTH, routes)

    def other_core(value):
        return move(value, lambda a, b: (a ^ 1, b))

    def along(value, step):
        return move(value, lambda a, b: (a, b + step + tensor_count))

    def across(value, r):
        return move(value, lambda a, b: (a ^ (2 * r), b))

    def exchange(value):
        return lax.all_to_all(value, "tensor", split_axis=0, concat_axis=0, tiled=True)

    def half_of(value, which):
        value = value.reshape(batches, 2, share, width)
        return lax.dynamic_index_in_dim(value, which, 1, keepdims=False)

    def both_halves(keep, come):
        both = jnp.where(core == 0, jnp.stack([keep, come], 1), jnp.stack([come, keep], 1))
        return both.reshape(2 * batches * share, width)

    def give(value):
        return exchange(value).reshape(2 * batches, share, width)

    chunk = norm1_gain.shape[0]
    devices = dp_count * tensor_count
    rand_rows = rand_blocks.reshape(-1, 128)
    rows_each = rand_rows.shape[0] // batches
    small = pack(
        [v.reshape(1, chunk) for v in (norm1_gain, norm1_bias, norm2_gain, norm2_bias, down_bias, up_bias)],
        rand_rows, glob_blocks.reshape(1, -1), devices,
    )
    shard = jnp.concatenate([w_query, w_key, w_value, w_out.T], axis=1)
    attn_slots = [along(shard, -k) for k in range(1, tensor_count)]
    their_segments = other_core(segments)
    x_come, cot_come = other_core(half_of(block_in, 1 - core)), other_core(half_of(cotangent, 1 - core))
    x_half = both_halves(half_of(block_in, core), x_come)
    small, x_half = lax.optimization_barrier((small, x_half))
    small = lax.all_to_all(small, BOTH, split_axis=0, concat_axis=0, tiled=True)
    attn_slots, small = lax.optimization_barrier((attn_slots, small))
    attn_slots = jnp.stack([shard, *attn_slots])
    x = exchange(x_half)
    small = small.reshape(dp_count, tensor_count, *small.shape[1:])
    vectors = small[:, :, :6, :chunk].astype(f32)
    up_shift = vectors[:, :, 5].transpose(1, 0, 2).reshape(tensor_count, 1, -1)
    places = jnp.arange(dp_count, dtype=jnp.int32)
    order = chunk_at(d, places, dp_count)
    vecs = jnp.take(vectors[:, 0, :5], order, axis=0).transpose(1, 0, 2).reshape(5, width)
    vecs = jnp.concatenate([vecs, jnp.zeros((3, width), f32)])
    ints = lax.dynamic_index_in_dim(small, d - core + z % 2, 0, keepdims=False).astype(jnp.int32)
    rand_heads = ints[:, 8 : 8 + rand_rows.shape[0]].reshape(tensor_count, batches, rows_each, 128)
    rand_heads = lax.dynamic_index_in_dim(rand_heads, z // 2, 1, keepdims=False)
    rand_heads = lax.dynamic_slice_in_dim(jnp.roll(rand_heads, -z, axis=0), 2 * core, 2, 0)
    rand_heads = rand_heads.reshape(2 * rand_blocks.shape[2], blocks, RAND)
    glob_row = ints[0, 8 + rand_rows.shape[0], : glob_blocks.size].reshape(batches, -1)
    glob_row = lax.dynamic_index_in_dim(glob_row, z // 2, 0, keepdims=False)
    segment_row = lax.dynamic_index_in_dim(
        jnp.where(z % 2 == core, segments, their_segments), z // 2, 0, keepdims=False
    )
    segment_lanes = jnp.broadcast_to(segment_row[:, None], (segment_row.shape[0], 128))
    per_piece = share // BLOCK
    half = tensor_count * share

    def row_of(block):
        source, place = block // (2 * per_piece), block % (2 * per_piece)
        side = place // per_piece
        return jnp.where(side == core, 0, half) + source * share + (place % per_piece) * BLOCK

    table = attention_table(rand_heads, glob_row, row_of, 2 * half)

    attn_own = [attn_slots] + [across(attn_slots, r) for r in range(1, pairs)]
    pair_shard = jnp.stack([w_up, w_down.T])
    pair_weights = lax.all_gather(pair_shard, BOTH, axis=0, tiled=False)
    pair_weights = pair_weights.reshape(dp_count, tensor_count, 2, *w_up.shape)
    cot_half = both_halves(half_of(cotangent, core), cot_come)
    x, attn_own, table, segment_lanes, vecs, up_shift, cot_half = lax.optimization_barrier(
        (x, attn_own, table, segment_lanes, vecs, up_shift, cot_half)
    )
    attn_own = jnp.concatenate(attn_own, axis=-2)
    attn_weights = (attn_own, other_core(attn_own))
    aligned = chunk % 128 == 0
    own_features = chunk_matrix(d, width, dp_count)
    if not aligned:
        x = jnp.dot(x, own_features, preferred_element_type=f32).astype(bf16)

    send, x, normed = project(where, x, vecs, attn_weights, True, dp_count)
    oth = other_core(send)
    own = project(where, normed, vecs, attn_weights, False, dp_count)
    ctx_own0, ctx_send0, lse0 = attn_fwd(table, own, oth, segment_lanes, blocks, 0)
    ctx_oth0 = other_core(ctx_send0)
    ctx_own1, ctx_send1, lse1 = attn_fwd(table, own, oth, segment_lanes, blocks, 1)
    ctx_oth1 = other_core(ctx_send1)
    cot = exchange(cot_half)
    resid, normed_two = out_project(
        where, x, (ctx_own0, ctx_own1, ctx_oth0, ctx_oth1), attn_weights, vecs, dp_count
    )
    if not aligned:
        normed_two = jnp.dot(normed_two, own_features.T, preferred_element_type=f32).astype(bf16)
    ffn0, gn0, pair0, bias0 = feed_forward(
        where, normed_two, cot, pair_weights, up_shift, 2
    )

    def reduce_rows(total):
        flat = total.reshape(-1, total.shape[-1])
        result = lax.psum_scatter(flat, "dp", scatter_dimension=0, tiled=True)
        return result.reshape(total.shape[1:])

    ffn1, gn1, pair1, bias1 = feed_forward(
        where, normed_two, cot, pair_weights, up_shift, 0
    )
    pair_total0 = reduce_rows(pair0)
    pair_total1 = reduce_rows(pair1)
    grad_bias = jnp.concatenate([bias1, bias0])
    ffn, grad_two = (ffn0, ffn1), (gn0, gn1)
    if not aligned:
        reorder = lambda v: jnp.dot(v, own_features, preferred_element_type=f32).astype(bf16)
        ffn, grad_two, cot = map(reorder, ffn), map(reorder, grad_two), reorder(cot)

    def reduce_core(own_half, other_half):
        theirs = other_core(other_half)
        size = own_half.shape[-2] // pairs
        return [
            (
                own_half[..., r * size : (r + 1) * size, :].astype(f32)
                + theirs[..., r * size : (r + 1) * size, :].astype(f32)
            ).astype(own_half.dtype)
            for r in range(pairs)
        ]

    def add_parts(first, others):
        total = first.astype(f32)
        for part in others:
            total = total + part.astype(f32)
        return total.astype(first.dtype)

    def reduce_across(parts):
        return add_parts(parts[0], [across(parts[r], r) for r in range(1, pairs)])

    piece = width // devices

    def exchange_sums(sums_one, sums_two, grad_bias):
        five = jnp.concatenate([sums_one[:2], sums_two[:3]]).reshape(5, dp_count, chunk)
        relative = places ^ d
        back = (relative % 2) * pairs + relative // 2
        five = jnp.take(five, back, axis=1).reshape(5, devices, piece).transpose(1, 0, 2)
        shift = jnp.roll(grad_bias, z, axis=0)
        shift = shift.reshape(tensor_count, dp_count, -1).transpose(1, 0, 2)
        sums = jnp.concatenate([five.reshape(devices, -1), shift.reshape(devices, -1)], axis=1)
        return lax.all_to_all(sums, BOTH, split_axis=0, concat_axis=0, tiled=True)

    def reduce_along(total, slots):
        return sum(
            (along(total[i], k) if k else total[i]).astype(f32) for i, k in enumerate(slots)
        )

    out, grad_resid, low, gctx_own, gctx_send, sums_two = middle(
        where, resid, tuple(ffn), tuple(grad_two), cot, attn_weights, vecs, dp_count
    )
    gctx_oth = other_core(gctx_send)
    out_back = give(out)
    d_own0, d_send0 = attn_bwd(
        table, own, oth, gctx_own, gctx_oth, segment_lanes, lse0, blocks, 0
    )
    d_send0, out_back = lax.optimization_barrier((d_send0, out_back))
    d_oth0 = other_core(d_send0)
    total_one, ga0, gb0, *turned = back_early(
        where, normed, low, (d_own0, d_oth0), (ctx_own0, ctx_oth0), attn_weights, 0
    )
    attn_parts0 = reduce_core(ga0, gb0)
    out_other = other_core(half_of(out_back, 1 - core))
    lse1, attn_parts0, out_other = lax.optimization_barrier((lse1, attn_parts0, out_other))
    d_own1, d_send1 = attn_bwd(
        table, own, oth, gctx_own, gctx_oth, segment_lanes, lse1, blocks, 1
    )
    attn_total0 = reduce_across(attn_parts0)
    pair_next = [along(pair_total0[0], 2), along(pair_total0[1], 3)]
    d_send1, attn_total0, pair_next = lax.optimization_barrier((d_send1, attn_total0, pair_next))
    d_oth1 = other_core(d_send1)
    ga1, gb1 = back_weights(where, (d_own1, d_oth1), (ctx_own1, ctx_oth1), turned)
    total_one, ga1, gb1 = lax.optimization_barrier((total_one, ga1, gb1))
    *grad_in, sums_one = back_tokens(
        where, (d_own1, d_oth1), attn_weights, 1, total_one, x, grad_resid, vecs
    )
    grad_in, out_back, out_other, pair_total1 = lax.optimization_barrier(
        (grad_in, out_back, out_other, pair_total1)
    )
    grad_back = [
        lax.ppermute(piece, BOTH, token_routes(dp_count, tensor_count, turn))
        for turn, piece in enumerate(grad_in)
    ]
    attn_parts1 = reduce_core(ga1, gb1)
    pair_next.append(along(pair_total1[1], 1))
    sums_one, attn_parts1 = lax.optimization_barrier((sums_one, attn_parts1))
    sums = exchange_sums(sums_one, sums_two, grad_bias)
    attn_come1 = [across(attn_parts1[r], r) for r in range(1, pairs)]
    sums, attn_come1 = lax.optimization_barrier((sums, attn_come1))
    attn_total1 = add_parts(attn_parts1[0], attn_come1)
    block_out = restore(where, out_back, out_other, dp_count, bf16).reshape(batches, local, width)
    g_attn = reduce_along(attn_total0, (0, 2)) + reduce_along(attn_total1, (1, 3))
    g_up, g_down = unpack_pair(pair_total1[0], *pair_next)
    grad_in = restore_direct(where, grad_back, dp_count, f32).reshape(batches, local, width)

    sums = jnp.sum(sums, axis=0)
    vector_grads = [sums[i * piece : (i + 1) * piece] for i in range(5)]
    quarter = width // 4
    return (
        block_out, grad_in, vector_grads[0], vector_grads[1],
        g_attn[:, :quarter], g_attn[:, quarter : 2 * quarter], g_attn[:, 2 * quarter : 3 * quarter],
        g_attn[:, 3 * quarter :].T, vector_grads[2], vector_grads[3],
        g_up, sums[5 * piece :][None], g_down, vector_grads[4],
    )


def solution(mesh):
    rows, both = P(None, BOTH, None), P(BOTH)
    dp, split, turned = P("dp"), P("dp", "tensor"), P("tensor", "dp")
    return jax.shard_map(
        per_device,
        mesh=mesh,
        in_specs=(
            rows, dp, dp, split, split, split, turned, dp, dp, split, turned, turned, dp,
            P(None, "dp"), P(None, "dp", "tensor", None, None), P(None, "dp", None), rows,
        ),
        out_specs=(
            rows, rows, both, both, split, split, split, turned, both, both, split, turned, turned,
            both,
        ),
        check_vma=False,
    )
```

```python
import functools
import jax
import jax.numpy as jnp
from jax import lax
from jax.sharding import PartitionSpec as P
from jax.experimental import pallas as pl
from jax.experimental.pallas import tpu as pltpu

HD = 64
BLOCK = 64
COMMON = 5
RAND = 3
BIG = 1e30
bf16 = jnp.bfloat16
f32 = jnp.float32


def cost(micros):
    return pl.CostEstimate(flops=int(micros * 10**9), bytes_accessed=1000, transcendentals=0)


def dot_nt(left, right):
    return lax.dot_general(left, right, (((1,), (1,)), ((), ())), preferred_element_type=f32)


def dot_tn(left, right):
    return lax.dot_general(left, right, (((0,), (0,)), ((), ())), preferred_element_type=f32)


def dot_nn(left, right):
    return lax.dot_general(left, right, (((1,), (0,)), ((), ())), preferred_element_type=f32)


def low_half(shape):
    return lax.broadcasted_iota(jnp.int32, shape, 1) % 128 < HD


def slot_offsets(tab, layout, pair, block):
    common_at, rand_at, blocks, heads = layout
    shared = [
        pl.multiple_of(tab[common_at + block * COMMON + slot], BLOCK) for slot in range(COMMON)
    ]
    first = rand_at + (2 * pair * blocks + block) * RAND
    second = first + blocks * RAND
    drawn = [
        (pl.multiple_of(tab[first + slot], BLOCK), pl.multiple_of(tab[second + slot], BLOCK))
        for slot in range(RAND)
    ]
    return shared, drawn


def gather_rows(ref, shared, drawn, width):
    keep = low_half((BLOCK, width))
    parts = [ref[pl.ds(start, BLOCK), :width] for start in shared]
    for left, right in drawn:
        parts.append(
            jnp.where(keep, ref[pl.ds(left, BLOCK), :width], ref[pl.ds(right, BLOCK), :width])
        )
    return jnp.concatenate(parts, axis=0)


def block_diag(rows):
    keep = low_half(rows.shape)
    zero = jnp.zeros_like(rows)
    return jnp.concatenate([jnp.where(keep, rows, zero), jnp.where(keep, zero, rows)], axis=0)


def fold_heads(rows):
    keep = low_half((BLOCK, 128))
    return jnp.where(keep, rows[:BLOCK], rows[BLOCK:])


def query_rows(qbuf, kaug, start):
    scaled = qbuf[pl.ds(start, BLOCK), :]
    hot = kaug[pl.ds(start, BLOCK), 128:]
    penalty = (hot - jnp.ones_like(hot)) * jnp.asarray(BIG, bf16)
    return block_diag(jnp.concatenate([scaled, penalty], axis=1))


def fill_keys(tab, layout, seg_ref, kaug, half, k_own, k_oth):
    blocks = layout[2]

    @pl.when(pl.program_id(0) == 0)
    def _():
        lane = lax.broadcasted_iota(jnp.int32, (BLOCK, 128), 1) % HD

        def one(block, carry):
            row = pl.multiple_of(tab[block], BLOCK)
            seg = seg_ref[pl.ds(pl.multiple_of(block * BLOCK, BLOCK), BLOCK), :]
            kaug[pl.ds(row, BLOCK), 128:] = jnp.where(seg == lane, 1.0, 0.0).astype(bf16)
            return carry

        lax.fori_loop(0, blocks, one, 0)
        kaug[2 * half :, :128] = jnp.zeros((BLOCK, 128), bf16)
        kaug[2 * half :, 128:] = jnp.where(lane == HD - 1, 1.0, 0.0).astype(bf16)

    kaug[:half, :128] = k_own[0]
    kaug[half : 2 * half, :128] = k_oth[0]


def attn_fwd_kernel(
    layout, first_pair, unroll, tab, q_own, q_oth, k_own, k_oth, v_own, v_oth, seg_ref,
    out_own, out_oth, lse_ref, kaug, vbuf, qbuf, obuf, sbuf,
):
    pair = first_pair + pl.program_id(0)
    half = q_own.shape[1]
    blocks = layout[2]
    fill_keys(tab, layout, seg_ref, kaug, half, k_own, k_oth)
    vbuf[:half, :] = v_own[0]
    vbuf[half : 2 * half, :] = v_oth[0]
    vbuf[2 * half :, :] = jnp.zeros((BLOCK, 128), bf16)
    scale = jnp.asarray(0.125, bf16)
    qbuf[:half, :] = q_own[0] * scale
    qbuf[half:, :] = q_oth[0] * scale

    def step(index, carry):
        group = [index * unroll + part for part in range(unroll)]
        rows = [pl.multiple_of(tab[block], BLOCK) for block in group]
        slots = [slot_offsets(tab, layout, pair, block) for block in group]
        scores = [
            dot_nt(gather_rows(kaug, *slot, 256), query_rows(qbuf, kaug, row))
            for slot, row in zip(slots, rows)
        ]
        top = [jnp.max(score, axis=0, keepdims=True) for score in scores]
        weight = [jnp.exp(score - most) for score, most in zip(scores, top)]
        total = [jnp.sum(part, axis=0, keepdims=True) for part in weight]
        probs = [(part * (1.0 / whole)).astype(bf16) for part, whole in zip(weight, total)]
        context = [
            dot_tn(prob, gather_rows(vbuf, *slot, 128)) for prob, slot in zip(probs, slots)
        ]
        for block, row, part, most, whole in zip(group, rows, context, top, total):
            obuf[pl.ds(row, BLOCK), :] = fold_heads(part).astype(bf16)
            lse_ref[0, pl.ds(block, 1), :] = most + jnp.log(whole)
        return carry

    lax.fori_loop(0, blocks // unroll, step, 0)

    first, second = tab[blocks], tab[blocks + 1]
    rows = [pl.multiple_of(tab[block], BLOCK) for block in (first, second)]
    query = jnp.concatenate([query_rows(qbuf, kaug, row) for row in rows], axis=0)
    chunk = 512
    pieces = [slice(at, at + chunk) for at in range(0, 2 * half, chunk)]
    top = jnp.full((1, 256), -3e38, f32)
    for here in pieces:
        scores = dot_nt(kaug[here, :], query)
        sbuf[here, :] = scores
        top = jnp.maximum(top, jnp.max(scores, axis=0, keepdims=True))
    total = jnp.zeros((1, 256), f32)
    for here in pieces:
        weight = jnp.exp(sbuf[here, :] - top)
        sbuf[here, :] = weight
        total = total + jnp.sum(weight, axis=0, keepdims=True)
    inverse = 1.0 / total
    context = jnp.zeros((256, 128), f32)
    for here in pieces:
        context = context + dot_tn((sbuf[here, :] * inverse).astype(bf16), vbuf[here, :])
    lse = top + jnp.log(total)
    for index, (block, row) in enumerate(zip((first, second), rows)):
        lanes = slice(index * 128, (index + 1) * 128)
        obuf[pl.ds(row, BLOCK), :] = fold_heads(context[lanes]).astype(bf16)
        lse_ref[0, pl.ds(block, 1), :] = lse[:, lanes]
    out_own[0] = obuf[:half, :]
    out_oth[0] = obuf[half:, :]


def attn_bwd_kernel(
    layout, first_pair, unroll, tab, q_own, q_oth, k_own, k_oth, v_own, v_oth, g_own, g_oth, seg_ref, lse_ref,
    own_ref, oth_ref,
    kaug, vbuf, qbuf, gbuf, dqbuf, dkbuf, dvbuf, sbuf, tbuf,
):
    pair = first_pair + pl.program_id(0)
    half = q_own.shape[1]
    blocks = layout[2]
    fill_keys(tab, layout, seg_ref, kaug, half, k_own, k_oth)
    vbuf[:half, :] = v_own[0]
    vbuf[half : 2 * half, :] = v_oth[0]
    vbuf[2 * half :, :] = jnp.zeros((BLOCK, 128), bf16)
    scale = jnp.asarray(0.125, bf16)
    qbuf[:half, :] = q_own[0] * scale
    qbuf[half:, :] = q_oth[0] * scale
    gbuf[:half, :] = g_own[0]
    gbuf[half:, :] = g_oth[0]
    dkbuf[...] = jnp.zeros_like(dkbuf)
    dvbuf[...] = jnp.zeros_like(dvbuf)
    keep = low_half((BLOCK, 128))

    dummy = 2 * half
    ends = [pl.multiple_of(tab[tab_block], BLOCK) for tab_block in (tab[blocks], tab[blocks + 1])]

    def scatter(ref, updates, slots, base):
        piece = lambda part, slot: updates[part][slot * BLOCK : (slot + 1) * BLOCK]
        for shift in range(-1, unroll + 1):
            block = base + shift
            inside = (block >= 0) & (block < blocks)
            row = jnp.where(inside, tab[jnp.clip(block, 0, blocks - 1)], dummy)
            near = [piece(p, shift - p + 1) for p in range(unroll) if 0 <= shift - p + 1 <= 2]
            ref[pl.ds(pl.multiple_of(row, BLOCK), BLOCK), :] += functools.reduce(jnp.add, near)
        for slot, row in zip((3, 4), ends):
            every = [piece(p, slot) for p in range(unroll)]
            ref[pl.ds(row, BLOCK), :] += functools.reduce(jnp.add, every)
        for part, (_, drawn) in enumerate(slots):
            for slot, (left, right) in enumerate(drawn):
                one = piece(part, COMMON + slot)
                ref[pl.ds(left, BLOCK), :] += jnp.where(keep, one, 0.0)
                ref[pl.ds(right, BLOCK), :] += jnp.where(keep, 0.0, one)

    def step(index, carry):
        group = [index * unroll + part for part in range(unroll)]
        rows = [pl.multiple_of(tab[block], BLOCK) for block in group]
        slots = [slot_offsets(tab, layout, pair, block) for block in group]
        query = [query_rows(qbuf, kaug, row) for row in rows]
        grad = [block_diag(gbuf[pl.ds(row, BLOCK), :]) for row in rows]
        keys = [gather_rows(kaug, *slot, 256) for slot in slots]
        scores = [dot_nt(key, one) for key, one in zip(keys, query)]
        grad_probs = [
            dot_nt(gather_rows(vbuf, *slot, 128), one) for slot, one in zip(slots, grad)
        ]
        probs = [
            jnp.exp(score - lse_ref[0, pl.ds(block, 1), :]) for score, block in zip(scores, group)
        ]
        delta = [jnp.sum(p * g, axis=0, keepdims=True) for p, g in zip(probs, grad_probs)]
        grad_scores = [
            (p * (g - one)).astype(bf16) for p, g, one in zip(probs, grad_probs, delta)
        ]
        grad_query = [dot_tn(one, key[:, :128]) for one, key in zip(grad_scores, keys)]
        grad_key = [dot_nn(one, q[:, :128]) for one, q in zip(grad_scores, query)]
        grad_value = [dot_nn(p.astype(bf16), g) for p, g in zip(probs, grad)]
        for row, one in zip(rows, grad_query):
            dqbuf[pl.ds(row, BLOCK), :] = (fold_heads(one) * 0.125).astype(bf16)
        scatter(dkbuf, grad_key, slots, index * unroll)
        scatter(dvbuf, grad_value, slots, index * unroll)
        return carry

    lax.fori_loop(0, blocks // unroll, step, 0)

    first, second = tab[blocks], tab[blocks + 1]
    rows = [pl.multiple_of(tab[block], BLOCK) for block in (first, second)]
    query = jnp.concatenate([query_rows(qbuf, kaug, row) for row in rows], axis=0)
    grads = [block_diag(gbuf[pl.ds(row, BLOCK), :]) for row in rows]
    grads[1] = jnp.where(first == second, jnp.zeros_like(grads[1]), grads[1])
    grad = jnp.concatenate(grads, axis=0)
    lse = jnp.concatenate([lse_ref[0, pl.ds(block, 1), :] for block in (first, second)], axis=1)
    chunk = 512
    pieces = [slice(at, at + chunk) for at in range(0, 2 * half, chunk)]
    delta = jnp.zeros((1, 256), f32)
    for here in pieces:
        probs = jnp.exp(dot_nt(kaug[here, :], query) - lse)
        grad_probs = dot_nt(vbuf[here, :], grad)
        delta = delta + jnp.sum(probs * grad_probs, axis=0, keepdims=True)
        sbuf[here, :] = probs
        tbuf[here, :] = grad_probs
    grad_query = jnp.zeros((256, 128), f32)
    for here in pieces:
        probs = sbuf[here, :]
        grad_scores = (probs * (tbuf[here, :] - delta)).astype(bf16)
        grad_query = grad_query + dot_tn(grad_scores, kaug[here, :128])
        dkbuf[here, :] += dot_nn(grad_scores, query[:, :128])
        dvbuf[here, :] += dot_nn(probs.astype(bf16), grad)
    for index in (1, 0):
        part = fold_heads(grad_query[index * 128 : (index + 1) * 128]) * 0.125
        dqbuf[pl.ds(rows[index], BLOCK), :] = part.astype(bf16)
    for part, buffer in enumerate((dqbuf, dkbuf, dvbuf)):
        lanes = pl.ds(pl.multiple_of((2 * part + pl.program_id(0)) * 128, 128), 128)
        own_ref[0, :, lanes] = buffer[:half, :].astype(bf16)
        oth_ref[0, :, lanes] = buffer[half : 2 * half, :].astype(bf16)


def table_layout(blocks, heads):
    common_at = blocks + 2
    rand_at = common_at + blocks * COMMON
    return (common_at, rand_at, blocks, heads)


def attention_table(rand_heads, glob_row, row_of, dummy_row):
    heads, blocks, _ = rand_heads.shape
    index = jnp.arange(blocks, dtype=jnp.int32)
    g0, g1 = glob_row[0], glob_row[1]
    dense = (index == g0) | (index == g1)
    near0, near1 = jnp.abs(index - g0) <= 1, jnp.abs(index - g1) <= 1
    full = jnp.broadcast_to
    shared = jnp.stack([index - 1, index, index + 1, full(g0, (blocks,)), full(g1, (blocks,))], axis=1)
    valid = jnp.stack(
        [index > 0, index >= 0, index < blocks - 1, ~near0, ~near1 & (g1 != g0)], axis=1
    ) & ~dense[:, None]
    shared = jnp.where(valid, row_of(jnp.clip(shared, 0, blocks - 1)), dummy_row)
    far = jnp.abs(rand_heads - index[None, :, None]) > 1
    far = far & (rand_heads != g0) & (rand_heads != g1) & ~dense[None, :, None]
    r0, r1, r2 = rand_heads[..., 0], rand_heads[..., 1], rand_heads[..., 2]
    fresh = jnp.stack([r0 == r0, r1 != r0, (r2 != r0) & (r2 != r1)], axis=-1)
    drawn = jnp.where(far & fresh, row_of(rand_heads), dummy_row)
    return jnp.concatenate(
        [row_of(index), glob_row, shared.reshape(-1), drawn.reshape(-1)]
    ).astype(jnp.int32)


def lane_spec(half, slot, column):
    return pl.BlockSpec((1, half, 128), lambda p, tab: (slot, 0, column * 2 + p))


def attn_fwd(tab, qkv_own, qkv_oth, seg_abs, blocks, slot, unroll=8):
    half = qkv_own.shape[1]
    layout = table_layout(blocks, 4 * qkv_own.shape[0])
    rows = 2 * half + BLOCK
    shape = jax.ShapeDtypeStruct((1, half, 256), bf16)
    result = pl.BlockSpec((1, half, 128), lambda p, tab: (0, 0, p))
    return pl.pallas_call(
        functools.partial(attn_fwd_kernel, layout, 2 * slot, unroll),
        out_shape=(shape, shape, jax.ShapeDtypeStruct((2, blocks, 128), f32)),
        grid_spec=pltpu.PrefetchScalarGridSpec(
            num_scalar_prefetch=1,
            grid=(2,),
            in_specs=[
                *[lane_spec(half, slot, column) for column in (0, 0, 1, 1, 2, 2)],
                pl.BlockSpec((2 * half, 128), lambda p, tab: (0, 0)),
            ],
            out_specs=(result, result, pl.BlockSpec((1, blocks, 128), lambda p, tab: (p, 0, 0))),
            scratch_shapes=[
                pltpu.VMEM((rows, 256), bf16), pltpu.VMEM((rows, 128), bf16),
                pltpu.VMEM((2 * half, 128), bf16), pltpu.VMEM((2 * half, 128), bf16),
                pltpu.VMEM((2 * half, 256), f32),
            ],
        ),
        compiler_params=pltpu.CompilerParams(vmem_limit_bytes=60 << 20),
        cost_estimate=cost(17),
        name="attn_fwd",
    )(tab, qkv_own, qkv_oth, qkv_own, qkv_oth, qkv_own, qkv_oth, seg_abs)


def attn_bwd(tab, qkv_own, qkv_oth, grad_own, grad_oth, seg_abs, lse, blocks, slot, unroll=8):
    half = qkv_own.shape[1]
    layout = table_layout(blocks, 4 * qkv_own.shape[0])
    rows = 2 * half + BLOCK
    shape = jax.ShapeDtypeStruct((1, half, 768), bf16)
    result = pl.BlockSpec((1, half, 768), lambda p, tab: (0, 0, 0))
    return pl.pallas_call(
        functools.partial(attn_bwd_kernel, layout, 2 * slot, unroll),
        out_shape=(shape, shape),
        grid_spec=pltpu.PrefetchScalarGridSpec(
            num_scalar_prefetch=1,
            grid=(2,),
            in_specs=[
                *[lane_spec(half, slot, column) for column in (0, 0, 1, 1, 2, 2, 0, 0)],
                pl.BlockSpec((2 * half, 128), lambda p, tab: (0, 0)),
                pl.BlockSpec((1, blocks, 128), lambda p, tab: (p, 0, 0)),
            ],
            out_specs=(result, result),
            scratch_shapes=[
                pltpu.VMEM((rows, 256), bf16), pltpu.VMEM((rows, 128), bf16),
                pltpu.VMEM((2 * half, 128), bf16), pltpu.VMEM((2 * half, 128), bf16),
                pltpu.VMEM((2 * half, 128), bf16),
                pltpu.VMEM((rows, 128), f32), pltpu.VMEM((rows, 128), f32),
                pltpu.VMEM((2 * half, 256), f32), pltpu.VMEM((2 * half, 256), f32),
            ],
        ),
        compiler_params=pltpu.CompilerParams(vmem_limit_bytes=60 << 20),
        cost_estimate=cost(29),
        name="attn_bwd",
    )(tab, qkv_own, qkv_oth, qkv_own, qkv_oth, qkv_own, qkv_oth, grad_own, grad_oth, seg_abs, lse)


EPS = 1e-05
BOTH = ("dp", "tensor")
ROWS = 256
WIDE = 512


def gelu_pair(u):
    c = 0.7978845608028654
    square = u * u
    bend = jnp.tanh(u * (c + (c * 0.044715) * square))
    half = 0.5 * (1.0 + bend)
    slope = half + (0.5 * u) * (1.0 - bend * bend) * (c + (3.0 * c * 0.044715) * square)
    return u * half, slope


def normalise(rows):
    center = rows - jnp.mean(rows, axis=-1, keepdims=True)
    inverse = lax.rsqrt(jnp.mean(center * center, axis=-1, keepdims=True) + EPS)
    return center * inverse, inverse


def norm_back(grad, unit, inverse, gain):
    scaled = grad * gain
    mean = jnp.mean(scaled, axis=-1, keepdims=True)
    along = jnp.mean(scaled * unit, axis=-1, keepdims=True)
    return inverse * (scaled - mean - unit * along)


def params(mib):
    return pltpu.CompilerParams(vmem_limit_bytes=mib << 20)


def prefetch(grid, in_specs, out_specs, scratch=()):
    return pltpu.PrefetchScalarGridSpec(
        num_scalar_prefetch=1, grid=grid, in_specs=in_specs, out_specs=out_specs,
        scratch_shapes=list(scratch),
    )


def struct(shape, dtype):
    return jax.ShapeDtypeStruct(shape, dtype)


def nn_halves(rows, low_ref, high_ref):
    split = rows.shape[1] // 2
    return dot_nn(rows[:, :split], low_ref) + dot_nn(rows[:, split:], high_ref)


def nt_halves(rows, low_ref, high_ref):
    return jnp.concatenate([dot_nt(rows, low_ref), dot_nt(rows, high_ref)], axis=1)


def chunk_at(d, place, count):
    return d ^ (2 * (place % (count // 2)) + place // (count // 2))


def restore_direct_kernel(count, where, p0, p1, p2, p3, out_ref):
    width = p0.shape[1]
    chunk = width // count
    core, d, z = where[0], where[1], where[2]
    for turn, piece in enumerate((p0, p1, p2, p3)):
        index = z ^ turn
        sender = d - core + index % 2
        for place in range(count):
            target = pl.ds(pl.multiple_of(chunk_at(sender, place, count) * chunk, chunk), chunk)
            out_ref[index, :, target] = piece[:, place * chunk : (place + 1) * chunk].astype(
                out_ref.dtype
            )


def chunk_matrix(d, width, count):
    chunk = width // count
    index = jnp.arange(width, dtype=jnp.int32)
    source = chunk_at(d, index // chunk, count) * chunk + index % chunk
    return (index[:, None] == source[None, :]).astype(bf16)


def scatter_chunks(where, ref, rows, count):
    chunk = rows.shape[1] // count
    if chunk % 128:
        ref[...] = rows
        return
    for place in range(count):
        target = pl.ds(pl.multiple_of(chunk_at(where[1], place, count) * chunk, chunk), chunk)
        ref[:, target] = rows[:, place * chunk : (place + 1) * chunk]


def gather_chunks(where, ref, count):
    chunk = ref.shape[1] // count
    if chunk % 128:
        return ref[...]
    return jnp.concatenate(
        [
            ref[:, pl.ds(pl.multiple_of(chunk_at(where[1], place, count) * chunk, chunk), chunk)]
            for place in range(count)
        ],
        axis=1,
    )


def project_kernel(count, where, x_ref, vec_ref, wa_ref, wb_ref, out_ref, rel_ref, n_ref, nbuf):
    slot, tile = pl.program_id(0), pl.program_id(1)
    here = pl.ds(pl.multiple_of(tile * WIDE, WIDE), WIDE)

    @pl.when(slot == 0)
    def _():
        rows = gather_chunks(where, x_ref, count)
        rel_ref[...] = rows
        unit, _ = normalise(rows.astype(f32))
        normed = (unit * vec_ref[0:1, :] + vec_ref[1:2, :]).astype(bf16)
        nbuf[here, :] = normed
        n_ref[...] = normed

    out_ref[0] = nn_halves(nbuf[here, :], wa_ref[0], wb_ref[0]).astype(bf16)


def project_more_kernel(where, n_ref, wa_ref, wb_ref, out_ref):
    out_ref[0] = nn_halves(n_ref[...], wa_ref[0], wb_ref[0]).astype(bf16)


def project(where, x, vecs, weights, first, count):
    rows, width = x.shape
    tiles = rows // WIDE
    out = width * 3 // 4
    half = width // 2
    weight = pl.BlockSpec(
        (1, half, out), lambda s, i, w: (2 * (1 - w[0] if first else w[0]) + s, 0, 0)
    )
    outs = pl.BlockSpec((1, WIDE, out), lambda s, i, w: (s, i, 0))
    once = pl.BlockSpec((WIDE, width), lambda s, i, w: (jnp.where(s == 0, i, tiles - 1), 0))
    shape = struct((2, rows, out), bf16)
    if first:
        return pl.pallas_call(
            functools.partial(project_kernel, count),
            out_shape=(shape, struct((rows, width), bf16), struct((rows, width), bf16)),
            grid_spec=prefetch(
                (2, tiles),
                [once, pl.BlockSpec(vecs.shape, lambda s, i, w: (0, 0)), weight, weight],
                (outs, once, once),
                [pltpu.VMEM((rows, width), bf16)],
            ),
            compiler_params=params(32),
            cost_estimate=cost(9),
            name="project",
        )(where, x, vecs, *weights)
    return pl.pallas_call(
        project_more_kernel,
        out_shape=shape,
        grid_spec=prefetch(
            (2, tiles),
            [pl.BlockSpec((WIDE, width), lambda s, i, w: (i, 0)), weight, weight],
            outs,
        ),
        compiler_params=params(32),
        cost_estimate=cost(8),
        name="project_more",
    )(where, x, *weights)


def out_kernel(count, where, x_ref, c0, c1, c2, c3, a0, a1, a2, a3, b0, b1, b2, b3, vec_ref,
               resid_ref, n_ref):
    total = x_ref[...].astype(f32)
    for part, low, high in ((c0, a0, b0), (c1, a1, b1), (c2, a2, b2), (c3, a3, b3)):
        total = total + nt_halves(part[0], low[0], high[0])
    resid_ref[...] = total
    unit, _ = normalise(total)
    scatter_chunks(where, n_ref, (unit * vec_ref[2:3, :] + vec_ref[3:4, :]).astype(bf16), count)


def out_weight_specs(width):
    return [
        pl.BlockSpec((1, width // 2, width // 4), lambda i, w, s=s: ((2 * w[0] + s) % 4, 0, 3))
        for s in range(4)
    ]


def out_project(where, x, contexts, weights, vecs, count):
    rows, width = x.shape
    tile = pl.BlockSpec((ROWS, width), lambda i, w: (i, 0))
    part = pl.BlockSpec((1, ROWS, width // 4), lambda i, w: (0, i, 0))
    return pl.pallas_call(
        functools.partial(out_kernel, count),
        out_shape=(struct((rows, width), f32), struct((rows, width), bf16)),
        grid_spec=prefetch(
            (rows // ROWS,),
            [tile, *[part] * 4, *out_weight_specs(width) * 2,
             pl.BlockSpec(vecs.shape, lambda i, w: (0, 0))],
            (tile, tile),
        ),
        compiler_params=params(60),
        cost_estimate=cost(7),
        name="out_project",
    )(where, x, *contexts, *[weights[0]] * 4, *[weights[1]] * 4, vecs)


def ffn_kernel(where, n_ref, cot_ref, up_ref, down_ref, bias_ref,
               ffn_ref, gn_ref, grad_ref, gbias_ref, nt, ct, act, gup, total, back_total):
    step = pl.program_id(0)
    rows, width = n_ref.shape
    hidden = act.shape[1]
    up = up_ref[...].reshape(width, hidden)
    down = down_ref[...].reshape(width, hidden)

    @pl.when(step == 0)
    def _():
        turn_rows(n_ref, nt)
        turn_rows(cot_ref, ct)
        total[...] = jnp.zeros_like(total)
        back_total[...] = jnp.zeros_like(back_total)

    value = dot_nn(n_ref[...], up) + bias_ref[0]
    out, slope = gelu_pair(value)
    out = out.astype(bf16)
    act[...] = out
    back = (dot_nn(cot_ref[...], down) * slope).astype(bf16)
    gup[...] = back
    gbias_ref[0] = jnp.sum(back.astype(f32), axis=0, keepdims=True)
    total[...] += dot_nt(out, down)
    back_total[...] += dot_nt(back, up)
    shape = grad_ref.shape[0], grad_ref.shape[3], hidden
    grad_ref[:, 0, 0] = dot_nn(nt[...], gup[...]).astype(bf16).reshape(shape)
    grad_ref[:, 0, 1] = dot_nn(ct[...], act[...]).astype(bf16).reshape(shape)

    @pl.when(step == pl.num_programs(0) - 1)
    def _():
        ffn_ref[...] = total[...].astype(bf16)
        gn_ref[...] = back_total[...].astype(bf16)


def feed_forward(where, normed, cot, weights, bias, slots_at):
    rows, width = normed.shape
    count, slots, _, chunk, hidden = weights.shape
    whole = fixed_spec((rows, width))
    slot = lambda s, w: (w[2] + slots_at + s) % slots
    weight = lambda k: pl.BlockSpec(
        (count, 1, 1, chunk, hidden), lambda s, w: (0, slot(s, w), k, 0, 0)
    )
    total = pl.BlockSpec((rows, width), lambda s, w: (0, 0))
    return pl.pallas_call(
        ffn_kernel,
        out_shape=(
            struct((rows, width), bf16), struct((rows, width), bf16),
            struct((count, 2, 2, chunk, hidden), bf16), struct((2, 1, hidden), f32),
        ),
        grid_spec=prefetch(
            (2,),
            [whole, whole, weight(0), weight(1),
             pl.BlockSpec((1, 1, hidden), lambda s, w: (slot(s, w), 0, 0))],
            (
                total, total,
                pl.BlockSpec((count, 1, 2, chunk, hidden), lambda s, w: (0, s, 0, 0, 0)),
                pl.BlockSpec((1, 1, hidden), lambda s, w: (s, 0, 0)),
            ),
            [
                pltpu.VMEM((width, rows), bf16), pltpu.VMEM((width, rows), bf16),
                pltpu.VMEM((rows, hidden), bf16), pltpu.VMEM((rows, hidden), bf16),
                pltpu.VMEM((rows, width), f32), pltpu.VMEM((rows, width), f32),
            ],
        ),
        compiler_params=params(60),
        cost_estimate=cost(38),
        name="feed_forward",
    )(where, normed, cot, weights, weights, bias)


def write_piece(where, tile, refs, rows):
    turn = tile ^ (where[2] // 2 * 2 + where[0])
    for index, ref in enumerate(refs):

        @pl.when(turn == index)
        def _(ref=ref):
            ref[...] = rows


def mid_kernel(count, where, resid_ref, f0_ref, f1_ref, n0_ref, n1_ref, cot_ref, a0, a1, a2, a3, b0, b1, b2, b3, vec_ref,
               o0, o1, o2, o3, gres_ref, low_ref, own_ref, send_ref, sums_ref):
    tile = pl.program_id(0)
    resid = resid_ref[...]
    cot = gather_chunks(where, cot_ref, count).astype(f32)
    result = resid + gather_chunks(where, f0_ref, count).astype(f32)
    result = result + gather_chunks(where, f1_ref, count).astype(f32)
    write_piece(where, tile, (o0, o1, o2, o3), (result + vec_ref[4:5, :]).astype(bf16))
    unit, inverse = normalise(resid)
    grad = gather_chunks(where, n0_ref, count).astype(f32)
    grad = grad + gather_chunks(where, n1_ref, count).astype(f32)
    gres = cot + norm_back(grad, unit, inverse, vec_ref[2:3, :])
    gres_ref[...] = gres
    low = gres.astype(bf16)
    low_ref[...] = low
    own_ref[0] = nn_halves(low, a0[0], b0[0]).astype(bf16)
    own_ref[1] = nn_halves(low, a1[0], b1[0]).astype(bf16)
    send_ref[0] = nn_halves(low, a2[0], b2[0]).astype(bf16)
    send_ref[1] = nn_halves(low, a3[0], b3[0]).astype(bf16)

    @pl.when(tile == 0)
    def _():
        sums_ref[...] = jnp.zeros_like(sums_ref)

    sums_ref[0:1, :] += jnp.sum(grad * unit, axis=0, keepdims=True)
    sums_ref[1:2, :] += jnp.sum(grad, axis=0, keepdims=True)
    sums_ref[2:3, :] += jnp.sum(cot, axis=0, keepdims=True)


def middle(where, resid, ffn, gn, cot, weights, vecs, count):
    rows, width = resid.shape
    tile = pl.BlockSpec((ROWS, width), lambda i, w: (i, 0))
    part = pl.BlockSpec((2, ROWS, width // 4), lambda i, w: (0, i, 0))
    piece = struct((2, rows, width // 4), bf16)
    return pl.pallas_call(
        functools.partial(mid_kernel, count),
        out_shape=(
            *[struct((ROWS, width), bf16)] * 4,
            struct((rows, width), f32), struct((rows, width), bf16),
            piece, piece, struct((8, width), f32),
        ),
        grid_spec=prefetch(
            (rows // ROWS,),
            [*[tile] * 6, *out_weight_specs(width) * 2,
             pl.BlockSpec(vecs.shape, lambda i, w: (0, 0))],
            (*[pl.BlockSpec((ROWS, width), lambda i, w: (0, 0))] * 4, tile, tile, part, part, pl.BlockSpec((8, width), lambda i, w: (0, 0))),
        ),
        compiler_params=params(60),
        cost_estimate=cost(12),
        name="middle",
    )(where, resid, *ffn, *gn, cot, *[weights[0]] * 4, *[weights[1]] * 4, vecs)


def token_part(inner, a_ref, b_ref, total):
    lanes = inner.shape[2]

    def tile(index, carry):
        here = pl.ds(pl.multiple_of(index * WIDE, WIDE), WIDE)
        total[here, :] += nt_halves(inner[0, here, :], a_ref[0, :, :lanes], b_ref[0, :, :lanes])
        return carry

    lax.fori_loop(0, total.shape[0] // WIDE, tile, 0)


def weight_part(nt, lt, inner, context, ga_ref, gb_ref):
    lanes = inner.shape[2]
    half = ga_ref.shape[1]
    for grad_ref, start in ((ga_ref, 0), (gb_ref, half)):

        def grads(index, carry, grad_ref=grad_ref, start=start):
            here = pl.ds(pl.multiple_of(index * WIDE, WIDE), WIDE)
            there = pl.ds(pl.multiple_of(start + index * WIDE, WIDE), WIDE)
            grad_ref[0, here, :lanes] = dot_nn(nt[there, :], inner[0]).astype(bf16)
            grad_ref[0, here, lanes:] = dot_nn(lt[there, :], context[0]).astype(bf16)
            return carry

        lax.fori_loop(0, half // WIDE, grads, 0)


def turn_rows(source, target):
    for at in range(0, source.shape[0], ROWS):
        target[:, at : at + ROWS] = source[at : at + ROWS, :].T


def back_early_kernel(where, d0, d1, a_ref, b_ref, n_ref, low_ref, c0, c1,
                      total_ref, ga_ref, gb_ref, nt_ref, lt_ref):
    step = pl.program_id(0)

    @pl.when(step == 0)
    def _():
        turn_rows(n_ref, nt_ref)
        turn_rows(low_ref, lt_ref)
        total_ref[...] = jnp.zeros_like(total_ref)
        token_part(d0, a_ref, b_ref, total_ref)
        weight_part(nt_ref, lt_ref, d0, c0, ga_ref, gb_ref)

    @pl.when(step == 1)
    def _():
        token_part(d1, a_ref, b_ref, total_ref)
        weight_part(nt_ref, lt_ref, d1, c1, ga_ref, gb_ref)


def back_tokens_kernel(where, d0, d1, a0, b0, a1, b1, before_ref, x_ref, gres_ref, vec_ref,
                       g0, g1, g2, g3, sums_ref):
    lanes = d0.shape[2]
    grad = before_ref[...] + nt_halves(d0[0], a0[0, :, :lanes], b0[0, :, :lanes])
    grad = grad + nt_halves(d1[0], a1[0, :, :lanes], b1[0, :, :lanes])
    unit, inverse = normalise(x_ref[...].astype(f32))
    result = gres_ref[...] + norm_back(grad, unit, inverse, vec_ref[0:1, :])
    result = result.astype(bf16)
    write_piece(where, pl.program_id(0), (g0, g1, g2, g3), result)

    @pl.when(pl.program_id(0) == 0)
    def _():
        sums_ref[...] = jnp.zeros_like(sums_ref)

    sums_ref[0:1, :] += jnp.sum(grad * unit, axis=0, keepdims=True)
    sums_ref[1:2, :] += jnp.sum(grad, axis=0, keepdims=True)


def back_weights_kernel(where, d0, d1, nt_ref, lt_ref, c0, c1, ga_ref, gb_ref):
    step = pl.program_id(0)

    @pl.when(step == 0)
    def _():
        weight_part(nt_ref, lt_ref, d0, c0, ga_ref, gb_ref)

    @pl.when(step == 1)
    def _():
        weight_part(nt_ref, lt_ref, d1, c1, ga_ref, gb_ref)


def side(s, w):
    return jnp.where(s == 0, w[0], 1 - w[0])


def fixed_spec(shape):
    return pl.BlockSpec(shape, lambda s, w: (0,) * len(shape), pipeline_mode=pl.Buffered(1))


def back_early(where, normed, low, grads, contexts, weights, part):
    rows, width = normed.shape
    whole, total = fixed_spec((rows, width)), pl.BlockSpec((rows, width), lambda s, w: (0, 0))
    inner, context = fixed_spec((1, rows, width * 3 // 4)), fixed_spec((1, rows, width // 4))
    weight = pl.BlockSpec((1, width // 2, width), lambda s, w: (2 * side(s, w) + part, 0, 0))
    grad = pl.BlockSpec((1, width // 2, width), lambda s, w: (side(s, w), 0, 0))
    shape = struct((2, width // 2, width), bf16)
    turned = struct((width, rows), bf16)
    return pl.pallas_call(
        back_early_kernel,
        out_shape=(struct((rows, width), f32), shape, shape, turned, turned),
        grid_spec=prefetch(
            (2,), [inner, inner, weight, weight, whole, whole, context, context],
            (total, grad, grad, total, total),
        ),
        compiler_params=params(60),
        cost_estimate=cost(19),
        name="back_early",
    )(where, *grads, *weights, normed, low, *contexts)


def back_tokens(where, grads, weights, part, before, x, gres, vecs):
    rows, width = x.shape
    tile = pl.BlockSpec((ROWS, width), lambda i, w: (i, 0))
    inner = pl.BlockSpec((1, ROWS, width * 3 // 4), lambda i, w: (0, i, 0))
    weight = lambda s: pl.BlockSpec(
        (1, width // 2, width), lambda i, w: (2 * side(s, w) + part, 0, 0)
    )
    return pl.pallas_call(
        back_tokens_kernel,
        out_shape=(*[struct((ROWS, width), bf16)] * 4, struct((8, width), f32)),
        grid_spec=prefetch(
            (rows // ROWS,),
            [inner, inner, weight(0), weight(0), weight(1), weight(1), tile, tile, tile,
             pl.BlockSpec(vecs.shape, lambda i, w: (0, 0))],
            (
                *[pl.BlockSpec((ROWS, width), lambda i, w: (0, 0))] * 4,
                pl.BlockSpec((8, width), lambda i, w: (0, 0)),
            ),
        ),
        compiler_params=params(60),
        cost_estimate=cost(11),
        name="back_tokens",
    )(where, *grads, *weights, *weights, before, x, gres, vecs)


def back_weights(where, grads, contexts, turned):
    width, rows = turned[0].shape
    inner, context = fixed_spec((1, rows, width * 3 // 4)), fixed_spec((1, rows, width // 4))
    grad = pl.BlockSpec((1, width // 2, width), lambda s, w: (side(s, w), 0, 0))
    shape = struct((2, width // 2, width), bf16)
    return pl.pallas_call(
        back_weights_kernel,
        out_shape=(shape, shape),
        grid_spec=prefetch(
            (2,), [inner, inner, *[fixed_spec((width, rows))] * 2, context, context], (grad, grad)
        ),
        compiler_params=params(60),
        cost_estimate=cost(10),
        name="back_weights",
    )(where, *grads, *turned, *contexts)


def restore_direct(where, pieces, count, dtype):
    rows, width = pieces[0].shape
    if (width // count) % 128:
        core, d, z = where[0], where[1], where[2]
        fixed = []
        for turn, piece in enumerate(pieces):
            matrix = chunk_matrix(d - core + (z ^ turn) % 2, width, count)
            fixed.append(jnp.dot(piece, matrix.T, preferred_element_type=f32).astype(dtype))
        fixed = jnp.stack(fixed)
        return jnp.stack([lax.dynamic_index_in_dim(fixed, z ^ i, 0, False) for i in range(4)])
    whole = lambda shape: pl.BlockSpec(shape, lambda i, w: (0,) * len(shape))
    return pl.pallas_call(
        functools.partial(restore_direct_kernel, count),
        out_shape=struct((4, rows, width), dtype),
        grid_spec=prefetch((1,), [whole((rows, width))] * 4, whole((4, rows, width))),
        compiler_params=params(24),
        cost_estimate=cost(4),
        name="restore_direct",
    )(where, *pieces)


def token_routes(dp_count, tensor_count, turn):
    routes = []
    for d in range(dp_count):
        for z in range(tensor_count):
            source = (2 * (z // 2) + d % 2) ^ turn
            routes.append((d * tensor_count + z, (d - d % 2 + z % 2) * tensor_count + source))
    return routes


def pack_kernel(*refs):
    *vectors, rand_ref, glob_ref, out_ref = refs
    lanes = out_ref.shape[2]
    out_ref[...] = jnp.zeros_like(out_ref)
    copies = out_ref.shape[0]
    spread = lambda row: jnp.broadcast_to(row.astype(f32)[None], (copies, *row.shape)).astype(bf16)
    for index, vector in enumerate(vectors):
        out_ref[:, index : index + 1, : vector.shape[1]] = spread(vector[...])
    start = 8
    out_ref[:, start : start + rand_ref.shape[0], :] = spread(rand_ref[...])
    start += rand_ref.shape[0]
    out_ref[:, start : start + 1, : glob_ref.shape[1]] = spread(glob_ref[...])


def pack(vectors, rand, glob, copies):
    rows = 8 + rand.shape[0] + 1
    rows = -(-rows // 16) * 16
    return pl.pallas_call(
        pack_kernel,
        out_shape=struct((copies, rows, rand.shape[1]), bf16),
        compiler_params=params(8),
        name="pack",
    )(*vectors, rand, glob)


def after(value, *others):
    return lax.optimization_barrier((value, others))[0]


def unpack_kernel(p0, p1, p2, p3, up_ref, down_ref):
    total = p0[...].astype(f32) + p1[...].astype(f32) + p2[...].astype(f32) + p3[...].astype(f32)
    up_ref[...] = total[0]
    down_ref[...] = total[1].T


def unpack_pair(*pairs):
    _, rows, width = pairs[0].shape
    return pl.pallas_call(
        unpack_kernel,
        out_shape=(struct((rows, width), f32), struct((width, rows), f32)),
        compiler_params=params(16),
        name="unpack_pair",
    )(*pairs)


def per_device(
    block_in, norm1_gain, norm1_bias, w_query, w_key, w_value, w_out, norm2_gain, norm2_bias,
    w_up, up_bias, w_down, down_bias, segments, rand_blocks, glob_blocks, cotangent,
):
    dp_count, tensor_count = lax.axis_size("dp"), lax.axis_size("tensor")
    d, z = lax.axis_index("dp").astype(jnp.int32), lax.axis_index("tensor").astype(jnp.int32)
    core = d % 2
    where = jnp.stack([core, d, z])
    batches, local, width = block_in.shape
    share = local // 2
    blocks = segments.shape[1] // BLOCK
    pairs = dp_count // 2

    def move(value, to):
        routes = [
            (a * tensor_count + b, to(a, b)[0] * tensor_count + to(a, b)[1] % tensor_count)
            for a in range(dp_count)
            for b in range(tensor_count)
        ]
        return lax.ppermute(value, BOTH, routes)

    def other_core(value):
        return move(value, lambda a, b: (a ^ 1, b))

    def along(value, step):
        return move(value, lambda a, b: (a, b + step + tensor_count))

    def across(value, r):
        return move(value, lambda a, b: (a ^ (2 * r), b))

    def exchange(value):
        return lax.all_to_all(value, "tensor", split_axis=0, concat_axis=0, tiled=True)

    def half_of(value, which):
        value = value.reshape(batches, 2, share, width)
        return lax.dynamic_index_in_dim(value, which, 1, keepdims=False)

    def both_halves(keep, come):
        both = jnp.where(core == 0, jnp.stack([keep, come], 1), jnp.stack([come, keep], 1))
        return both.reshape(2 * batches * share, width)

    chunk = norm1_gain.shape[0]
    devices = dp_count * tensor_count
    rand_rows = rand_blocks.reshape(-1, 128)
    rows_each = rand_rows.shape[0] // batches
    small = pack(
        [v.reshape(1, chunk) for v in (norm1_gain, norm1_bias, norm2_gain, norm2_bias, down_bias, up_bias)],
        rand_rows, glob_blocks.reshape(1, -1), devices,
    )
    shard = jnp.concatenate([w_query, w_key, w_value, w_out.T], axis=1)
    attn_slots = [along(shard, -k) for k in range(1, tensor_count)]
    their_segments = other_core(segments)
    x_come, cot_come = other_core(half_of(block_in, 1 - core)), other_core(half_of(cotangent, 1 - core))
    x_half = both_halves(half_of(block_in, core), x_come)
    small, x_half = lax.optimization_barrier((small, x_half))
    small = lax.all_to_all(small, BOTH, split_axis=0, concat_axis=0, tiled=True)
    attn_slots, small = lax.optimization_barrier((attn_slots, small))
    attn_slots = jnp.stack([shard, *attn_slots])
    x = exchange(x_half)
    small = small.reshape(dp_count, tensor_count, *small.shape[1:])
    vectors = small[:, :, :6, :chunk].astype(f32)
    up_shift = vectors[:, :, 5].transpose(1, 0, 2).reshape(tensor_count, 1, -1)
    places = jnp.arange(dp_count, dtype=jnp.int32)
    order = chunk_at(d, places, dp_count)
    vecs = jnp.take(vectors[:, 0, :5], order, axis=0).transpose(1, 0, 2).reshape(5, width)
    vecs = jnp.concatenate([vecs, jnp.zeros((3, width), f32)])
    ints = lax.dynamic_index_in_dim(small, d - core + z % 2, 0, keepdims=False).astype(jnp.int32)
    rand_heads = ints[:, 8 : 8 + rand_rows.shape[0]].reshape(tensor_count, batches, rows_each, 128)
    rand_heads = lax.dynamic_index_in_dim(rand_heads, z // 2, 1, keepdims=False)
    rand_heads = lax.dynamic_slice_in_dim(jnp.roll(rand_heads, -z, axis=0), 2 * core, 2, 0)
    rand_heads = rand_heads.reshape(2 * rand_blocks.shape[2], blocks, RAND)
    glob_row = ints[0, 8 + rand_rows.shape[0], : glob_blocks.size].reshape(batches, -1)
    glob_row = lax.dynamic_index_in_dim(glob_row, z // 2, 0, keepdims=False)
    segment_row = lax.dynamic_index_in_dim(
        jnp.where(z % 2 == core, segments, their_segments), z // 2, 0, keepdims=False
    )
    segment_lanes = jnp.broadcast_to(segment_row[:, None], (segment_row.shape[0], 128))
    per_piece = share // BLOCK
    half = tensor_count * share

    def row_of(block):
        source, place = block // (2 * per_piece), block % (2 * per_piece)
        side = place // per_piece
        return jnp.where(side == core, 0, half) + source * share + (place % per_piece) * BLOCK

    table = attention_table(rand_heads, glob_row, row_of, 2 * half)

    attn_own = [attn_slots] + [across(attn_slots, r) for r in range(1, pairs)]
    pair_shard = jnp.stack([w_up, w_down.T])
    pair_weights = lax.all_gather(pair_shard, BOTH, axis=0, tiled=False)
    pair_weights = pair_weights.reshape(dp_count, tensor_count, 2, *w_up.shape)
    cot_half = both_halves(half_of(cotangent, core), cot_come)
    x, attn_own, table, segment_lanes, vecs, up_shift, cot_half = lax.optimization_barrier(
        (x, attn_own, table, segment_lanes, vecs, up_shift, cot_half)
    )
    attn_own = jnp.concatenate(attn_own, axis=-2)
    attn_weights = (attn_own, other_core(attn_own))
    aligned = chunk % 128 == 0
    own_features = chunk_matrix(d, width, dp_count)
    if not aligned:
        x = jnp.dot(x, own_features, preferred_element_type=f32).astype(bf16)

    send, x, normed = project(where, x, vecs, attn_weights, True, dp_count)
    oth = other_core(send)
    own = project(where, normed, vecs, attn_weights, False, dp_count)
    ctx_own0, ctx_send0, lse0 = attn_fwd(table, own, oth, segment_lanes, blocks, 0)
    ctx_oth0 = other_core(ctx_send0)
    ctx_own1, ctx_send1, lse1 = attn_fwd(table, own, oth, segment_lanes, blocks, 1)
    ctx_oth1 = other_core(ctx_send1)
    cot = exchange(cot_half)
    resid, normed_two = out_project(
        where, x, (ctx_own0, ctx_own1, ctx_oth0, ctx_oth1), attn_weights, vecs, dp_count
    )
    if not aligned:
        normed_two = jnp.dot(normed_two, own_features.T, preferred_element_type=f32).astype(bf16)
    ffn0, gn0, pair0, bias0 = feed_forward(
        where, normed_two, cot, pair_weights, up_shift, 2
    )

    def reduce_rows(total):
        flat = total.reshape(-1, total.shape[-1])
        result = lax.psum_scatter(flat, "dp", scatter_dimension=0, tiled=True)
        return result.reshape(total.shape[1:])

    ffn1, gn1, pair1, bias1 = feed_forward(
        where, normed_two, cot, pair_weights, up_shift, 0
    )
    pair_total0 = reduce_rows(pair0)
    pair_total1 = reduce_rows(pair1)
    grad_bias = jnp.concatenate([bias1, bias0])
    ffn, grad_two = (ffn0, ffn1), (gn0, gn1)
    if not aligned:
        reorder = lambda v: jnp.dot(v, own_features, preferred_element_type=f32).astype(bf16)
        ffn, grad_two, cot = map(reorder, ffn), map(reorder, grad_two), reorder(cot)

    def reduce_core(own_half, other_half):
        theirs = other_core(other_half)
        size = own_half.shape[-2] // pairs
        return [
            (
                own_half[..., r * size : (r + 1) * size, :].astype(f32)
                + theirs[..., r * size : (r + 1) * size, :].astype(f32)
            ).astype(own_half.dtype)
            for r in range(pairs)
        ]

    def add_parts(first, others):
        total = first.astype(f32)
        for part in others:
            total = total + part.astype(f32)
        return total.astype(first.dtype)

    def reduce_across(parts):
        return add_parts(parts[0], [across(parts[r], r) for r in range(1, pairs)])

    piece = width // devices

    def exchange_sums(sums_one, sums_two, grad_bias):
        five = jnp.concatenate([sums_one[:2], sums_two[:3]]).reshape(5, dp_count, chunk)
        relative = places ^ d
        back = (relative % 2) * pairs + relative // 2
        five = jnp.take(five, back, axis=1).reshape(5, devices, piece).transpose(1, 0, 2)
        shift = jnp.roll(grad_bias, z, axis=0)
        shift = shift.reshape(tensor_count, dp_count, -1).transpose(1, 0, 2)
        sums = jnp.concatenate([five.reshape(devices, -1), shift.reshape(devices, -1)], axis=1)
        return lax.all_to_all(sums, BOTH, split_axis=0, concat_axis=0, tiled=True)

    def reduce_along(total, slots):
        return sum(
            (along(total[i], k) if k else total[i]).astype(f32) for i, k in enumerate(slots)
        )

    *out, grad_resid, low, gctx_own, gctx_send, sums_two = middle(
        where, resid, tuple(ffn), tuple(grad_two), cot, attn_weights, vecs, dp_count
    )
    gctx_oth = other_core(gctx_send)
    out_back = [None] * tensor_count

    def give(piece, turn):
        return lax.ppermute(piece, BOTH, token_routes(dp_count, tensor_count, turn))

    out_back[0], out_back[2] = give(out[0], 0), give(out[2], 2)
    d_own0, d_send0 = attn_bwd(
        table, own, oth, gctx_own, gctx_oth, segment_lanes, lse0, blocks, 0
    )
    d_send0, out_back[0], out_back[2] = lax.optimization_barrier(
        (d_send0, out_back[0], out_back[2])
    )
    d_oth0 = other_core(d_send0)
    total_one, ga0, gb0, *turned = back_early(
        where, normed, low, (d_own0, d_oth0), (ctx_own0, ctx_oth0), attn_weights, 0
    )
    out[1], out[3], d_oth0 = lax.optimization_barrier((out[1], out[3], d_oth0))
    out_back[1], out_back[3] = give(out[1], 1), give(out[3], 3)
    ga0, gb0, out_back = lax.optimization_barrier((ga0, gb0, out_back))
    attn_parts0 = reduce_core(ga0, gb0)
    lse1, attn_parts0 = lax.optimization_barrier((lse1, attn_parts0))
    d_own1, d_send1 = attn_bwd(
        table, own, oth, gctx_own, gctx_oth, segment_lanes, lse1, blocks, 1
    )
    attn_total0 = reduce_across(attn_parts0)
    pair_next = [along(pair_total0[0], 2), along(pair_total0[1], 3)]
    d_send1, attn_total0, pair_next = lax.optimization_barrier((d_send1, attn_total0, pair_next))
    d_oth1 = other_core(d_send1)
    pair_next.append(along(pair_total1[1], 1))
    *grad_in, sums_one = back_tokens(
        where, (d_own1, d_oth1), attn_weights, 1, total_one, x, grad_resid, vecs
    )
    grad_in, out_back, turned = lax.optimization_barrier((grad_in, out_back, turned))
    grad_back = [give(piece, turn) for turn, piece in enumerate(grad_in)]
    ga1, gb1 = back_weights(where, (d_own1, d_oth1), (ctx_own1, ctx_oth1), turned)
    ga1, gb1, pair_next = lax.optimization_barrier((ga1, gb1, pair_next))
    attn_parts1 = reduce_core(ga1, gb1)
    sums_one, attn_parts1 = lax.optimization_barrier((sums_one, attn_parts1))
    sums = exchange_sums(sums_one, sums_two, grad_bias)
    attn_come1 = [across(attn_parts1[r], r) for r in range(1, pairs)]
    attn_total1 = add_parts(attn_parts1[0], attn_come1)
    block_out = restore_direct(where, out_back, dp_count, bf16).reshape(batches, local, width)
    g_attn = reduce_along(attn_total0, (0, 2)) + reduce_along(attn_total1, (1, 3))
    g_up, g_down = unpack_pair(pair_total1[0], *pair_next)
    grad_in = restore_direct(where, grad_back, dp_count, f32).reshape(batches, local, width)

    sums = jnp.sum(sums, axis=0)
    vector_grads = [sums[i * piece : (i + 1) * piece] for i in range(5)]
    quarter = width // 4
    return (
        block_out, grad_in, vector_grads[0], vector_grads[1],
        g_attn[:, :quarter], g_attn[:, quarter : 2 * quarter], g_attn[:, 2 * quarter : 3 * quarter],
        g_attn[:, 3 * quarter :].T, vector_grads[2], vector_grads[3],
        g_up, sums[5 * piece :][None], g_down, vector_grads[4],
    )


def solution(mesh):
    rows, both = P(None, BOTH, None), P(BOTH)
    dp, split, turned = P("dp"), P("dp", "tensor"), P("tensor", "dp")
    return jax.shard_map(
        per_device,
        mesh=mesh,
        in_specs=(
            rows, dp, dp, split, split, split, turned, dp, dp, split, turned, turned, dp,
            P(None, "dp"), P(None, "dp", "tensor", None, None), P(None, "dp", None), rows,
        ),
        out_specs=(
            rows, rows, both, both, split, split, split, turned, both, both, split, turned, turned,
            both,
        ),
        check_vma=False,
    )
```

```python
import functools
import jax
import jax.numpy as jnp
from jax import lax
from jax.sharding import PartitionSpec as P
from jax.experimental import pallas as pl
from jax.experimental.pallas import tpu as pltpu

HD = 64
BLOCK = 64
COMMON = 5
RAND = 3
BIG = 1e30
bf16 = jnp.bfloat16
f32 = jnp.float32


def cost(micros):
    return pl.CostEstimate(flops=int(micros * 10**9), bytes_accessed=1000, transcendentals=0)


def dot_nt(left, right):
    return lax.dot_general(left, right, (((1,), (1,)), ((), ())), preferred_element_type=f32)


def dot_tn(left, right):
    return lax.dot_general(left, right, (((0,), (0,)), ((), ())), preferred_element_type=f32)


def dot_nn(left, right):
    return lax.dot_general(left, right, (((1,), (0,)), ((), ())), preferred_element_type=f32)


def low_half(shape):
    return lax.broadcasted_iota(jnp.int32, shape, 1) % 128 < HD


def slot_offsets(tab, layout, pair, block):
    common_at, rand_at, blocks, heads = layout
    shared = [
        pl.multiple_of(tab[common_at + block * COMMON + slot], BLOCK) for slot in range(COMMON)
    ]
    first = rand_at + (2 * pair * blocks + block) * RAND
    second = first + blocks * RAND
    drawn = [
        (pl.multiple_of(tab[first + slot], BLOCK), pl.multiple_of(tab[second + slot], BLOCK))
        for slot in range(RAND)
    ]
    return shared, drawn


def gather_rows(ref, shared, drawn, width):
    keep = low_half((BLOCK, width))
    parts = [ref[pl.ds(start, BLOCK), :width] for start in shared]
    for left, right in drawn:
        parts.append(
            jnp.where(keep, ref[pl.ds(left, BLOCK), :width], ref[pl.ds(right, BLOCK), :width])
        )
    return jnp.concatenate(parts, axis=0)


def block_diag(rows):
    keep = low_half(rows.shape)
    zero = jnp.zeros_like(rows)
    return jnp.concatenate([jnp.where(keep, rows, zero), jnp.where(keep, zero, rows)], axis=0)


def fold_heads(rows):
    keep = low_half((BLOCK, 128))
    return jnp.where(keep, rows[:BLOCK], rows[BLOCK:])


def query_rows(qbuf, kaug, start):
    scaled = qbuf[pl.ds(start, BLOCK), :]
    hot = kaug[pl.ds(start, BLOCK), 128:]
    penalty = (hot - jnp.ones_like(hot)) * jnp.asarray(BIG, bf16)
    return block_diag(jnp.concatenate([scaled, penalty], axis=1))


def fill_keys(tab, layout, seg_ref, kaug, half, k_own, k_oth):
    blocks = layout[2]

    @pl.when(pl.program_id(0) == 0)
    def _():
        lane = lax.broadcasted_iota(jnp.int32, (BLOCK, 128), 1) % HD

        def one(block, carry):
            row = pl.multiple_of(tab[block], BLOCK)
            seg = seg_ref[pl.ds(pl.multiple_of(block * BLOCK, BLOCK), BLOCK), :]
            kaug[pl.ds(row, BLOCK), 128:] = jnp.where(seg == lane, 1.0, 0.0).astype(bf16)
            return carry

        lax.fori_loop(0, blocks, one, 0)
        kaug[2 * half :, :128] = jnp.zeros((BLOCK, 128), bf16)
        kaug[2 * half :, 128:] = jnp.where(lane == HD - 1, 1.0, 0.0).astype(bf16)

    kaug[:half, :128] = k_own[0]
    kaug[half : 2 * half, :128] = k_oth[0]


def attn_fwd_kernel(
    layout, first_pair, unroll, tab, q_own, q_oth, k_own, k_oth, v_own, v_oth, seg_ref,
    out_own, out_oth, lse_ref, kaug, vbuf, qbuf, obuf, sbuf,
):
    pair = first_pair + pl.program_id(0)
    half = q_own.shape[1]
    blocks = layout[2]
    fill_keys(tab, layout, seg_ref, kaug, half, k_own, k_oth)
    vbuf[:half, :] = v_own[0]
    vbuf[half : 2 * half, :] = v_oth[0]
    vbuf[2 * half :, :] = jnp.zeros((BLOCK, 128), bf16)
    scale = jnp.asarray(0.125, bf16)
    qbuf[:half, :] = q_own[0] * scale
    qbuf[half:, :] = q_oth[0] * scale

    def step(index, carry):
        group = [index * unroll + part for part in range(unroll)]
        rows = [pl.multiple_of(tab[block], BLOCK) for block in group]
        slots = [slot_offsets(tab, layout, pair, block) for block in group]
        scores = [
            dot_nt(gather_rows(kaug, *slot, 256), query_rows(qbuf, kaug, row))
            for slot, row in zip(slots, rows)
        ]
        top = [jnp.max(score, axis=0, keepdims=True) for score in scores]
        weight = [jnp.exp(score - most) for score, most in zip(scores, top)]
        total = [jnp.sum(part, axis=0, keepdims=True) for part in weight]
        probs = [(part * (1.0 / whole)).astype(bf16) for part, whole in zip(weight, total)]
        context = [
            dot_tn(prob, gather_rows(vbuf, *slot, 128)) for prob, slot in zip(probs, slots)
        ]
        for block, row, part, most, whole in zip(group, rows, context, top, total):
            obuf[pl.ds(row, BLOCK), :] = fold_heads(part).astype(bf16)
            lse_ref[0, pl.ds(block, 1), :] = most + jnp.log(whole)
        return carry

    lax.fori_loop(0, blocks // unroll, step, 0)

    first, second = tab[blocks], tab[blocks + 1]
    rows = [pl.multiple_of(tab[block], BLOCK) for block in (first, second)]
    query = jnp.concatenate([query_rows(qbuf, kaug, row) for row in rows], axis=0)
    chunk = 512
    pieces = [slice(at, at + chunk) for at in range(0, 2 * half, chunk)]
    top = jnp.full((1, 256), -3e38, f32)
    for here in pieces:
        scores = dot_nt(kaug[here, :], query)
        sbuf[here, :] = scores
        top = jnp.maximum(top, jnp.max(scores, axis=0, keepdims=True))
    total = jnp.zeros((1, 256), f32)
    for here in pieces:
        weight = jnp.exp(sbuf[here, :] - top)
        sbuf[here, :] = weight
        total = total + jnp.sum(weight, axis=0, keepdims=True)
    inverse = 1.0 / total
    context = jnp.zeros((256, 128), f32)
    for here in pieces:
        context = context + dot_tn((sbuf[here, :] * inverse).astype(bf16), vbuf[here, :])
    lse = top + jnp.log(total)
    for index, (block, row) in enumerate(zip((first, second), rows)):
        lanes = slice(index * 128, (index + 1) * 128)
        obuf[pl.ds(row, BLOCK), :] = fold_heads(context[lanes]).astype(bf16)
        lse_ref[0, pl.ds(block, 1), :] = lse[:, lanes]
    out_own[0] = obuf[:half, :]
    out_oth[0] = obuf[half:, :]


def attn_bwd_kernel(
    layout, first_pair, unroll, tab, q_own, q_oth, k_own, k_oth, v_own, v_oth, g_own, g_oth, seg_ref, lse_ref,
    own_ref, oth_ref,
    kaug, vbuf, qbuf, gbuf, dqbuf, dkbuf, dvbuf, sbuf, tbuf,
):
    pair = first_pair + pl.program_id(0)
    half = q_own.shape[1]
    blocks = layout[2]
    fill_keys(tab, layout, seg_ref, kaug, half, k_own, k_oth)
    vbuf[:half, :] = v_own[0]
    vbuf[half : 2 * half, :] = v_oth[0]
    vbuf[2 * half :, :] = jnp.zeros((BLOCK, 128), bf16)
    scale = jnp.asarray(0.125, bf16)
    qbuf[:half, :] = q_own[0] * scale
    qbuf[half:, :] = q_oth[0] * scale
    gbuf[:half, :] = g_own[0]
    gbuf[half:, :] = g_oth[0]
    dkbuf[...] = jnp.zeros_like(dkbuf)
    dvbuf[...] = jnp.zeros_like(dvbuf)
    keep = low_half((BLOCK, 128))

    dummy = 2 * half
    ends = [pl.multiple_of(tab[tab_block], BLOCK) for tab_block in (tab[blocks], tab[blocks + 1])]

    def scatter(ref, updates, slots, base):
        piece = lambda part, slot: updates[part][slot * BLOCK : (slot + 1) * BLOCK]
        for shift in range(-1, unroll + 1):
            block = base + shift
            inside = (block >= 0) & (block < blocks)
            row = jnp.where(inside, tab[jnp.clip(block, 0, blocks - 1)], dummy)
            near = [piece(p, shift - p + 1) for p in range(unroll) if 0 <= shift - p + 1 <= 2]
            ref[pl.ds(pl.multiple_of(row, BLOCK), BLOCK), :] += functools.reduce(jnp.add, near)
        for slot, row in zip((3, 4), ends):
            every = [piece(p, slot) for p in range(unroll)]
            ref[pl.ds(row, BLOCK), :] += functools.reduce(jnp.add, every)
        for part, (_, drawn) in enumerate(slots):
            for slot, (left, right) in enumerate(drawn):
                one = piece(part, COMMON + slot)
                ref[pl.ds(left, BLOCK), :] += jnp.where(keep, one, 0.0)
                ref[pl.ds(right, BLOCK), :] += jnp.where(keep, 0.0, one)

    def step(index, carry):
        group = [index * unroll + part for part in range(unroll)]
        rows = [pl.multiple_of(tab[block], BLOCK) for block in group]
        slots = [slot_offsets(tab, layout, pair, block) for block in group]
        query = [query_rows(qbuf, kaug, row) for row in rows]
        grad = [block_diag(gbuf[pl.ds(row, BLOCK), :]) for row in rows]
        keys = [gather_rows(kaug, *slot, 256) for slot in slots]
        scores = [dot_nt(key, one) for key, one in zip(keys, query)]
        grad_probs = [
            dot_nt(gather_rows(vbuf, *slot, 128), one) for slot, one in zip(slots, grad)
        ]
        probs = [
            jnp.exp(score - lse_ref[0, pl.ds(block, 1), :]) for score, block in zip(scores, group)
        ]
        delta = [jnp.sum(p * g, axis=0, keepdims=True) for p, g in zip(probs, grad_probs)]
        grad_scores = [
            (p * (g - one)).astype(bf16) for p, g, one in zip(probs, grad_probs, delta)
        ]
        grad_query = [dot_tn(one, key[:, :128]) for one, key in zip(grad_scores, keys)]
        grad_key = [dot_nn(one, q[:, :128]) for one, q in zip(grad_scores, query)]
        grad_value = [dot_nn(p.astype(bf16), g) for p, g in zip(probs, grad)]
        for row, one in zip(rows, grad_query):
            dqbuf[pl.ds(row, BLOCK), :] = (fold_heads(one) * 0.125).astype(bf16)
        scatter(dkbuf, grad_key, slots, index * unroll)
        scatter(dvbuf, grad_value, slots, index * unroll)
        return carry

    lax.fori_loop(0, blocks // unroll, step, 0)

    first, second = tab[blocks], tab[blocks + 1]
    rows = [pl.multiple_of(tab[block], BLOCK) for block in (first, second)]
    query = jnp.concatenate([query_rows(qbuf, kaug, row) for row in rows], axis=0)
    grads = [block_diag(gbuf[pl.ds(row, BLOCK), :]) for row in rows]
    grads[1] = jnp.where(first == second, jnp.zeros_like(grads[1]), grads[1])
    grad = jnp.concatenate(grads, axis=0)
    lse = jnp.concatenate([lse_ref[0, pl.ds(block, 1), :] for block in (first, second)], axis=1)
    chunk = 512
    pieces = [slice(at, at + chunk) for at in range(0, 2 * half, chunk)]
    delta = jnp.zeros((1, 256), f32)
    for here in pieces:
        probs = jnp.exp(dot_nt(kaug[here, :], query) - lse)
        grad_probs = dot_nt(vbuf[here, :], grad)
        delta = delta + jnp.sum(probs * grad_probs, axis=0, keepdims=True)
        sbuf[here, :] = probs
        tbuf[here, :] = grad_probs
    grad_query = jnp.zeros((256, 128), f32)
    for here in pieces:
        probs = sbuf[here, :]
        grad_scores = (probs * (tbuf[here, :] - delta)).astype(bf16)
        grad_query = grad_query + dot_tn(grad_scores, kaug[here, :128])
        dkbuf[here, :] += dot_nn(grad_scores, query[:, :128])
        dvbuf[here, :] += dot_nn(probs.astype(bf16), grad)
    for index in (1, 0):
        part = fold_heads(grad_query[index * 128 : (index + 1) * 128]) * 0.125
        dqbuf[pl.ds(rows[index], BLOCK), :] = part.astype(bf16)
    for part, buffer in enumerate((dqbuf, dkbuf, dvbuf)):
        lanes = pl.ds(pl.multiple_of((2 * part + pl.program_id(0)) * 128, 128), 128)
        own_ref[0, :, lanes] = buffer[:half, :].astype(bf16)
        oth_ref[0, :, lanes] = buffer[half : 2 * half, :].astype(bf16)


def table_layout(blocks, heads):
    common_at = blocks + 2
    rand_at = common_at + blocks * COMMON
    return (common_at, rand_at, blocks, heads)


def attention_table(rand_heads, glob_row, row_of, dummy_row):
    heads, blocks, _ = rand_heads.shape
    index = jnp.arange(blocks, dtype=jnp.int32)
    g0, g1 = glob_row[0], glob_row[1]
    dense = (index == g0) | (index == g1)
    near0, near1 = jnp.abs(index - g0) <= 1, jnp.abs(index - g1) <= 1
    full = jnp.broadcast_to
    shared = jnp.stack([index - 1, index, index + 1, full(g0, (blocks,)), full(g1, (blocks,))], axis=1)
    valid = jnp.stack(
        [index > 0, index >= 0, index < blocks - 1, ~near0, ~near1 & (g1 != g0)], axis=1
    ) & ~dense[:, None]
    shared = jnp.where(valid, row_of(jnp.clip(shared, 0, blocks - 1)), dummy_row)
    far = jnp.abs(rand_heads - index[None, :, None]) > 1
    far = far & (rand_heads != g0) & (rand_heads != g1) & ~dense[None, :, None]
    r0, r1, r2 = rand_heads[..., 0], rand_heads[..., 1], rand_heads[..., 2]
    fresh = jnp.stack([r0 == r0, r1 != r0, (r2 != r0) & (r2 != r1)], axis=-1)
    drawn = jnp.where(far & fresh, row_of(rand_heads), dummy_row)
    return jnp.concatenate(
        [row_of(index), glob_row, shared.reshape(-1), drawn.reshape(-1)]
    ).astype(jnp.int32)


def lane_spec(half, slot, column):
    return pl.BlockSpec((1, half, 128), lambda p, tab: (slot, 0, column * 2 + p))


def attn_fwd(tab, qkv_own, qkv_oth, seg_abs, blocks, slot, unroll=8):
    half = qkv_own.shape[1]
    layout = table_layout(blocks, 4 * qkv_own.shape[0])
    rows = 2 * half + BLOCK
    shape = jax.ShapeDtypeStruct((1, half, 256), bf16)
    result = pl.BlockSpec((1, half, 128), lambda p, tab: (0, 0, p))
    return pl.pallas_call(
        functools.partial(attn_fwd_kernel, layout, 2 * slot, unroll),
        out_shape=(shape, shape, jax.ShapeDtypeStruct((2, blocks, 128), f32)),
        grid_spec=pltpu.PrefetchScalarGridSpec(
            num_scalar_prefetch=1,
            grid=(2,),
            in_specs=[
                *[lane_spec(half, slot, column) for column in (0, 0, 1, 1, 2, 2)],
                pl.BlockSpec((2 * half, 128), lambda p, tab: (0, 0)),
            ],
            out_specs=(result, result, pl.BlockSpec((1, blocks, 128), lambda p, tab: (p, 0, 0))),
            scratch_shapes=[
                pltpu.VMEM((rows, 256), bf16), pltpu.VMEM((rows, 128), bf16),
                pltpu.VMEM((2 * half, 128), bf16), pltpu.VMEM((2 * half, 128), bf16),
                pltpu.VMEM((2 * half, 256), f32),
            ],
        ),
        compiler_params=pltpu.CompilerParams(vmem_limit_bytes=60 << 20),
        cost_estimate=cost(17),
        name="attn_fwd",
    )(tab, qkv_own, qkv_oth, qkv_own, qkv_oth, qkv_own, qkv_oth, seg_abs)


def attn_bwd(tab, qkv_own, qkv_oth, grad_own, grad_oth, seg_abs, lse, blocks, slot, unroll=8):
    half = qkv_own.shape[1]
    layout = table_layout(blocks, 4 * qkv_own.shape[0])
    rows = 2 * half + BLOCK
    shape = jax.ShapeDtypeStruct((1, half, 768), bf16)
    result = pl.BlockSpec((1, half, 768), lambda p, tab: (0, 0, 0))
    return pl.pallas_call(
        functools.partial(attn_bwd_kernel, layout, 2 * slot, unroll),
        out_shape=(shape, shape),
        grid_spec=pltpu.PrefetchScalarGridSpec(
            num_scalar_prefetch=1,
            grid=(2,),
            in_specs=[
                *[lane_spec(half, slot, column) for column in (0, 0, 1, 1, 2, 2, 0, 0)],
                pl.BlockSpec((2 * half, 128), lambda p, tab: (0, 0)),
                pl.BlockSpec((1, blocks, 128), lambda p, tab: (p, 0, 0)),
            ],
            out_specs=(result, result),
            scratch_shapes=[
                pltpu.VMEM((rows, 256), bf16), pltpu.VMEM((rows, 128), bf16),
                pltpu.VMEM((2 * half, 128), bf16), pltpu.VMEM((2 * half, 128), bf16),
                pltpu.VMEM((2 * half, 128), bf16),
                pltpu.VMEM((rows, 128), f32), pltpu.VMEM((rows, 128), f32),
                pltpu.VMEM((2 * half, 256), f32), pltpu.VMEM((2 * half, 256), f32),
            ],
        ),
        compiler_params=pltpu.CompilerParams(vmem_limit_bytes=60 << 20),
        cost_estimate=cost(29),
        name="attn_bwd",
    )(tab, qkv_own, qkv_oth, qkv_own, qkv_oth, qkv_own, qkv_oth, grad_own, grad_oth, seg_abs, lse)


EPS = 1e-05
BOTH = ("dp", "tensor")
ROWS = 256
WIDE = 512


def gelu_pair(u):
    c = 0.7978845608028654
    square = u * u
    bend = jnp.tanh(u * (c + (c * 0.044715) * square))
    half = 0.5 * (1.0 + bend)
    slope = half + (0.5 * u) * (1.0 - bend * bend) * (c + (3.0 * c * 0.044715) * square)
    return u * half, slope


def normalise(rows):
    center = rows - jnp.mean(rows, axis=-1, keepdims=True)
    inverse = lax.rsqrt(jnp.mean(center * center, axis=-1, keepdims=True) + EPS)
    return center * inverse, inverse


def norm_back(grad, unit, inverse, gain):
    scaled = grad * gain
    mean = jnp.mean(scaled, axis=-1, keepdims=True)
    along = jnp.mean(scaled * unit, axis=-1, keepdims=True)
    return inverse * (scaled - mean - unit * along)


def params(mib):
    return pltpu.CompilerParams(vmem_limit_bytes=mib << 20)


def prefetch(grid, in_specs, out_specs, scratch=()):
    return pltpu.PrefetchScalarGridSpec(
        num_scalar_prefetch=1, grid=grid, in_specs=in_specs, out_specs=out_specs,
        scratch_shapes=list(scratch),
    )


def struct(shape, dtype):
    return jax.ShapeDtypeStruct(shape, dtype)


def nn_halves(rows, low_ref, high_ref):
    split = rows.shape[1] // 2
    return dot_nn(rows[:, :split], low_ref) + dot_nn(rows[:, split:], high_ref)


def nt_halves(rows, low_ref, high_ref):
    return jnp.concatenate([dot_nt(rows, low_ref), dot_nt(rows, high_ref)], axis=1)


def chunk_at(d, place, count):
    return d ^ (2 * (place % (count // 2)) + place // (count // 2))


def restore_direct_kernel(count, where, p0, p1, p2, p3, out_ref):
    width = p0.shape[1]
    chunk = width // count
    core, d, z = where[0], where[1], where[2]
    for turn, piece in enumerate((p0, p1, p2, p3)):
        index = z ^ turn
        sender = d - core + index % 2
        for place in range(count):
            target = pl.ds(pl.multiple_of(chunk_at(sender, place, count) * chunk, chunk), chunk)
            out_ref[index, :, target] = piece[:, place * chunk : (place + 1) * chunk].astype(
                out_ref.dtype
            )


def chunk_matrix(d, width, count):
    chunk = width // count
    index = jnp.arange(width, dtype=jnp.int32)
    source = chunk_at(d, index // chunk, count) * chunk + index % chunk
    return (index[:, None] == source[None, :]).astype(bf16)


def scatter_chunks(where, ref, rows, count):
    chunk = rows.shape[1] // count
    if chunk % 128:
        ref[...] = rows
        return
    for place in range(count):
        target = pl.ds(pl.multiple_of(chunk_at(where[1], place, count) * chunk, chunk), chunk)
        ref[:, target] = rows[:, place * chunk : (place + 1) * chunk]


def gather_chunks(where, ref, count):
    chunk = ref.shape[1] // count
    if chunk % 128:
        return ref[...]
    return jnp.concatenate(
        [
            ref[:, pl.ds(pl.multiple_of(chunk_at(where[1], place, count) * chunk, chunk), chunk)]
            for place in range(count)
        ],
        axis=1,
    )


def project_kernel(count, where, x_ref, vec_ref, wa_ref, wb_ref, out_ref, rel_ref, n_ref, nbuf):
    slot, tile = pl.program_id(0), pl.program_id(1)
    here = pl.ds(pl.multiple_of(tile * WIDE, WIDE), WIDE)

    @pl.when(slot == 0)
    def _():
        rows = gather_chunks(where, x_ref, count)
        rel_ref[...] = rows
        unit, _ = normalise(rows.astype(f32))
        normed = (unit * vec_ref[0:1, :] + vec_ref[1:2, :]).astype(bf16)
        nbuf[here, :] = normed
        n_ref[...] = normed

    out_ref[0] = nn_halves(nbuf[here, :], wa_ref[0], wb_ref[0]).astype(bf16)


def project_more_kernel(where, n_ref, wa_ref, wb_ref, out_ref):
    out_ref[0] = nn_halves(n_ref[...], wa_ref[0], wb_ref[0]).astype(bf16)


def project(where, x, vecs, weights, first, count):
    rows, width = x.shape
    tiles = rows // WIDE
    out = width * 3 // 4
    half = width // 2
    weight = pl.BlockSpec(
        (1, half, out), lambda s, i, w: (2 * (1 - w[0] if first else w[0]) + s, 0, 0)
    )
    outs = pl.BlockSpec((1, WIDE, out), lambda s, i, w: (s, i, 0))
    once = pl.BlockSpec((WIDE, width), lambda s, i, w: (jnp.where(s == 0, i, tiles - 1), 0))
    shape = struct((2, rows, out), bf16)
    if first:
        return pl.pallas_call(
            functools.partial(project_kernel, count),
            out_shape=(shape, struct((rows, width), bf16), struct((rows, width), bf16)),
            grid_spec=prefetch(
                (2, tiles),
                [once, pl.BlockSpec(vecs.shape, lambda s, i, w: (0, 0)), weight, weight],
                (outs, once, once),
                [pltpu.VMEM((rows, width), bf16)],
            ),
            compiler_params=params(32),
            cost_estimate=cost(9),
            name="project",
        )(where, x, vecs, *weights)
    return pl.pallas_call(
        project_more_kernel,
        out_shape=shape,
        grid_spec=prefetch(
            (2, tiles),
            [pl.BlockSpec((WIDE, width), lambda s, i, w: (i, 0)), weight, weight],
            outs,
        ),
        compiler_params=params(32),
        cost_estimate=cost(8),
        name="project_more",
    )(where, x, *weights)


def out_kernel(count, where, x_ref, c0, c1, c2, c3, a0, a1, a2, a3, b0, b1, b2, b3, vec_ref,
               resid_ref, n_ref):
    total = x_ref[...].astype(f32)
    for part, low, high in ((c0, a0, b0), (c1, a1, b1), (c2, a2, b2), (c3, a3, b3)):
        total = total + nt_halves(part[0], low[0], high[0])
    resid_ref[...] = total
    unit, _ = normalise(total)
    scatter_chunks(where, n_ref, (unit * vec_ref[2:3, :] + vec_ref[3:4, :]).astype(bf16), count)


def out_weight_specs(width):
    return [
        pl.BlockSpec((1, width // 2, width // 4), lambda i, w, s=s: ((2 * w[0] + s) % 4, 0, 3))
        for s in range(4)
    ]


def out_project(where, x, contexts, weights, vecs, count):
    rows, width = x.shape
    tile = pl.BlockSpec((ROWS, width), lambda i, w: (i, 0))
    part = pl.BlockSpec((1, ROWS, width // 4), lambda i, w: (0, i, 0))
    return pl.pallas_call(
        functools.partial(out_kernel, count),
        out_shape=(struct((rows, width), f32), struct((rows, width), bf16)),
        grid_spec=prefetch(
            (rows // ROWS,),
            [tile, *[part] * 4, *out_weight_specs(width) * 2,
             pl.BlockSpec(vecs.shape, lambda i, w: (0, 0))],
            (tile, tile),
        ),
        compiler_params=params(60),
        cost_estimate=cost(7),
        name="out_project",
    )(where, x, *contexts, *[weights[0]] * 4, *[weights[1]] * 4, vecs)


def ffn_kernel(where, n_ref, cot_ref, up_ref, down_ref, bias_ref,
               ffn_ref, gn_ref, grad_ref, gbias_ref, nt, ct, act, gup, total, back_total):
    step = pl.program_id(0)
    rows, width = n_ref.shape
    hidden = act.shape[1]
    up = up_ref[...].reshape(width, hidden)
    down = down_ref[...].reshape(width, hidden)

    @pl.when(step == 0)
    def _():
        turn_rows(n_ref, nt)
        turn_rows(cot_ref, ct)
        total[...] = jnp.zeros_like(total)
        back_total[...] = jnp.zeros_like(back_total)

    value = dot_nn(n_ref[...], up) + bias_ref[0]
    out, slope = gelu_pair(value)
    out = out.astype(bf16)
    act[...] = out
    back = (dot_nn(cot_ref[...], down) * slope).astype(bf16)
    gup[...] = back
    gbias_ref[0] = jnp.sum(back.astype(f32), axis=0, keepdims=True)
    total[...] += dot_nt(out, down)
    back_total[...] += dot_nt(back, up)
    shape = grad_ref.shape[0], grad_ref.shape[3], hidden
    grad_ref[:, 0, 0] = dot_nn(nt[...], gup[...]).astype(bf16).reshape(shape)
    grad_ref[:, 0, 1] = dot_nn(ct[...], act[...]).astype(bf16).reshape(shape)

    @pl.when(step == pl.num_programs(0) - 1)
    def _():
        ffn_ref[...] = total[...].astype(bf16)
        gn_ref[...] = back_total[...].astype(bf16)


def feed_forward(where, normed, cot, weights, bias, slots_at):
    rows, width = normed.shape
    count, slots, _, chunk, hidden = weights.shape
    whole = fixed_spec((rows, width))
    slot = lambda s, w: (w[2] + slots_at + s) % slots
    weight = lambda k: pl.BlockSpec(
        (count, 1, 1, chunk, hidden), lambda s, w: (0, slot(s, w), k, 0, 0)
    )
    total = pl.BlockSpec((rows, width), lambda s, w: (0, 0))
    return pl.pallas_call(
        ffn_kernel,
        out_shape=(
            struct((rows, width), bf16), struct((rows, width), bf16),
            struct((count, 2, 2, chunk, hidden), bf16), struct((2, 1, hidden), f32),
        ),
        grid_spec=prefetch(
            (2,),
            [whole, whole, weight(0), weight(1),
             pl.BlockSpec((1, 1, hidden), lambda s, w: (slot(s, w), 0, 0))],
            (
                total, total,
                pl.BlockSpec((count, 1, 2, chunk, hidden), lambda s, w: (0, s, 0, 0, 0)),
                pl.BlockSpec((1, 1, hidden), lambda s, w: (s, 0, 0)),
            ),
            [
                pltpu.VMEM((width, rows), bf16), pltpu.VMEM((width, rows), bf16),
                pltpu.VMEM((rows, hidden), bf16), pltpu.VMEM((rows, hidden), bf16),
                pltpu.VMEM((rows, width), f32), pltpu.VMEM((rows, width), f32),
            ],
        ),
        compiler_params=params(60),
        cost_estimate=cost(38),
        name="feed_forward",
    )(where, normed, cot, weights, weights, bias)


def write_piece(where, tile, refs, rows):
    turn = tile ^ (where[2] // 2 * 2 + where[0])
    for index, ref in enumerate(refs):

        @pl.when(turn == index)
        def _(ref=ref):
            ref[...] = rows


def mid_kernel(count, where, resid_ref, f0_ref, f1_ref, n0_ref, n1_ref, cot_ref, a0, a1, a2, a3, b0, b1, b2, b3, vec_ref,
               o0, o1, o2, o3, gres_ref, low_ref, own_ref, send_ref, sums_ref):
    tile = pl.program_id(0)
    resid = resid_ref[...]
    cot = gather_chunks(where, cot_ref, count).astype(f32)
    result = resid + gather_chunks(where, f0_ref, count).astype(f32)
    result = result + gather_chunks(where, f1_ref, count).astype(f32)
    write_piece(where, tile, (o0, o1, o2, o3), (result + vec_ref[4:5, :]).astype(bf16))
    unit, inverse = normalise(resid)
    grad = gather_chunks(where, n0_ref, count).astype(f32)
    grad = grad + gather_chunks(where, n1_ref, count).astype(f32)
    gres = cot + norm_back(grad, unit, inverse, vec_ref[2:3, :])
    gres_ref[...] = gres
    low = gres.astype(bf16)
    low_ref[...] = low
    own_ref[0] = nn_halves(low, a0[0], b0[0]).astype(bf16)
    own_ref[1] = nn_halves(low, a1[0], b1[0]).astype(bf16)
    send_ref[0] = nn_halves(low, a2[0], b2[0]).astype(bf16)
    send_ref[1] = nn_halves(low, a3[0], b3[0]).astype(bf16)

    @pl.when(tile == 0)
    def _():
        sums_ref[...] = jnp.zeros_like(sums_ref)

    sums_ref[0:1, :] += jnp.sum(grad * unit, axis=0, keepdims=True)
    sums_ref[1:2, :] += jnp.sum(grad, axis=0, keepdims=True)
    sums_ref[2:3, :] += jnp.sum(cot, axis=0, keepdims=True)


def middle(where, resid, ffn, gn, cot, weights, vecs, count):
    rows, width = resid.shape
    tile = pl.BlockSpec((ROWS, width), lambda i, w: (i, 0))
    part = pl.BlockSpec((2, ROWS, width // 4), lambda i, w: (0, i, 0))
    piece = struct((2, rows, width // 4), bf16)
    return pl.pallas_call(
        functools.partial(mid_kernel, count),
        out_shape=(
            *[struct((ROWS, width), bf16)] * 4,
            struct((rows, width), f32), struct((rows, width), bf16),
            piece, piece, struct((8, width), f32),
        ),
        grid_spec=prefetch(
            (rows // ROWS,),
            [*[tile] * 6, *out_weight_specs(width) * 2,
             pl.BlockSpec(vecs.shape, lambda i, w: (0, 0))],
            (*[pl.BlockSpec((ROWS, width), lambda i, w: (0, 0))] * 4, tile, tile, part, part, pl.BlockSpec((8, width), lambda i, w: (0, 0))),
        ),
        compiler_params=params(60),
        cost_estimate=cost(12),
        name="middle",
    )(where, resid, *ffn, *gn, cot, *[weights[0]] * 4, *[weights[1]] * 4, vecs)


def token_part(inner, a_ref, b_ref, total):
    lanes = inner.shape[2]

    def tile(index, carry):
        here = pl.ds(pl.multiple_of(index * WIDE, WIDE), WIDE)
        total[here, :] += nt_halves(inner[0, here, :], a_ref[0, :, :lanes], b_ref[0, :, :lanes])
        return carry

    lax.fori_loop(0, total.shape[0] // WIDE, tile, 0)


def weight_part(nt, lt, inner, context, ga_ref, gb_ref):
    lanes = inner.shape[2]
    half = ga_ref.shape[1]
    for grad_ref, start in ((ga_ref, 0), (gb_ref, half)):

        def grads(index, carry, grad_ref=grad_ref, start=start):
            here = pl.ds(pl.multiple_of(index * WIDE, WIDE), WIDE)
            there = pl.ds(pl.multiple_of(start + index * WIDE, WIDE), WIDE)
            grad_ref[0, here, :lanes] = dot_nn(nt[there, :], inner[0]).astype(bf16)
            grad_ref[0, here, lanes:] = dot_nn(lt[there, :], context[0]).astype(bf16)
            return carry

        lax.fori_loop(0, half // WIDE, grads, 0)


def turn_rows(source, target):
    for at in range(0, source.shape[0], ROWS):
        target[:, at : at + ROWS] = source[at : at + ROWS, :].T


def back_early_kernel(where, d0, d1, a_ref, b_ref, n_ref, low_ref, c0, c1,
                      total_ref, ga_ref, gb_ref, nt_ref, lt_ref):
    step = pl.program_id(0)

    @pl.when(step == 0)
    def _():
        turn_rows(n_ref, nt_ref)
        turn_rows(low_ref, lt_ref)
        total_ref[...] = jnp.zeros_like(total_ref)
        token_part(d0, a_ref, b_ref, total_ref)
        weight_part(nt_ref, lt_ref, d0, c0, ga_ref, gb_ref)

    @pl.when(step == 1)
    def _():
        token_part(d1, a_ref, b_ref, total_ref)
        weight_part(nt_ref, lt_ref, d1, c1, ga_ref, gb_ref)


def back_tokens_kernel(where, d0, d1, a0, b0, a1, b1, before_ref, x_ref, gres_ref, vec_ref,
                       g0, g1, g2, g3, sums_ref):
    lanes = d0.shape[2]
    grad = before_ref[...] + nt_halves(d0[0], a0[0, :, :lanes], b0[0, :, :lanes])
    grad = grad + nt_halves(d1[0], a1[0, :, :lanes], b1[0, :, :lanes])
    unit, inverse = normalise(x_ref[...].astype(f32))
    result = gres_ref[...] + norm_back(grad, unit, inverse, vec_ref[0:1, :])
    result = result.astype(bf16)
    write_piece(where, pl.program_id(0), (g0, g1, g2, g3), result)

    @pl.when(pl.program_id(0) == 0)
    def _():
        sums_ref[...] = jnp.zeros_like(sums_ref)

    sums_ref[0:1, :] += jnp.sum(grad * unit, axis=0, keepdims=True)
    sums_ref[1:2, :] += jnp.sum(grad, axis=0, keepdims=True)


def back_weights_kernel(where, d0, d1, nt_ref, lt_ref, c0, c1, ga_ref, gb_ref):
    step = pl.program_id(0)

    @pl.when(step == 0)
    def _():
        weight_part(nt_ref, lt_ref, d0, c0, ga_ref, gb_ref)

    @pl.when(step == 1)
    def _():
        weight_part(nt_ref, lt_ref, d1, c1, ga_ref, gb_ref)


def side(s, w):
    return jnp.where(s == 0, w[0], 1 - w[0])


def fixed_spec(shape):
    return pl.BlockSpec(shape, lambda s, w: (0,) * len(shape), pipeline_mode=pl.Buffered(1))


def back_early(where, normed, low, grads, contexts, weights, part):
    rows, width = normed.shape
    whole, total = fixed_spec((rows, width)), pl.BlockSpec((rows, width), lambda s, w: (0, 0))
    inner, context = fixed_spec((1, rows, width * 3 // 4)), fixed_spec((1, rows, width // 4))
    weight = pl.BlockSpec((1, width // 2, width), lambda s, w: (2 * side(s, w) + part, 0, 0))
    grad = pl.BlockSpec((1, width // 2, width), lambda s, w: (side(s, w), 0, 0))
    shape = struct((2, width // 2, width), bf16)
    turned = struct((width, rows), bf16)
    return pl.pallas_call(
        back_early_kernel,
        out_shape=(struct((rows, width), f32), shape, shape, turned, turned),
        grid_spec=prefetch(
            (2,), [inner, inner, weight, weight, whole, whole, context, context],
            (total, grad, grad, total, total),
        ),
        compiler_params=params(60),
        cost_estimate=cost(19),
        name="back_early",
    )(where, *grads, *weights, normed, low, *contexts)


def back_tokens(where, grads, weights, part, before, x, gres, vecs):
    rows, width = x.shape
    tile = pl.BlockSpec((ROWS, width), lambda i, w: (i, 0))
    inner = pl.BlockSpec((1, ROWS, width * 3 // 4), lambda i, w: (0, i, 0))
    weight = lambda s: pl.BlockSpec(
        (1, width // 2, width), lambda i, w: (2 * side(s, w) + part, 0, 0)
    )
    return pl.pallas_call(
        back_tokens_kernel,
        out_shape=(*[struct((ROWS, width), bf16)] * 4, struct((8, width), f32)),
        grid_spec=prefetch(
            (rows // ROWS,),
            [inner, inner, weight(0), weight(0), weight(1), weight(1), tile, tile, tile,
             pl.BlockSpec(vecs.shape, lambda i, w: (0, 0))],
            (
                *[pl.BlockSpec((ROWS, width), lambda i, w: (0, 0))] * 4,
                pl.BlockSpec((8, width), lambda i, w: (0, 0)),
            ),
        ),
        compiler_params=params(60),
        cost_estimate=cost(11),
        name="back_tokens",
    )(where, *grads, *weights, *weights, before, x, gres, vecs)


def back_weights(where, grads, contexts, turned):
    width, rows = turned[0].shape
    inner, context = fixed_spec((1, rows, width * 3 // 4)), fixed_spec((1, rows, width // 4))
    grad = pl.BlockSpec((1, width // 2, width), lambda s, w: (side(s, w), 0, 0))
    shape = struct((2, width // 2, width), bf16)
    return pl.pallas_call(
        back_weights_kernel,
        out_shape=(shape, shape),
        grid_spec=prefetch(
            (2,), [inner, inner, *[fixed_spec((width, rows))] * 2, context, context], (grad, grad)
        ),
        compiler_params=params(60),
        cost_estimate=cost(10),
        name="back_weights",
    )(where, *grads, *turned, *contexts)


def restore_direct(where, pieces, count, dtype):
    rows, width = pieces[0].shape
    if (width // count) % 128:
        core, d, z = where[0], where[1], where[2]
        fixed = []
        for turn, piece in enumerate(pieces):
            matrix = chunk_matrix(d - core + (z ^ turn) % 2, width, count)
            fixed.append(jnp.dot(piece, matrix.T, preferred_element_type=f32).astype(dtype))
        fixed = jnp.stack(fixed)
        return jnp.stack([lax.dynamic_index_in_dim(fixed, z ^ i, 0, False) for i in range(4)])
    whole = lambda shape: pl.BlockSpec(shape, lambda i, w: (0,) * len(shape))
    return pl.pallas_call(
        functools.partial(restore_direct_kernel, count),
        out_shape=struct((4, rows, width), dtype),
        grid_spec=prefetch((1,), [whole((rows, width))] * 4, whole((4, rows, width))),
        compiler_params=params(24),
        cost_estimate=cost(4),
        name="restore_direct",
    )(where, *pieces)


def token_routes(dp_count, tensor_count, turn):
    routes = []
    for d in range(dp_count):
        for z in range(tensor_count):
            source = (2 * (z // 2) + d % 2) ^ turn
            routes.append((d * tensor_count + z, (d - d % 2 + z % 2) * tensor_count + source))
    return routes


def pack_kernel(*refs):
    *vectors, rand_ref, glob_ref, out_ref = refs
    lanes = out_ref.shape[2]
    out_ref[...] = jnp.zeros_like(out_ref)
    copies = out_ref.shape[0]
    spread = lambda row: jnp.broadcast_to(row.astype(f32)[None], (copies, *row.shape)).astype(bf16)
    for index, vector in enumerate(vectors):
        out_ref[:, index : index + 1, : vector.shape[1]] = spread(vector[...])
    start = 8
    out_ref[:, start : start + rand_ref.shape[0], :] = spread(rand_ref[...])
    start += rand_ref.shape[0]
    out_ref[:, start : start + 1, : glob_ref.shape[1]] = spread(glob_ref[...])


def pack(vectors, rand, glob, copies):
    rows = 8 + rand.shape[0] + 1
    rows = -(-rows // 16) * 16
    return pl.pallas_call(
        pack_kernel,
        out_shape=struct((copies, rows, rand.shape[1]), bf16),
        compiler_params=params(8),
        name="pack",
    )(*vectors, rand, glob)


def join_kernel(*refs):
    *pieces, out_ref = refs
    size = pieces[0].shape[1]
    for index, piece in enumerate(pieces):
        out_ref[0, index * size : (index + 1) * size, :] = piece[0]


def join(pieces):
    slots, size, width = pieces[0].shape
    rows = size * len(pieces)
    return pl.pallas_call(
        join_kernel,
        out_shape=struct((slots, rows, width), pieces[0].dtype),
        grid=(slots,),
        in_specs=[pl.BlockSpec((1, size, width), lambda s: (s, 0, 0))] * len(pieces),
        out_specs=pl.BlockSpec((1, rows, width), lambda s: (s, 0, 0)),
        compiler_params=params(16),
        cost_estimate=cost(4),
        name="join",
    )(*pieces)


def after(value, *others):
    return lax.optimization_barrier((value, others))[0]


def unpack_kernel(p0, p1, p2, p3, up_ref, down_ref):
    total = p0[...].astype(f32) + p1[...].astype(f32) + p2[...].astype(f32) + p3[...].astype(f32)
    up_ref[...] = total[0]
    down_ref[...] = total[1].T


def unpack_pair(*pairs):
    _, rows, width = pairs[0].shape
    return pl.pallas_call(
        unpack_kernel,
        out_shape=(struct((rows, width), f32), struct((width, rows), f32)),
        compiler_params=params(16),
        name="unpack_pair",
    )(*pairs)


def per_device(
    block_in, norm1_gain, norm1_bias, w_query, w_key, w_value, w_out, norm2_gain, norm2_bias,
    w_up, up_bias, w_down, down_bias, segments, rand_blocks, glob_blocks, cotangent,
):
    dp_count, tensor_count = lax.axis_size("dp"), lax.axis_size("tensor")
    d, z = lax.axis_index("dp").astype(jnp.int32), lax.axis_index("tensor").astype(jnp.int32)
    core = d % 2
    where = jnp.stack([core, d, z])
    batches, local, width = block_in.shape
    share = local // 2
    blocks = segments.shape[1] // BLOCK
    pairs = dp_count // 2

    def move(value, to):
        routes = [
            (a * tensor_count + b, to(a, b)[0] * tensor_count + to(a, b)[1] % tensor_count)
            for a in range(dp_count)
            for b in range(tensor_count)
        ]
        return lax.ppermute(value, BOTH, routes)

    def other_core(value):
        return move(value, lambda a, b: (a ^ 1, b))

    def along(value, step):
        return move(value, lambda a, b: (a, b + step + tensor_count))

    def across(value, r):
        return move(value, lambda a, b: (a ^ (2 * r), b))

    def exchange(value):
        return lax.all_to_all(value, "tensor", split_axis=0, concat_axis=0, tiled=True)

    def half_of(value, which):
        value = value.reshape(batches, 2, share, width)
        return lax.dynamic_index_in_dim(value, which, 1, keepdims=False)

    def both_halves(keep, come):
        both = jnp.where(core == 0, jnp.stack([keep, come], 1), jnp.stack([come, keep], 1))
        return both.reshape(2 * batches * share, width)

    chunk = norm1_gain.shape[0]
    devices = dp_count * tensor_count
    rand_rows = rand_blocks.reshape(-1, 128)
    rows_each = rand_rows.shape[0] // batches
    small = pack(
        [v.reshape(1, chunk) for v in (norm1_gain, norm1_bias, norm2_gain, norm2_bias, down_bias, up_bias)],
        rand_rows, glob_blocks.reshape(1, -1), devices,
    )
    shard = jnp.concatenate([w_query, w_key, w_value, w_out.T], axis=1)
    attn_slots = [along(shard, -k) for k in range(1, tensor_count)]
    their_segments = other_core(segments)
    x_come, cot_come = other_core(half_of(block_in, 1 - core)), other_core(half_of(cotangent, 1 - core))
    x_half = both_halves(half_of(block_in, core), x_come)
    small, x_half = lax.optimization_barrier((small, x_half))
    small = lax.all_to_all(small, BOTH, split_axis=0, concat_axis=0, tiled=True)
    attn_slots, small = lax.optimization_barrier((attn_slots, small))
    attn_slots = jnp.stack([shard, *attn_slots])
    x = exchange(x_half)
    small = small.reshape(dp_count, tensor_count, *small.shape[1:])
    vectors = small[:, :, :6, :chunk].astype(f32)
    up_shift = vectors[:, :, 5].transpose(1, 0, 2).reshape(tensor_count, 1, -1)
    places = jnp.arange(dp_count, dtype=jnp.int32)
    order = chunk_at(d, places, dp_count)
    vecs = jnp.take(vectors[:, 0, :5], order, axis=0).transpose(1, 0, 2).reshape(5, width)
    vecs = jnp.concatenate([vecs, jnp.zeros((3, width), f32)])
    ints = lax.dynamic_index_in_dim(small, d - core + z % 2, 0, keepdims=False).astype(jnp.int32)
    rand_heads = ints[:, 8 : 8 + rand_rows.shape[0]].reshape(tensor_count, batches, rows_each, 128)
    rand_heads = lax.dynamic_index_in_dim(rand_heads, z // 2, 1, keepdims=False)
    rand_heads = lax.dynamic_slice_in_dim(jnp.roll(rand_heads, -z, axis=0), 2 * core, 2, 0)
    rand_heads = rand_heads.reshape(2 * rand_blocks.shape[2], blocks, RAND)
    glob_row = ints[0, 8 + rand_rows.shape[0], : glob_blocks.size].reshape(batches, -1)
    glob_row = lax.dynamic_index_in_dim(glob_row, z // 2, 0, keepdims=False)
    segment_row = lax.dynamic_index_in_dim(
        jnp.where(z % 2 == core, segments, their_segments), z // 2, 0, keepdims=False
    )
    segment_lanes = jnp.broadcast_to(segment_row[:, None], (segment_row.shape[0], 128))
    per_piece = share // BLOCK
    half = tensor_count * share

    def row_of(block):
        source, place = block // (2 * per_piece), block % (2 * per_piece)
        side = place // per_piece
        return jnp.where(side == core, 0, half) + source * share + (place % per_piece) * BLOCK

    table = attention_table(rand_heads, glob_row, row_of, 2 * half)

    attn_own = [attn_slots] + [across(attn_slots, r) for r in range(1, pairs)]
    pair_shard = jnp.stack([w_up, w_down.T])
    pair_weights = lax.all_gather(pair_shard, BOTH, axis=0, tiled=False)
    pair_weights = pair_weights.reshape(dp_count, tensor_count, 2, *w_up.shape)
    cot_half = both_halves(half_of(cotangent, core), cot_come)
    x, attn_own, table, segment_lanes, vecs, up_shift, cot_half = lax.optimization_barrier(
        (x, attn_own, table, segment_lanes, vecs, up_shift, cot_half)
    )
    attn_own = join(attn_own)
    attn_weights = (attn_own, other_core(attn_own))
    aligned = chunk % 128 == 0
    own_features = chunk_matrix(d, width, dp_count)
    if not aligned:
        x = jnp.dot(x, own_features, preferred_element_type=f32).astype(bf16)

    send, x, normed = project(where, x, vecs, attn_weights, True, dp_count)
    oth = other_core(send)
    own = project(where, normed, vecs, attn_weights, False, dp_count)
    ctx_own0, ctx_send0, lse0 = attn_fwd(table, own, oth, segment_lanes, blocks, 0)
    ctx_oth0 = other_core(ctx_send0)
    ctx_own1, ctx_send1, lse1 = attn_fwd(table, own, oth, segment_lanes, blocks, 1)
    ctx_oth1 = other_core(ctx_send1)
    cot = exchange(cot_half)
    resid, normed_two = out_project(
        where, x, (ctx_own0, ctx_own1, ctx_oth0, ctx_oth1), attn_weights, vecs, dp_count
    )
    if not aligned:
        normed_two = jnp.dot(normed_two, own_features.T, preferred_element_type=f32).astype(bf16)
    ffn0, gn0, pair0, bias0 = feed_forward(
        where, normed_two, cot, pair_weights, up_shift, 2
    )

    def reduce_rows(total):
        flat = total.reshape(-1, total.shape[-1])
        result = lax.psum_scatter(flat, "dp", scatter_dimension=0, tiled=True)
        return result.reshape(total.shape[1:])

    ffn1, gn1, pair1, bias1 = feed_forward(
        where, normed_two, cot, pair_weights, up_shift, 0
    )
    pair_total0 = reduce_rows(pair0)
    pair_total1 = reduce_rows(pair1)
    grad_bias = jnp.concatenate([bias1, bias0])
    ffn, grad_two = (ffn0, ffn1), (gn0, gn1)
    if not aligned:
        reorder = lambda v: jnp.dot(v, own_features, preferred_element_type=f32).astype(bf16)
        ffn, grad_two, cot = map(reorder, ffn), map(reorder, grad_two), reorder(cot)

    def reduce_core(own_half, other_half):
        theirs = other_core(other_half)
        size = own_half.shape[-2] // pairs
        return [
            (
                own_half[..., r * size : (r + 1) * size, :].astype(f32)
                + theirs[..., r * size : (r + 1) * size, :].astype(f32)
            ).astype(own_half.dtype)
            for r in range(pairs)
        ]

    def add_parts(first, others):
        total = first.astype(f32)
        for part in others:
            total = total + part.astype(f32)
        return total.astype(first.dtype)

    def reduce_across(parts):
        return add_parts(parts[0], [across(parts[r], r) for r in range(1, pairs)])

    piece = width // devices

    def exchange_sums(sums_one, sums_two, grad_bias):
        five = jnp.concatenate([sums_one[:2], sums_two[:3]]).reshape(5, dp_count, chunk)
        relative = places ^ d
        back = (relative % 2) * pairs + relative // 2
        five = jnp.take(five, back, axis=1).reshape(5, devices, piece).transpose(1, 0, 2)
        shift = jnp.roll(grad_bias, z, axis=0)
        shift = shift.reshape(tensor_count, dp_count, -1).transpose(1, 0, 2)
        sums = jnp.concatenate([five.reshape(devices, -1), shift.reshape(devices, -1)], axis=1)
        return lax.all_to_all(sums, BOTH, split_axis=0, concat_axis=0, tiled=True)

    def reduce_along(total, slots):
        return sum(
            (along(total[i], k) if k else total[i]).astype(f32) for i, k in enumerate(slots)
        )

    *out, grad_resid, low, gctx_own, gctx_send, sums_two = middle(
        where, resid, tuple(ffn), tuple(grad_two), cot, attn_weights, vecs, dp_count
    )
    gctx_oth = other_core(gctx_send)
    out_back = [None] * tensor_count

    def give(piece, turn):
        return lax.ppermute(piece, BOTH, token_routes(dp_count, tensor_count, turn))

    out_back[0], out_back[1], out_back[2] = (give(out[turn], turn) for turn in range(3))
    d_own0, d_send0 = attn_bwd(
        table, own, oth, gctx_own, gctx_oth, segment_lanes, lse0, blocks, 0
    )
    d_send0, out_back[0], out_back[1], out_back[2] = lax.optimization_barrier(
        (d_send0, *out_back[:3])
    )
    d_oth0 = other_core(d_send0)
    total_one, ga0, gb0, *turned = back_early(
        where, normed, low, (d_own0, d_oth0), (ctx_own0, ctx_oth0), attn_weights, 0
    )
    out[3], d_oth0 = lax.optimization_barrier((out[3], d_oth0))
    out_back[3] = give(out[3], 3)
    ga0, gb0, out_back = lax.optimization_barrier((ga0, gb0, out_back))
    attn_parts0 = reduce_core(ga0, gb0)
    lse1, attn_parts0 = lax.optimization_barrier((lse1, attn_parts0))
    d_own1, d_send1 = attn_bwd(
        table, own, oth, gctx_own, gctx_oth, segment_lanes, lse1, blocks, 1
    )
    attn_total0 = reduce_across(attn_parts0)
    pair_next = [along(pair_total0[0], 2), along(pair_total0[1], 3)]
    d_send1, attn_total0, pair_next = lax.optimization_barrier((d_send1, attn_total0, pair_next))
    d_oth1 = other_core(d_send1)
    pair_next.append(along(pair_total1[1], 1))
    *grad_in, sums_one = back_tokens(
        where, (d_own1, d_oth1), attn_weights, 1, total_one, x, grad_resid, vecs
    )
    grad_in, out_back, turned = lax.optimization_barrier((grad_in, out_back, turned))
    grad_back = [give(piece, turn) for turn, piece in enumerate(grad_in)]
    ga1, gb1 = back_weights(where, (d_own1, d_oth1), (ctx_own1, ctx_oth1), turned)
    ga1, gb1, pair_next = lax.optimization_barrier((ga1, gb1, pair_next))
    attn_parts1 = reduce_core(ga1, gb1)
    sums_one, attn_parts1 = lax.optimization_barrier((sums_one, attn_parts1))
    sums = exchange_sums(sums_one, sums_two, grad_bias)
    attn_come1 = [across(attn_parts1[r], r) for r in range(1, pairs)]
    attn_total1 = add_parts(attn_parts1[0], attn_come1)
    block_out = restore_direct(where, out_back, dp_count, bf16).reshape(batches, local, width)
    g_attn = reduce_along(attn_total0, (0, 2)) + reduce_along(attn_total1, (1, 3))
    g_up, g_down = unpack_pair(pair_total1[0], *pair_next)
    grad_in = restore_direct(where, grad_back, dp_count, f32).reshape(batches, local, width)

    sums = jnp.sum(sums, axis=0)
    vector_grads = [sums[i * piece : (i + 1) * piece] for i in range(5)]
    quarter = width // 4
    return (
        block_out, grad_in, vector_grads[0], vector_grads[1],
        g_attn[:, :quarter], g_attn[:, quarter : 2 * quarter], g_attn[:, 2 * quarter : 3 * quarter],
        g_attn[:, 3 * quarter :].T, vector_grads[2], vector_grads[3],
        g_up, sums[5 * piece :][None], g_down, vector_grads[4],
    )


def solution(mesh):
    rows, both = P(None, BOTH, None), P(BOTH)
    dp, split, turned = P("dp"), P("dp", "tensor"), P("tensor", "dp")
    return jax.shard_map(
        per_device,
        mesh=mesh,
        in_specs=(
            rows, dp, dp, split, split, split, turned, dp, dp, split, turned, turned, dp,
            P(None, "dp"), P(None, "dp", "tensor", None, None), P(None, "dp", None), rows,
        ),
        out_specs=(
            rows, rows, both, both, split, split, split, turned, both, both, split, turned, turned,
            both,
        ),
        check_vma=False,
    )
```
